32 devices in a mesh: wshard: 4 (over y, x), seq: 8 (over z, core).
Axes of the slice: x: 2, y: 2, z: 4, core: 2. Of those that a mesh axis runs over, the one named last changes fastest.
Arguments:
- block_input: bfloat16 [8, 1024, 1536], P('wshard', 'seq'), may hold values from -6 to 6
- cotangent: bfloat16 [8, 1024, 1536], P('wshard', 'seq'), may hold values from -6 to 6
- norm_gain: bfloat16 [1536], P('wshard'), may hold values from 0.5 to 1.5
- norm_mean: float32 [1536], P(('wshard', 'seq')), may hold values from -16 to 16
- norm_square: float32 [1536], P(('wshard', 'seq')), may hold values from 0.16384 to 1.6384
- inproj_weight: bfloat16 [1536, 6448], P('wshard'), may hold values from -0.15625 to 0.15625
- inproj_mean: float32 [1536, 6448], P(('wshard', 'seq')), may hold values from -16 to 16
- inproj_square: float32 [1536, 6448], P(('wshard', 'seq')), may hold values from 0.16384 to 1.6384
- conv_params: bfloat16 [5, 3328], P(None, 'wshard'), may hold values from -0.5 to 0.5
- conv_mean: float32 [5, 3328], P(None, ('wshard', 'seq')), may hold values from -16 to 16
- conv_square: float32 [5, 3328], P(None, ('wshard', 'seq')), may hold values from 0.16384 to 1.6384
- head_params: bfloat16 [3, 48], P(None, 'wshard'), may hold values from -7 to 2.8, as said below
- head_mean: float32 [3, 48], P(None, 'wshard'), may hold values from -16 to 16
- head_square: float32 [3, 48], P(None, 'wshard'), may hold values from 0.16384 to 1.6384
- gate_gain: bfloat16 [3072], P('wshard'), may hold values from 0.5 to 1.5
- gate_mean: float32 [3072], P(('wshard', 'seq')), may hold values from -16 to 16
- gate_square: float32 [3072], P(('wshard', 'seq')), may hold values from 0.16384 to 1.6384
- outproj_weight: bfloat16 [3072, 1536], P('wshard'), may hold values from -0.109375 to 0.109375
- outproj_mean: float32 [3072, 1536], P(('wshard', 'seq')), may hold values from -16 to 16
- outproj_square: float32 [3072, 1536], P(('wshard', 'seq')), may hold values from 0.16384 to 1.6384
Outputs:
- block_output: float32 [8, 1024, 1536], P('wshard', 'seq')
- input_grad: float32 [8, 1024, 1536], P('wshard', 'seq')
- norm_grad: float32 [1536], P(('wshard', 'seq'))
- norm_newmean: float32 [1536], P(('wshard', 'seq'))
- norm_newsquare: float32 [1536], P(('wshard', 'seq'))
- norm_update: float32 [1536], P(('wshard', 'seq'))
- inproj_grad: float32 [1536, 6448], P(('wshard', 'seq'))
- inproj_newmean: float32 [1536, 6448], P(('wshard', 'seq'))
- inproj_newsquare: float32 [1536, 6448], P(('wshard', 'seq'))
- inproj_update: float32 [1536, 6448], P(('wshard', 'seq'))
- conv_grad: float32 [5, 3328], P(None, ('wshard', 'seq'))
- conv_newmean: float32 [5, 3328], P(None, ('wshard', 'seq'))
- conv_newsquare: float32 [5, 3328], P(None, ('wshard', 'seq'))
- conv_update: float32 [5, 3328], P(None, ('wshard', 'seq'))
- head_grad: float32 [3, 48], P(None, 'wshard')
- head_newmean: float32 [3, 48], P(None, 'wshard')
- head_newsquare: float32 [3, 48], P(None, 'wshard')
- head_update: float32 [3, 48], P(None, 'wshard')
- gate_grad: float32 [3072], P(('wshard', 'seq'))
- gate_newmean: float32 [3072], P(('wshard', 'seq'))
- gate_newsquare: float32 [3072], P(('wshard', 'seq'))
- gate_update: float32 [3072], P(('wshard', 'seq'))
- outproj_grad: float32 [3072, 1536], P(('wshard', 'seq'))
- outproj_newmean: float32 [3072, 1536], P(('wshard', 'seq'))
- outproj_newsquare: float32 [3072, 1536], P(('wshard', 'seq'))
- outproj_update: float32 [3072, 1536], P(('wshard', 'seq'))
The draws below stay inside these ranges and needn't reach their ends.
Inputs may be any that keep to these rules, and one draw needn't show every extreme that they name: `head_params`: row 0 holds logarithms of decay rates, row 1 step biases, row 2 skip factors.
All inputs are finite; a program needn't handle non-finite values.
Results may differ from the reference program's by a relative error of at most 0.012.
The reference program's roundings to bfloat16 on the way count: a program that leaves them out, or rounds other values in their place, can miss the bound.
Values may be sent and summed in bfloat16 or wider, within the bound.
No kernel may reach another device: no remote copies, remote signals or barrier semaphores. Data moves between devices by JAX's collectives and lax.ppermute only.
A program may use at most 256 MiB of HBM per device.

```python
import math
import jax
import jax.numpy as jnp
from jax import lax

D = 1536
HEADS = 48
STATE = 128
KERNEL = 4
SPAN = 256
LEN = 1024
INNER = 3072
CONV = 3328
PROJ = 6448
BATCH = 8


def draw_head_params(key, part):
    key_rate = jax.random.fold_in(key, 11)
    key_step = jax.random.fold_in(key, 12)
    key_skip = jax.random.fold_in(key, 13)
    rate_vals = jax.random.uniform(key_rate, (HEADS,), jnp.float32, 1.0, 16.0)
    step_vals = jnp.exp(jax.random.uniform(key_step, (HEADS,), jnp.float32, math.log(0.001), math.log(0.1)))
    step_bias = step_vals + jnp.log(-jnp.expm1(-step_vals))
    skip_vals = jax.random.uniform(key_skip, (HEADS,), jnp.float32, 0.5, 1.5)
    return jnp.stack([jnp.log(rate_vals), step_bias, skip_vals]).astype(jnp.bfloat16)


def shard_levels(key, dims, pieces, least, largest):
    gain = 1.0
    for axis_at, parts in pieces:
        heights = jax.random.uniform(jax.random.fold_in(jax.random.fold_in(key, 6), axis_at), (parts,), jnp.float32, least / len(pieces), largest / len(pieces))
        gain = gain * jnp.repeat(jnp.exp(heights), dims[axis_at] // parts).reshape((-1,) + (1,) * (len(dims) - 1 - axis_at))
    return gain


def scatter_about(own_key, dims, deviation, bound, shards=(), dtype=jnp.bfloat16):
    values = deviation * jax.random.normal(own_key, dims, jnp.float32)
    if shards:
        values = values * shard_levels(own_key, dims, shards, -0.22, 0.18)
    return jnp.clip(values, -bound, bound).astype(dtype)


def setup_inputs(seed: int = 0) -> dict:
    arg_keys = jax.random.split(jax.random.key(seed), 21)
    block_input = scatter_about(arg_keys[0], (BATCH, LEN, D), 1.0, 6.0, ((0, 4), (1, 8)))
    cotangent = scatter_about(arg_keys[1], (BATCH, LEN, D), 1.0, 6.0, ((0, 4), (1, 8)))
    norm_gain = jnp.clip(1.0 + 0.1 * jax.random.normal(arg_keys[2], (D,), jnp.float32), 0.5, 1.5).astype(jnp.bfloat16)
    norm_mean = scatter_about(arg_keys[3], (D,), (0.03 * (BATCH * LEN) ** 0.5), 16.0, ((0, 32),), jnp.float32)
    norm_square = jnp.clip(jnp.exp(math.log(1.6384) - 2.3025851 * jax.random.uniform(arg_keys[4], (D,), jnp.float32) ** shard_levels(arg_keys[4], (D,), ((0, 32),), -0.2, 0.2)), 0.16384, 1.6384)
    inproj_weight = scatter_about(arg_keys[5], (D, PROJ), D ** -0.5, 0.15625, ((0, 4),))
    inproj_mean = scatter_about(arg_keys[6], (D, PROJ), (0.03 * (BATCH * LEN) ** 0.5), 16.0, ((0, 32),), jnp.float32)
    inproj_square = jnp.clip(jnp.exp(math.log(1.6384) - 2.3025851 * jax.random.uniform(arg_keys[7], (D, PROJ), jnp.float32) ** shard_levels(arg_keys[7], (D, PROJ), ((0, 32),), -0.2, 0.2)), 0.16384, 1.6384)
    conv_params = jnp.clip(jax.random.uniform(arg_keys[8], (KERNEL + 1, CONV), jnp.float32, -0.5, 0.5) * shard_levels(arg_keys[8], (KERNEL + 1, CONV), ((1, 4),), -0.4, 0.0), -0.5, 0.5).astype(jnp.bfloat16)
    conv_mean = scatter_about(arg_keys[9], (KERNEL + 1, CONV), (0.03 * (BATCH * LEN) ** 0.5), 16.0, ((1, 32),), jnp.float32)
    conv_square = jnp.clip(jnp.exp(math.log(1.6384) - 2.3025851 * jax.random.uniform(arg_keys[10], (KERNEL + 1, CONV), jnp.float32) ** shard_levels(arg_keys[10], (KERNEL + 1, CONV), ((1, 32),), -0.2, 0.2)), 0.16384, 1.6384)
    head_params = draw_head_params(jax.random.fold_in(arg_keys[20], 71), 0)
    head_mean = scatter_about(arg_keys[12], (3, HEADS), (0.03 * (BATCH * LEN) ** 0.5), 16.0, ((1, 4),), jnp.float32)
    head_square = jnp.clip(jnp.exp(math.log(1.6384) - 2.3025851 * jax.random.uniform(arg_keys[13], (3, HEADS), jnp.float32) ** shard_levels(arg_keys[13], (3, HEADS), ((1, 4),), -0.2, 0.2)), 0.16384, 1.6384)
    gate_gain = jnp.clip(1.0 + 0.1 * jax.random.normal(arg_keys[14], (INNER,), jnp.float32), 0.5, 1.5).astype(jnp.bfloat16)
    gate_mean = scatter_about(arg_keys[15], (INNER,), (0.03 * (BATCH * LEN) ** 0.5), 16.0, ((0, 32),), jnp.float32)
    gate_square = jnp.clip(jnp.exp(math.log(1.6384) - 2.3025851 * jax.random.uniform(arg_keys[16], (INNER,), jnp.float32) ** shard_levels(arg_keys[16], (INNER,), ((0, 32),), -0.2, 0.2)), 0.16384, 1.6384)
    outproj_weight = scatter_about(arg_keys[17], (INNER, D), INNER ** -0.5, 0.109375, ((0, 4),))
    outproj_mean = scatter_about(arg_keys[18], (INNER, D), (0.03 * (BATCH * LEN) ** 0.5), 16.0, ((0, 32),), jnp.float32)
    outproj_square = jnp.clip(jnp.exp(math.log(1.6384) - 2.3025851 * jax.random.uniform(arg_keys[19], (INNER, D), jnp.float32) ** shard_levels(arg_keys[19], (INNER, D), ((0, 32),), -0.2, 0.2)), 0.16384, 1.6384)
    return {"block_input": block_input, "cotangent": cotangent, "norm_gain": norm_gain, "norm_mean": norm_mean, "norm_square": norm_square, "inproj_weight": inproj_weight, "inproj_mean": inproj_mean, "inproj_square": inproj_square, "conv_params": conv_params, "conv_mean": conv_mean, "conv_square": conv_square, "head_params": head_params, "head_mean": head_mean, "head_square": head_square, "gate_gain": gate_gain, "gate_mean": gate_mean, "gate_square": gate_square, "outproj_weight": outproj_weight, "outproj_mean": outproj_mean, "outproj_square": outproj_square}


@jax.custom_vjp
def low(v):
    return lax.optimization_barrier(v.astype(jnp.bfloat16)).astype(jnp.float32)

@jax.custom_vjp
def low_back(v):
    return v

def low_keep(v):
    return (low(v), None)

def low_pass(kept, grad):
    return (grad,)

def back_keep(v):
    return (v, None)

def back_low(kept, grad):
    return (low(grad),)
low.defvjp(low_keep, low_pass)
low_back.defvjp(back_keep, back_low)
norm_eps = 1e-05
adam_eps = 1e-08
learn_rate = 0.02
beta_one = 0.9
beta_two = 0.999
first_fix = 1.0 - 0.9 ** 10
second_fix = 1.0 - 0.999 ** 10
highest = lax.Precision.HIGHEST

def depthwise(values, taps_all):
    kernel_len = taps_all.shape[0] - 1
    length = values.shape[0]
    padded = jnp.pad(values, ((kernel_len - 1, 0), (0, 0)))
    summed = taps_all[kernel_len] + taps_all[0] * padded[0:length]
    for offset in range(1, kernel_len):
        summed = summed + taps_all[offset] * padded[offset:offset + length]
    return summed

def state_scan(inputs, steps, rates, bmatrix, cmatrix):
    length, head_count, head_dim = inputs.shape
    blocks = length // SPAN
    xblock = inputs.reshape(blocks, SPAN, head_count, head_dim)
    dblock = steps.reshape(blocks, SPAN, head_count)
    bblock = bmatrix.reshape(blocks, SPAN, -1)
    cblock = cmatrix.reshape(blocks, SPAN, -1)
    within = jnp.cumsum(dblock * rates, axis=1)
    distance = within[:, :, None, :] - within[:, None, :, :]
    causal = (jnp.arange(SPAN)[:, None] >= jnp.arange(SPAN)[None, :])[None, :, :, None]
    mixing = jnp.exp(jnp.where(causal, distance, -jnp.inf))
    scores = jnp.einsum('cin,cjn->cij', cblock, bblock, precision=highest)
    weights = mixing * scores[:, :, :, None] * dblock[:, None, :, :]
    inside = jnp.einsum('cijh,cjhp->cihp', weights, xblock, precision=highest)
    final_log = within[:, -1, :]
    tail_scale = jnp.exp(final_log[:, None, :] - within) * dblock
    states = jnp.einsum('cjn,cjhp->chpn', bblock, xblock * tail_scale[:, :, :, None], precision=highest)
    totals = jnp.cumsum(final_log, axis=0)
    between = (totals - final_log)[:, None, :] - totals[None, :, :]
    earlier = (jnp.arange(blocks)[:, None] > jnp.arange(blocks)[None, :])[:, :, None]
    carried = jnp.exp(jnp.where(earlier, between, -jnp.inf))
    incoming = jnp.einsum('kmh,mhpn->khpn', carried, states, precision=highest)
    outside = jnp.einsum('cin,chpn->cihp', cblock, incoming, precision=highest) * jnp.exp(within)[:, :, :, None]
    return (inside + outside).reshape(length, head_count, head_dim)

def mixer(values_in, shared_in, steps_in, taps_x, taps_shared, head_table):
    state_half = shared_in.shape[1] // 2
    length = values_in.shape[0]
    head_count = head_table.shape[1]
    x_active = jax.nn.silu(depthwise(values_in, taps_x))
    shared_active = jax.nn.silu(depthwise(shared_in, taps_shared))
    inputs = x_active.reshape(length, head_count, -1)
    steps = jax.nn.softplus(steps_in + head_table[1])
    rates = -jnp.exp(head_table[0])
    result = state_scan(inputs, steps, rates, shared_active[:, :state_half], shared_active[:, state_half:])
    result = result + head_table[2][:, None] * inputs
    return result.reshape(length, -1)

def layer(seq_input, gain_w, inproj_w, conv_w, head_w, gate_w, outproj_w):
    scale = lax.rsqrt(lax.optimization_barrier(jnp.mean(seq_input * seq_input, axis=-1, keepdims=True)) + norm_eps)
    normed = low(seq_input * scale * gain_w)
    projected = low_back(jnp.dot(normed, inproj_w, precision=highest))
    gates = projected[:, :INNER]
    values_in = low(projected[:, INNER:2 * INNER])
    shared_in = low(projected[:, 2 * INNER:2 * INNER + 2 * STATE])
    steps_in = low(projected[:, 2 * INNER + 2 * STATE:])
    mixed = mixer(values_in, shared_in, steps_in, conv_w[:, :INNER], conv_w[:, INNER:], head_w)
    mixed = low_back(low(mixed))
    gated = mixed * jax.nn.silu(gates)
    grms = lax.rsqrt(lax.optimization_barrier(jnp.mean(gated * gated, axis=-1, keepdims=True)) + norm_eps)
    branch = low(gated * grms * gate_w)
    return seq_input + jnp.dot(branch, outproj_w, precision=highest)

def adamw(grad, weight, first, second, decay):
    first_new = beta_one * first + (1.0 - beta_one) * grad
    second_new = beta_two * second + (1.0 - beta_two) * grad * grad
    update = -learn_rate * (first_new / first_fix / (jnp.sqrt(second_new / second_fix) + adam_eps) + decay * weight)
    return (grad, first_new, second_new, update)

def reference(block_input, cotangent, norm_gain, norm_mean, norm_square, inproj_weight, inproj_mean, inproj_square, conv_params, conv_mean, conv_square, head_params, head_mean, head_square, gate_gain, gate_mean, gate_square, outproj_weight, outproj_mean, outproj_square):
    gain_f = norm_gain.astype(jnp.float32)
    inproj_f = inproj_weight.astype(jnp.float32)
    conv_f = conv_params.astype(jnp.float32)
    head_f = head_params.astype(jnp.float32)
    gate_f = gate_gain.astype(jnp.float32)
    outproj_f = outproj_weight.astype(jnp.float32)
    inputs = block_input.astype(jnp.float32)

    def forward(all_input, gain_w, inproj_w, conv_w, head_w, gate_w, outproj_w):

        def one_sequence(seq_input):
            return layer(seq_input, gain_w, inproj_w, conv_w, head_w, gate_w, outproj_w)
        saved = jax.checkpoint(one_sequence)

        def advance(carry, seq_input):
            return (carry, saved(seq_input))
        unused, outputs = lax.scan(advance, jnp.zeros((), jnp.float32), all_input)
        return outputs
    outputs, pull = jax.vjp(forward, inputs, gain_f, inproj_f, conv_f, head_f, gate_f, outproj_f)
    grads = pull(cotangent.astype(jnp.float32))
    norm_res = adamw(grads[1], gain_f, norm_mean, norm_square, 0.0)
    inproj_res = adamw(grads[2], inproj_f, inproj_mean, inproj_square, 0.1)
    conv_res = adamw(grads[3], conv_f, conv_mean, conv_square, 0.0)
    head_res = adamw(grads[4], head_f, head_mean, head_square, 0.0)
    gate_res = adamw(grads[5], gate_f, gate_mean, gate_square, 0.0)
    outproj_res = adamw(grads[6], outproj_f, outproj_mean, outproj_square, 0.1)
    return (outputs, grads[0], norm_res[0], norm_res[1], norm_res[2], norm_res[3], inproj_res[0], inproj_res[1], inproj_res[2], inproj_res[3], conv_res[0], conv_res[1], conv_res[2], conv_res[3], head_res[0], head_res[1], head_res[2], head_res[3], gate_res[0], gate_res[1], gate_res[2], gate_res[3], outproj_res[0], outproj_res[1], outproj_res[2], outproj_res[3])
```

```python
import functools

import jax
import jax.numpy as jnp
from jax import lax
from jax.experimental import pallas as pl
from jax.experimental.pallas import tpu as pltpu
from jax.sharding import PartitionSpec as P

norm_eps = 1e-05
adam_eps = 1e-08
learn_rate = 0.02
beta_one = 0.9
beta_two = 0.999
first_fix = 1.0 - 0.9**10
second_fix = 1.0 - 0.999**10

f32 = jnp.float32
bf16 = jnp.bfloat16
Q = 128
HP = 16
FLOOR = -1e30
VMEM_LIMIT = 56 * 1024 * 1024


def dot_nn(a, b):
    return lax.dot_general(a, b, (((1,), (0,)), ((), ())), preferred_element_type=f32)


def dot_nt(a, b):
    return lax.dot_general(a, b, (((1,), (1,)), ((), ())), preferred_element_type=f32)


def dot_tn(a, b):
    return lax.dot_general(a, b, (((0,), (0,)), ((), ())), preferred_element_type=f32)


def sigmoid(a):
    return 1.0 / (1.0 + jnp.exp(-a))


def lanes(shape):
    return lax.broadcasted_iota(jnp.int32, shape, 1)


def earlier_by(current, previous, lane, shift):
    return pltpu.roll(jnp.where(lane >= Q - shift, previous, current), shift, 1)


def later_by(current, following, lane, shift):
    return pltpu.roll(jnp.where(lane < shift, following, current), Q - shift, 1)


def running_sum(a, lane):
    shift = 1
    while shift < Q:
        a = a + jnp.where(lane >= shift, pltpu.roll(a, shift, 1), 0.0)
        shift *= 2
    return a


def running_sum_back(a, lane):
    shift = 1
    while shift < Q:
        a = a + jnp.where(lane < Q - shift, pltpu.roll(a, Q - shift, 1), 0.0)
        shift *= 2
    return a


def mixer_forward(
    own_width,
    heads,
    kernel_len,
    order_ref,
    normed_ref,
    weight_ref,
    chan_ref,
    head_ref,
    gates_ref,
    values_ref,
    conv_ref,
    sent_ref,
    table_ref,
    state_ref,
    before,
    state,
    active,
    steps,
    inter,
    scaled,
):
    channels = chan_ref.shape[0]
    width = own_width // heads
    token_block = normed_ref.shape[0]

    @pl.when(pl.program_id(0) == 0)
    def _():
        before[...] = jnp.zeros_like(before)
        state[...] = jnp.zeros_like(state)

    normed = normed_ref[...]
    gates_ref[...] = dot_nt(weight_ref[0:own_width, :], normed)
    values_ref[...] = dot_nt(weight_ref[own_width : own_width + channels, :], normed).astype(bf16)
    steps[...] = dot_nt(weight_ref[own_width + channels :, :], normed).astype(bf16).astype(f32)
    lane = lanes((Q, Q))
    lane_head = lanes((HP, Q))
    causal = lax.broadcasted_iota(jnp.int32, (Q, Q), 0) <= lane

    def block(at, carry):
        here = pl.ds(pl.multiple_of(at * Q, Q), Q)

        def convolve(tile, inner):
            rows = pl.ds(pl.multiple_of(tile * Q, Q), Q)
            raw = values_ref[rows, here]
            current = raw.astype(f32)
            previous = before[rows, :].astype(f32)
            taps = chan_ref[rows, :]
            out = taps[:, kernel_len : kernel_len + 1] + taps[:, kernel_len - 1 : kernel_len] * current
            for shift in range(1, kernel_len):
                tap = kernel_len - 1 - shift
                out = out + taps[:, tap : tap + 1] * earlier_by(current, previous, lane, shift)
            before[rows, :] = raw
            conv_ref[rows, here] = out
            active[rows, :] = out * sigmoid(out)
            return inner

        lax.fori_loop(0, channels // Q, convolve, 0)
        drive = steps[:, here] + head_ref[:, 1:2]
        step = jnp.maximum(drive, 0.0) + jnp.log1p(jnp.exp(-jnp.abs(drive)))
        within = running_sum(step * head_ref[:, 0:1], lane_head)
        table_ref[0, :, here] = step
        table_ref[1, :, here] = within
        table_ref[2, :, here] = sigmoid(drive)
        within_col = jnp.transpose(within)
        total = within[:, Q - 1 : Q]
        grow = jnp.exp(within)
        tail = jnp.exp(total - within) * step
        total_decay = jnp.exp(total)
        b_rows = jnp.transpose(active[own_width : own_width + Q, :]).astype(bf16)
        c_cols = active[own_width + Q : own_width + 2 * Q, :].astype(bf16)
        scores = dot_nn(b_rows, c_cols)
        held = state[...].astype(bf16)
        state_ref[at] = held
        inter[...] = dot_nn(held, c_cols)
        for head in range(heads):
            rows = slice(head * width, (head + 1) * width)
            x = active[rows, :]
            decay = jnp.exp(
                jnp.where(causal, within[head : head + 1, :] - within_col[:, head : head + 1], FLOOR)
            )
            weights = (decay * scores).astype(bf16)
            driven = (x * step[head : head + 1, :]).astype(bf16)
            mixed = dot_nn(driven, weights)
            mixed = mixed + inter[rows, :] * grow[head : head + 1, :]
            mixed = mixed + chan_ref[rows, 6:7] * x
            sent_ref[rows, here] = mixed.astype(bf16)
            scaled[rows, :] = (x * tail[head : head + 1, :]).astype(bf16)
            state[rows, :] = state[rows, :] * total_decay[head : head + 1, :]
        state[...] += dot_nn(scaled[...], b_rows)
        return carry

    lax.fori_loop(0, token_block // Q, block, 0)


def gate_statistics(order_ref, gates_ref, sent_ref, cot_ref, weight_ref, chan_ref, dbranch_ref, stat_ref):
    dbranch = dot_nt(weight_ref[...], cot_ref[...])
    dbranch_ref[...] = dbranch
    gates = gates_ref[...]
    gated = sent_ref[...].astype(f32) * (gates * sigmoid(gates))
    square = jnp.sum(gated * gated, axis=0, keepdims=True)
    cross = jnp.sum(gated * (dbranch * chan_ref[0 : gates.shape[0], 7:8]), axis=0, keepdims=True)
    stat_ref[...] = jnp.concatenate([square, cross, jnp.zeros((6, square.shape[1]), f32)], axis=0)


def mixer_backward(
    own_width,
    heads,
    kernel_len,
    order_ref,
    gates_ref,
    sent_ref,
    dbranch_ref,
    conv_ref,
    values_ref,
    table_ref,
    state_ref,
    stat_ref,
    chan_ref,
    head_ref,
    dproj_ref,
    branch_ref,
    conv_acc,
    head_acc,
    adjoint,
    following,
    active,
    dactive,
    dsent,
    inter,
    reach,
    driven,
    tailed,
    rows_scr,
):
    channels = chan_ref.shape[0]
    width = own_width // heads
    token_block = gates_ref.shape[1]

    @pl.when(pl.program_id(0) == 0)
    def _():
        adjoint[...] = jnp.zeros_like(adjoint)
        following[...] = jnp.zeros_like(following)
        conv_acc[...] = jnp.zeros_like(conv_acc)
        head_acc[...] = jnp.zeros_like(head_acc)
        rows_scr[...] = jnp.zeros_like(rows_scr)

    lane = lanes((Q, Q))
    sub = lax.broadcasted_iota(jnp.int32, (Q, Q), 0)
    lane_head = lanes((HP, Q))
    causal = sub >= lane
    strict = (sub < lane).astype(bf16)

    def block(index, carry):
        at = token_block // Q - 1 - index
        here = pl.ds(pl.multiple_of(at * Q, Q), Q)
        grms = stat_ref[0:1, here]
        pull = stat_ref[1:2, here]

        def gate(tile, inner):
            rows = pl.ds(pl.multiple_of(tile * Q, Q), Q)
            gates = gates_ref[rows, here]
            sent = sent_ref[rows, here].astype(f32)
            gain = chan_ref[rows, 7:8]
            sig = sigmoid(gates)
            swish = gates * sig
            gated = sent * swish
            dgated = grms * (dbranch_ref[rows, here] * gain - gated * pull)
            dsent[rows, :] = (dgated * swish).astype(bf16)
            dproj_ref[rows, here] = (dgated * sent * sig * (1.0 + gates * (1.0 - sig))).astype(bf16)
            branch_ref[rows, here] = (gated * grms * gain).astype(bf16)
            return inner

        lax.fori_loop(0, own_width // Q, gate, 0)

        def activate(tile, inner):
            rows = pl.ds(pl.multiple_of(tile * Q, Q), Q)
            conv = conv_ref[rows, here]
            active[rows, :] = conv * sigmoid(conv)
            return inner

        lax.fori_loop(0, channels // Q, activate, 0)
        step = table_ref[0, :, here]
        within = table_ref[1, :, here]
        within_col = jnp.transpose(within)
        total = within[:, Q - 1 : Q]
        grow = jnp.exp(within)
        fade = jnp.exp(total - within)
        tail = fade * step
        total_decay = jnp.exp(total)
        b_cols_f = active[own_width : own_width + Q, :]
        c_cols_f = active[own_width + Q : own_width + 2 * Q, :]
        b_cols = b_cols_f.astype(bf16)
        c_cols = c_cols_f.astype(bf16)
        c_rows = jnp.transpose(c_cols_f).astype(bf16)
        scores = dot_nn(c_rows, b_cols)
        held = state_ref[at]
        after = adjoint[...].astype(bf16)
        inter[...] = dot_nn(held, c_cols)
        reach[...] = dot_nn(after, b_cols)
        dscores = jnp.zeros((Q, Q), f32)
        blank = jnp.zeros((width, Q), bf16)
        for pair in range(heads // 2):
            turned = jnp.transpose(dsent[pair * 2 * width : (pair + 1) * 2 * width, :].astype(f32)).astype(bf16)
            for half in range(2):
                head = 2 * pair + half
                rows = slice(head * width, (head + 1) * width)
                one = slice(head, head + 1)
                x = active[rows, :]
                x_low = x.astype(bf16)
                grad_low = dsent[rows, :]
                grad = grad_low.astype(f32)
                decay = jnp.exp(
                    jnp.where(causal, within_col[:, head : head + 1] - within[one, :], FLOOR)
                )
                lone = jnp.concatenate([x_low, blank] if half == 0 else [blank, x_low], axis=0)
                dweights = dot_nn(turned, lone)
                spread = decay * dweights * step[one, :]
                dscores = dscores + spread
                crossing = dot_nn((spread * scores).astype(bf16), strict)
                rows_scr[0, one, :] = jnp.sum(jnp.where(causal, crossing, 0.0), axis=0, keepdims=True)
                far = reach[rows, :]
                back = dot_nn(grad_low, (decay * scores).astype(bf16)) + far * fade[one, :]
                rows_scr[1, one, :] = jnp.sum(x * back, axis=0, keepdims=True)
                rows_scr[2, one, :] = jnp.sum(x * far, axis=0, keepdims=True) * tail[one, :]
                rows_scr[3, one, :] = jnp.sum(grad * inter[rows, :], axis=0, keepdims=True) * grow[one, :]
                rows_scr[4, one, :] = jnp.sum(grad * x, axis=0, keepdims=True)
                old = adjoint[rows, :]
                rows_scr[5, one, :] = jnp.sum(old * held[rows, :].astype(f32), axis=0, keepdims=True)
                dactive[rows, :] = back * step[one, :] + chan_ref[rows, 6:7] * grad
                driven[rows, :] = (grad * grow[one, :]).astype(bf16)
                tailed[rows, :] = (x * tail[one, :]).astype(bf16)
                adjoint[rows, :] = old * total_decay[one, :]
        dlow = dscores.astype(bf16)
        dactive[own_width : own_width + Q, :] = dot_nn(c_cols, dlow) + dot_tn(after, tailed[...])
        dactive[own_width + Q : own_width + 2 * Q, :] = dot_nt(b_cols, dlow) + dot_tn(held, driven[...])
        adjoint[...] += dot_nn(driven[...], c_rows)
        ahead = rows_scr[2]
        dlog = (
            rows_scr[0]
            + running_sum_back(rows_scr[3], lane_head)
            + (running_sum(ahead, lane_head) - ahead)
            + total_decay * jnp.sum(rows_scr[5], axis=1, keepdims=True)
        )
        dstep = (rows_scr[1] + head_ref[:, 0:1] * dlog) * table_ref[2, :, here]
        dproj_ref[own_width + channels :, here] = dstep.astype(bf16)
        head_acc[0] += step * dlog
        head_acc[1] += dstep
        head_acc[2] += rows_scr[4]

        def convolve(tile, inner):
            rows = pl.ds(pl.multiple_of(tile * Q, Q), Q)
            conv = conv_ref[rows, here]
            sig = sigmoid(conv)
            dconv = dactive[rows, :] * sig * (1.0 + conv * (1.0 - sig))
            taps = chan_ref[rows, :]
            raw = values_ref[rows, here].astype(f32)
            nxt = following[rows, :]
            dvalue = taps[:, kernel_len - 1 : kernel_len] * dconv
            conv_acc[kernel_len - 1, rows, :] += raw * dconv
            for shift in range(1, kernel_len):
                tap = kernel_len - 1 - shift
                moved = later_by(dconv, nxt, lane, shift)
                dvalue = dvalue + taps[:, tap : tap + 1] * moved
                conv_acc[tap, rows, :] += raw * moved
            conv_acc[kernel_len, rows, :] += dconv
            following[rows, :] = dconv
            dproj_ref[pl.ds(pl.multiple_of(own_width + tile * Q, Q), Q), here] = dvalue.astype(bf16)
            return inner

        lax.fori_loop(0, channels // Q, convolve, 0)
        return carry

    lax.fori_loop(0, token_block // Q, block, 0)


def run_forward(order, normed, weight, chan, head_table, own_width, heads, kernel_len):
    places, token_block, model_width = normed.shape
    channels = chan.shape[0]
    full = places * token_block
    fixed = lambda k, order: (0, 0)
    cols = lambda k, order: (0, k)
    spec = pltpu.PrefetchScalarGridSpec(
        num_scalar_prefetch=1,
        grid=(places,),
        in_specs=[
            pl.BlockSpec((None, token_block, model_width), lambda k, order: (order[k], 0, 0)),
            pl.BlockSpec(weight.shape, fixed),
            pl.BlockSpec(chan.shape, fixed),
            pl.BlockSpec(head_table.shape, fixed),
        ],
        out_specs=[
            pl.BlockSpec((own_width, token_block), cols),
            pl.BlockSpec((channels, token_block), cols),
            pl.BlockSpec((channels, token_block), cols),
            pl.BlockSpec((own_width, token_block), cols),
            pl.BlockSpec((3, HP, token_block), lambda k, order: (0, 0, k)),
            pl.BlockSpec((token_block // Q, own_width, Q), lambda k, order: (k, 0, 0)),
        ],
        scratch_shapes=[
            pltpu.VMEM((channels, Q), bf16),
            pltpu.VMEM((own_width, Q), f32),
            pltpu.VMEM((channels, Q), f32),
            pltpu.VMEM((HP, token_block), f32),
            pltpu.VMEM((own_width, Q), f32),
            pltpu.VMEM((own_width, Q), bf16),
        ],
    )
    flops = 2 * full * model_width * weight.shape[0]
    return pl.pallas_call(
        functools.partial(mixer_forward, own_width, heads, kernel_len),
        grid_spec=spec,
        out_shape=[
            jax.ShapeDtypeStruct((own_width, full), f32),
            jax.ShapeDtypeStruct((channels, full), bf16),
            jax.ShapeDtypeStruct((channels, full), f32),
            jax.ShapeDtypeStruct((own_width, full), bf16),
            jax.ShapeDtypeStruct((3, HP, full), f32),
            jax.ShapeDtypeStruct((full // Q, own_width, Q), bf16),
        ],
        compiler_params=pltpu.CompilerParams(
            dimension_semantics=("arbitrary",), vmem_limit_bytes=VMEM_LIMIT
        ),
        cost_estimate=pl.CostEstimate(
            flops=2 * flops, bytes_accessed=24 * 1024 * 1024, transcendentals=4 * 1024 * 1024
        ),
        name="mixer_forward",
    )(order, normed, weight, chan, head_table)


def run_statistics(order, gates, sent, cotangent, weight, chan):
    places, token_block, model_width = cotangent.shape
    own_width, full = gates.shape
    fixed = lambda k, order: (0, 0)
    cols = lambda k, order: (0, k)
    spec = pltpu.PrefetchScalarGridSpec(
        num_scalar_prefetch=1,
        grid=(places,),
        in_specs=[
            pl.BlockSpec((own_width, token_block), cols),
            pl.BlockSpec((own_width, token_block), cols),
            pl.BlockSpec((None, token_block, model_width), lambda k, order: (order[k], 0, 0)),
            pl.BlockSpec(weight.shape, fixed),
            pl.BlockSpec(chan.shape, fixed),
        ],
        out_specs=[
            pl.BlockSpec((own_width, token_block), cols),
            pl.BlockSpec((8, token_block), cols),
        ],
    )
    return pl.pallas_call(
        gate_statistics,
        grid_spec=spec,
        out_shape=[
            jax.ShapeDtypeStruct((own_width, full), f32),
            jax.ShapeDtypeStruct((8, full), f32),
        ],
        compiler_params=pltpu.CompilerParams(
            dimension_semantics=("arbitrary",), vmem_limit_bytes=VMEM_LIMIT
        ),
        cost_estimate=pl.CostEstimate(
            flops=2 * full * model_width * own_width,
            bytes_accessed=16 * 1024 * 1024,
            transcendentals=own_width * full,
        ),
        name="gate_statistics",
    )(order, gates, sent, cotangent, weight, chan)


def run_backward(
    order, gates, sent, dbranch, conv, values, table, states, stats, chan, head_table, heads, kernel_len, places
):
    own_width, full = gates.shape
    channels = chan.shape[0]
    token_block = full // places
    out_rows = own_width + channels + HP
    last = places - 1
    fixed = lambda k, order: (0, 0)
    cols = lambda k, order: (0, last - k)
    turned = lambda k, order: (0, order[last - k])
    spec = pltpu.PrefetchScalarGridSpec(
        num_scalar_prefetch=1,
        grid=(places,),
        in_specs=[
            pl.BlockSpec((own_width, token_block), cols),
            pl.BlockSpec((own_width, token_block), cols),
            pl.BlockSpec((own_width, token_block), cols),
            pl.BlockSpec((channels, token_block), cols),
            pl.BlockSpec((channels, token_block), cols),
            pl.BlockSpec((3, HP, token_block), lambda k, order: (0, 0, last - k)),
            pl.BlockSpec((token_block // Q, own_width, Q), lambda k, order: (last - k, 0, 0)),
            pl.BlockSpec((8, token_block), cols),
            pl.BlockSpec(chan.shape, fixed),
            pl.BlockSpec(head_table.shape, fixed),
        ],
        out_specs=[
            pl.BlockSpec((out_rows, token_block), turned),
            pl.BlockSpec((own_width, token_block), turned),
            pl.BlockSpec((kernel_len + 1, channels, Q), lambda k, order: (0, 0, 0)),
            pl.BlockSpec((3, HP, Q), lambda k, order: (0, 0, 0)),
        ],
        scratch_shapes=[
            pltpu.VMEM((own_width, Q), f32),
            pltpu.VMEM((channels, Q), f32),
            pltpu.VMEM((channels, Q), f32),
            pltpu.VMEM((channels, Q), f32),
            pltpu.VMEM((own_width, Q), bf16),
            pltpu.VMEM((own_width, Q), f32),
            pltpu.VMEM((own_width, Q), f32),
            pltpu.VMEM((own_width, Q), bf16),
            pltpu.VMEM((own_width, Q), bf16),
            pltpu.VMEM((6, HP, Q), f32),
        ],
    )
    return pl.pallas_call(
        functools.partial(mixer_backward, own_width, heads, kernel_len),
        grid_spec=spec,
        out_shape=[
            jax.ShapeDtypeStruct((out_rows, full), bf16),
            jax.ShapeDtypeStruct((own_width, full), bf16),
            jax.ShapeDtypeStruct((kernel_len + 1, channels, Q), f32),
            jax.ShapeDtypeStruct((3, HP, Q), f32),
        ],
        compiler_params=pltpu.CompilerParams(
            dimension_semantics=("arbitrary",), vmem_limit_bytes=VMEM_LIMIT
        ),
        cost_estimate=pl.CostEstimate(
            flops=16 * 1024 * 1024 * 1024, bytes_accessed=32 * 1024 * 1024, transcendentals=4 * 1024 * 1024
        ),
        name="mixer_backward",
    )(order, gates, sent, dbranch, conv, values, table, states, stats, chan, head_table)


def adamw(grad, weight, first, second, decay):
    first_new = beta_one * first + (1.0 - beta_one) * grad
    second_new = beta_two * second + (1.0 - beta_two) * grad * grad
    update = -learn_rate * (
        first_new / first_fix / (jnp.sqrt(second_new / second_fix) + adam_eps) + decay * weight
    )
    return (grad, first_new, second_new, update)


def pieces_for(stacked, index):
    return lax.dynamic_index_in_dim(stacked, index, 0, keepdims=False)


def local(
    block_input,
    cotangent,
    norm_gain,
    norm_mean,
    norm_square,
    inproj_weight,
    inproj_mean,
    inproj_square,
    conv_params,
    conv_mean,
    conv_square,
    head_params,
    head_mean,
    head_square,
    gate_gain,
    gate_mean,
    gate_square,
    outproj_weight,
    outproj_mean,
    outproj_square,
):
    group = lax.axis_size("seq")
    shards = lax.axis_size("wshard")
    seq_index = lax.axis_index("seq")
    shard = lax.axis_index("wshard")
    places = group // 2
    place = seq_index // 2
    core = seq_index % 2
    sequences, local_len, model_width = block_input.shape
    inner_width = gate_gain.shape[0] * shards
    head_count = head_params.shape[1] * shards
    kernel_len = conv_params.shape[0] - 1
    state_two = conv_params.shape[1] * shards - inner_width
    if sequences != 2 or places != shards or state_two != 2 * Q:
        raise ValueError("unexpected sizes")
    own_width = inner_width // places
    heads = head_count // places
    width = inner_width // head_count

    def swap(x):
        return lax.ppermute(x, "seq", [(i, i ^ 1) for i in range(group)])

    def along(x, step):
        return lax.ppermute(
            x, "seq", [(i, (i - 2 * step) % group) for i in range(group)]
        )

    def across(x, mask):
        return lax.ppermute(x, "wshard", [(i, i ^ mask) for i in range(shards)])

    def shard_gather(x):
        found = jnp.stack([x] + [across(x, mask) for mask in range(1, shards)])
        return jnp.stack([pieces_for(found, shard ^ k) for k in range(shards)])

    small = jnp.concatenate(
        [norm_gain, gate_gain, conv_params.reshape(-1), head_params.reshape(-1)]
    )
    small_all = shard_gather(small)
    at_gate = norm_gain.shape[0]
    at_conv = at_gate + gate_gain.shape[0]
    at_head = at_conv + conv_params.size
    gain_f = small_all[:, :at_gate].reshape(-1).astype(f32)
    gate_f = small_all[:, at_gate:at_conv].reshape(-1).astype(f32)
    conv_f = (
        small_all[:, at_conv:at_head]
        .reshape(shards, kernel_len + 1, -1)
        .transpose(1, 0, 2)
        .reshape(kernel_len + 1, -1)
        .astype(f32)
    )
    head_f = (
        small_all[:, at_head:].reshape(shards, 3, -1).transpose(1, 0, 2).reshape(3, -1).astype(f32)
    )
    taps = jnp.concatenate(
        [
            lax.dynamic_slice_in_dim(conv_f, place * own_width, own_width, 1),
            conv_f[:, inner_width:],
        ],
        axis=1,
    )
    channels = taps.shape[1]
    head_own = lax.dynamic_slice_in_dim(head_f, place * heads, heads, 1)
    gate_own = lax.dynamic_slice_in_dim(gate_f, place * own_width, own_width, 0)
    skip_gain = jnp.pad(
        jnp.stack([jnp.repeat(head_own[2], width), gate_own]), ((0, 0), (0, state_two))
    )
    chan = jnp.concatenate(
        [taps, jnp.zeros((6 - taps.shape[0], channels), f32), skip_gain], axis=0
    ).T
    rates = -jnp.exp(head_own[0])
    head_table = jnp.pad(
        jnp.stack([rates, head_own[1]], axis=1), ((0, HP - heads), (0, Q - 2))
    )

    tokens = block_input.astype(f32)
    scale = lax.rsqrt(jnp.mean(tokens * tokens, axis=-1, keepdims=True) + norm_eps)
    normed = (tokens * scale * gain_f).astype(bf16)

    def join(kept, other):
        return jnp.where(core == 0, jnp.concatenate([kept, other]), jnp.concatenate([other, kept]))

    def to_sequence(x):
        kept = lax.dynamic_index_in_dim(x, core, 0, keepdims=False)
        other = swap(lax.dynamic_index_in_dim(x, 1 - core, 0, keepdims=False))
        return join(kept, other)

    def to_tokens(x):
        halves = x.reshape(2, local_len, -1)
        kept = lax.dynamic_index_in_dim(halves, core, 0, keepdims=True)
        other = swap(lax.dynamic_index_in_dim(halves, 1 - core, 0, keepdims=True))
        return join(kept, other)

    def line_gather(x):
        return jnp.stack([x] + [along(x, step) for step in range(1, places)])

    def in_order(found):
        stacked = jnp.stack(found)
        return jnp.stack([pieces_for(stacked, (place - k) % places) for k in range(places)])

    order = (jnp.arange(places, dtype=jnp.int32) - place) % places
    normed_all = line_gather(to_sequence(normed))
    cot_all = line_gather(to_sequence(cotangent))

    half_cols = jnp.concatenate(
        [
            lax.dynamic_slice_in_dim(
                inproj_weight, core * inner_width + place * own_width, own_width, 1
            ),
            lax.dynamic_slice_in_dim(inproj_weight, 2 * inner_width + core * Q, Q, 1),
            jnp.pad(
                lax.dynamic_slice_in_dim(
                    inproj_weight, 2 * inner_width + state_two + place * heads, heads, 1
                ),
                ((0, 0), (0, HP - heads)),
            ),
        ],
        axis=1,
    ).T
    found = shard_gather(half_cols)
    half = found.transpose(1, 0, 2).reshape(half_cols.shape[0], model_width)
    other_half = swap(half)
    first = jnp.where(core == 0, half, other_half)
    second = jnp.where(core == 0, other_half, half)
    weight = jnp.concatenate(
        [
            first[:own_width],
            second[:own_width],
            first[own_width : own_width + Q],
            second[own_width : own_width + Q],
            half[own_width + Q :],
        ]
    )
    outproj_all = lax.all_gather(outproj_weight, "wshard", axis=0, tiled=True)
    outproj_own = lax.dynamic_slice_in_dim(outproj_all, place * own_width, own_width, 0)

    gates, values, conv, sent, table, states = run_forward(
        order, normed_all, weight, chan, head_table, own_width, heads, kernel_len
    )
    dbranch, stat = run_statistics(order, gates, sent, cot_all, outproj_own, chan)
    stat = stat[:2]
    stat = stat + sum(along(stat, step) for step in range(1, places))
    grms = lax.rsqrt(stat[0] / inner_width + norm_eps)
    stats = jnp.pad(
        jnp.stack([grms, grms * grms * (stat[1] / inner_width)]), ((0, 6), (0, 0))
    )
    dproj, branch, conv_acc, head_acc = run_backward(
        order, gates, sent, dbranch, conv, values, table, states, stats, chan, head_table,
        heads, kernel_len, places,
    )
    token_block = 2 * local_len
    flat = places * token_block

    def columns(x, m):
        return x[:, m * token_block : (m + 1) * token_block]

    branch_all = in_order([along(columns(branch, m), -m) if m else columns(branch, 0) for m in range(places)])
    out = dot_tn(branch_all.reshape(inner_width, token_block), outproj_all)
    block_output = tokens + to_tokens(out)

    dnormed_part = lax.dot_general(
        dproj, weight, (((0,), (0,)), ((), ())), preferred_element_type=f32
    ).astype(bf16)
    dnormed = dnormed_part[:token_block].astype(f32)
    for m in range(1, places):
        dnormed = dnormed + along(dnormed_part[m * token_block : (m + 1) * token_block], -m).astype(f32)
    dn_scaled = to_tokens(dnormed) * gain_f
    input_grad = (
        cotangent.astype(f32)
        + scale * dn_scaled
        - tokens * scale * scale * scale * jnp.mean(dn_scaled * tokens, axis=-1, keepdims=True)
    )

    def over_cores(x, axis):
        kept = lax.dynamic_index_in_dim(x, core, axis, keepdims=False)
        other = lax.dynamic_index_in_dim(x, 1 - core, axis, keepdims=False)
        return (kept.astype(f32) + swap(other).astype(f32)).astype(bf16)

    def over_shards(x):
        total = pieces_for(x, shard).astype(f32)
        for mask in range(1, shards):
            total = total + across(pieces_for(x, shard ^ mask), mask).astype(f32)
        return total

    in_rows = inproj_mean.shape[0]
    inproj_part = lax.dot_general(
        normed_all.reshape(flat, model_width), dproj, (((0,), (1,)), ((), ())), preferred_element_type=f32
    ).astype(bf16)
    inproj_part = over_cores(inproj_part.reshape(shards, places, 2, in_rows, -1), 2)
    inproj_part = over_shards(inproj_part).astype(bf16)
    received = in_order(
        [pieces_for(inproj_part, place)]
        + [along(pieces_for(inproj_part, (place + m) % places), -m) for m in range(1, places)]
    ).astype(f32)
    side = lambda lo, hi: received[:, :, lo:hi].transpose(1, 0, 2).reshape(in_rows, -1)
    at_shared = 2 * own_width
    inproj_grad = jnp.concatenate(
        [
            side(0, own_width),
            side(own_width, at_shared),
            jnp.sum(received[:, :, at_shared : at_shared + state_two], axis=0),
            side(at_shared + state_two, at_shared + state_two + heads),
        ],
        axis=1,
    )
    out_rows = outproj_mean.shape[0]
    outproj_part = jnp.dot(branch, cot_all.reshape(flat, model_width), preferred_element_type=f32).astype(bf16)
    outproj_part = over_cores(outproj_part.reshape(places, 2, out_rows, model_width), 1)
    outproj_part = over_shards(outproj_part)
    outproj_grad = lax.ppermute(
        outproj_part,
        ("wshard", "seq"),
        [
            (a * group + 2 * b + c, b * group + 2 * a + c)
            for a in range(shards)
            for b in range(places)
            for c in range(2)
        ],
    )

    conv_sums = jnp.sum(conv_acc, axis=-1)
    conv_part = jnp.concatenate(
        [
            lax.dynamic_update_slice_in_dim(
                jnp.zeros((kernel_len + 1, inner_width), f32),
                conv_sums[:, :own_width],
                place * own_width,
                1,
            ),
            conv_sums[:, own_width:],
        ],
        axis=1,
    )
    head_sums = jnp.sum(head_acc, axis=-1)[:, :heads]
    head_sums = jnp.concatenate([head_sums[:1] * rates, head_sums[1:]])
    head_part = lax.dynamic_update_slice_in_dim(
        jnp.zeros((3, head_count), f32), head_sums, place * heads, 1
    )
    sums = lax.psum(
        jnp.concatenate([conv_part.reshape(-1), head_part.reshape(-1)]), ("wshard", "seq")
    )
    conv_total = sums[: conv_part.size].reshape(conv_part.shape)
    head_total = sums[conv_part.size :].reshape(3, head_count)
    conv_width = conv_mean.shape[1]
    conv_grad = lax.dynamic_slice_in_dim(
        conv_total, (shard * group + seq_index) * conv_width, conv_width, 1
    )
    head_width = head_params.shape[1]
    head_grad = lax.dynamic_slice_in_dim(head_total, shard * head_width, head_width, 1)

    def own_piece(param, count, axis_dim):
        return lax.dynamic_slice_in_dim(param, seq_index * count, count, axis_dim).astype(f32)

    inproj_own = own_piece(inproj_weight, in_rows, 0)
    outproj_piece = own_piece(outproj_weight, out_rows, 0)
    norm_own = own_piece(norm_gain, in_rows, 0)
    gate_piece = own_piece(gate_gain, out_rows, 0)
    norm_grad = jnp.sum(inproj_own * inproj_grad, axis=1) / norm_own
    gate_grad = jnp.sum(outproj_piece * outproj_grad, axis=1) / gate_piece
    norm_res = adamw(norm_grad, norm_own, norm_mean, norm_square, 0.0)
    inproj_res = adamw(inproj_grad, inproj_own, inproj_mean, inproj_square, 0.1)
    conv_res = adamw(conv_grad, own_piece(conv_params, conv_width, 1), conv_mean, conv_square, 0.0)
    head_res = adamw(head_grad, head_params.astype(f32), head_mean, head_square, 0.0)
    gate_res = adamw(gate_grad, gate_piece, gate_mean, gate_square, 0.0)
    outproj_res = adamw(outproj_grad, outproj_piece, outproj_mean, outproj_square, 0.1)
    return (
        block_output,
        input_grad,
        norm_res[0],
        norm_res[1],
        norm_res[2],
        norm_res[3],
        inproj_res[0],
        inproj_res[1],
        inproj_res[2],
        inproj_res[3],
        conv_res[0],
        conv_res[1],
        conv_res[2],
        conv_res[3],
        head_res[0],
        head_res[1],
        head_res[2],
        head_res[3],
        gate_res[0],
        gate_res[1],
        gate_res[2],
        gate_res[3],
        outproj_res[0],
        outproj_res[1],
        outproj_res[2],
        outproj_res[3],
    )


def solution(mesh):
    placed = (
        P("wshard", "seq", None),
        P("wshard", "seq", None),
        P("wshard"),
        P(("wshard", "seq")),
        P(("wshard", "seq")),
        P("wshard", None),
        P(("wshard", "seq"), None),
        P(("wshard", "seq"), None),
        P(None, "wshard"),
        P(None, ("wshard", "seq")),
        P(None, ("wshard", "seq")),
        P(None, "wshard"),
        P(None, "wshard"),
        P(None, "wshard"),
        P("wshard"),
        P(("wshard", "seq")),
        P(("wshard", "seq")),
        P("wshard", None),
        P(("wshard", "seq"), None),
        P(("wshard", "seq"), None),
    )
    return jax.shard_map(
        local,
        mesh=mesh,
        in_specs=placed,
        out_specs=(
            P("wshard", "seq", None),
            P("wshard", "seq", None),
            P(("wshard", "seq")),
            P(("wshard", "seq")),
            P(("wshard", "seq")),
            P(("wshard", "seq")),
            P(("wshard", "seq"), None),
            P(("wshard", "seq"), None),
            P(("wshard", "seq"), None),
            P(("wshard", "seq"), None),
            P(None, ("wshard", "seq")),
            P(None, ("wshard", "seq")),
            P(None, ("wshard", "seq")),
            P(None, ("wshard", "seq")),
            P(None, "wshard"),
            P(None, "wshard"),
            P(None, "wshard"),
            P(None, "wshard"),
            P(("wshard", "seq")),
            P(("wshard", "seq")),
            P(("wshard", "seq")),
            P(("wshard", "seq")),
            P(("wshard", "seq"), None),
            P(("wshard", "seq"), None),
            P(("wshard", "seq"), None),
            P(("wshard", "seq"), None),
        ),
        check_vma=False,
    )
```

```python
import functools

import jax
import jax.numpy as jnp
from jax import lax
from jax.experimental import pallas as pl
from jax.experimental.pallas import tpu as pltpu
from jax.sharding import PartitionSpec as P

norm_eps = 1e-05
adam_eps = 1e-08
learn_rate = 0.02
beta_one = 0.9
beta_two = 0.999
first_fix = 1.0 - 0.9**10
second_fix = 1.0 - 0.999**10

f32 = jnp.float32
bf16 = jnp.bfloat16
Q = 128
HP = 16
FLOOR = -1e30
MIB = 1024 * 1024


def dot_nn(a, b):
    return lax.dot_general(a, b, (((1,), (0,)), ((), ())), preferred_element_type=f32)


def dot_nt(a, b):
    return lax.dot_general(a, b, (((1,), (1,)), ((), ())), preferred_element_type=f32)


def dot_tn(a, b):
    return lax.dot_general(a, b, (((0,), (0,)), ((), ())), preferred_element_type=f32)


def sigmoid(a):
    return 1.0 / (1.0 + jnp.exp(-a))


def lanes(shape):
    return lax.broadcasted_iota(jnp.int32, shape, 1)


def earlier_by(current, previous, lane, shift):
    return pltpu.roll(jnp.where(lane >= Q - shift, previous, current), shift, 1)


def later_by(current, following, lane, shift):
    return pltpu.roll(jnp.where(lane < shift, following, current), Q - shift, 1)


def running_sum(a, lane):
    shift = 1
    while shift < Q:
        a = a + jnp.where(lane >= shift, pltpu.roll(a, shift, 1), 0.0)
        shift *= 2
    return a


def running_sum_back(a, lane):
    shift = 1
    while shift < Q:
        a = a + jnp.where(lane < Q - shift, pltpu.roll(a, Q - shift, 1), 0.0)
        shift *= 2
    return a


def join_weight(own_width, channels, core, own_ref, other_ref, weight_ref):
    shards, _, depth = own_ref.shape
    for even in range(2):

        @pl.when(core == even)
        def _(first=(own_ref, other_ref)[even], second=(other_ref, own_ref)[even]):
            for at in range(shards):
                here = slice(at * depth, (at + 1) * depth)
                low = 2 * own_width
                weight_ref[:own_width, here] = first[at, :own_width, :]
                weight_ref[own_width:low, here] = second[at, :own_width, :]
                weight_ref[low : low + Q, here] = first[at, own_width : own_width + Q, :]
                weight_ref[low + Q : low + 2 * Q, here] = second[at, own_width : own_width + Q, :]
                weight_ref[low + 2 * Q :, here] = own_ref[at, own_width + Q : own_width + Q + HP, :]


def mixer_forward(own_width, heads, kernel_len, places, start, assemble, order_ref, *refs):
    token_refs = refs[:places]
    gain_ref, chan_ref, head_ref = refs[places : places + 3]
    given = refs[places + 3 : -14]
    (
        weight_out,
        normed_ref,
        gates_ref,
        values_ref,
        conv_ref,
        sent_ref,
        table_ref,
        state_ref,
        before,
        state,
        active,
        steps,
        inter,
        scaled,
    ) = refs[-14:]
    channels = chan_ref.shape[0]
    width = own_width // heads
    token_block = normed_ref.shape[0]

    @pl.when(pl.program_id(0) == 0)
    def _():
        before[...] = given[1][...] if start else jnp.zeros_like(before)
        state[...] = given[2][...] if start else jnp.zeros_like(state)
        if not assemble:
            weight_out[...] = jnp.zeros_like(weight_out)
        else:
            join_weight(own_width, channels, order_ref[places], *given[:2], weight_out)

    for piece in range(places):

        @pl.when(order_ref[start + pl.program_id(0)] == piece)
        def _(token_ref=token_refs[piece]):
            tokens = token_ref[...].astype(f32)
            scale = lax.rsqrt(jnp.mean(tokens * tokens, axis=1, keepdims=True) + norm_eps)
            normed_ref[...] = (tokens * scale * gain_ref[...]).astype(bf16)

    weight_ref = weight_out if assemble else given[0]
    normed = normed_ref[...]
    gates_ref[...] = dot_nt(weight_ref[0:own_width, :], normed)
    values_ref[...] = dot_nt(weight_ref[own_width : own_width + channels, :], normed).astype(bf16)
    steps[...] = dot_nt(weight_ref[own_width + channels :, :], normed).astype(bf16).astype(f32)
    lane = lanes((Q, Q))
    lane_head = lanes((HP, Q))
    causal = lax.broadcasted_iota(jnp.int32, (Q, Q), 0) <= lane

    def block(at, carry):
        here = pl.ds(pl.multiple_of(at * Q, Q), Q)

        def convolve(tile, inner):
            rows = pl.ds(pl.multiple_of(tile * Q, Q), Q)
            raw = values_ref[rows, here]
            current = raw.astype(f32)
            previous = before[rows, :].astype(f32)
            taps = chan_ref[rows, :]
            out = taps[:, kernel_len : kernel_len + 1] + taps[:, kernel_len - 1 : kernel_len] * current
            for shift in range(1, kernel_len):
                tap = kernel_len - 1 - shift
                out = out + taps[:, tap : tap + 1] * earlier_by(current, previous, lane, shift)
            before[rows, :] = raw
            conv_ref[rows, here] = out
            active[rows, :] = out * sigmoid(out)
            return inner

        lax.fori_loop(0, channels // Q, convolve, 0, unroll=True)
        drive = steps[:, here] + head_ref[:, 1:2]
        step = jnp.maximum(drive, 0.0) + jnp.log1p(jnp.exp(-jnp.abs(drive)))
        within = running_sum(step * head_ref[:, 0:1], lane_head)
        table_ref[0, :, here] = step
        table_ref[1, :, here] = within
        table_ref[2, :, here] = sigmoid(drive)
        within_col = jnp.transpose(within)
        total = within[:, Q - 1 : Q]
        grow = jnp.exp(within)
        tail = jnp.exp(total - within) * step
        total_decay = jnp.exp(total)
        b_rows = jnp.transpose(active[own_width : own_width + Q, :]).astype(bf16)
        c_cols = active[own_width + Q : own_width + 2 * Q, :].astype(bf16)
        scores = dot_nn(b_rows, c_cols)
        held = state[...].astype(bf16)
        state_ref[at] = held
        inter[...] = dot_nn(held, c_cols)
        for head in range(heads):
            rows = slice(head * width, (head + 1) * width)
            x = active[rows, :]
            decay = jnp.exp(
                jnp.where(causal, within[head : head + 1, :] - within_col[:, head : head + 1], FLOOR)
            )
            weights = (decay * scores).astype(bf16)
            driven = (x * step[head : head + 1, :]).astype(bf16)
            mixed = dot_nn(driven, weights)
            mixed = mixed + inter[rows, :] * grow[head : head + 1, :]
            mixed = mixed + chan_ref[rows, 6:7] * x
            sent_ref[rows, here] = mixed.astype(bf16)
            scaled[rows, :] = (x * tail[head : head + 1, :]).astype(bf16)
            state[rows, :] = state[rows, :] * total_decay[head : head + 1, :]
        state[...] += dot_nn(scaled[...], b_rows)
        return carry

    lax.fori_loop(0, token_block // Q, block, 0, unroll=True)


def gate_statistics(places, order_ref, gates_ref, sent_ref, *refs):
    cot_refs = refs[:places]
    weight_ref, chan_ref, cot_all, dbranch_ref, stat_ref = refs[places:]
    for piece in range(places):

        @pl.when(order_ref[pl.program_id(0)] == piece)
        def _(cot_ref=cot_refs[piece]):
            cot_all[...] = cot_ref[...]

    dbranch = dot_nt(weight_ref[...], cot_all[...])
    dbranch_ref[...] = dbranch
    gates = gates_ref[...]
    gated = sent_ref[...].astype(f32) * (gates * sigmoid(gates))
    square = jnp.sum(gated * gated, axis=0, keepdims=True)
    cross = jnp.sum(gated * (dbranch * chan_ref[0 : gates.shape[0], 7:8]), axis=0, keepdims=True)
    stat_ref[...] = jnp.concatenate([square, cross, jnp.zeros((6, square.shape[1]), f32)], axis=0)


def gate_backward(
    order_ref, gates_ref, sent_ref, dbranch_ref, stat_ref, chan_ref, dsent_ref, dgates_ref, branch_ref
):
    grms = stat_ref[0:1, :]
    pull = stat_ref[1:2, :]

    def gate(tile, carry):
        rows = pl.ds(pl.multiple_of(tile * Q, Q), Q)
        gates = gates_ref[rows, :]
        sent = sent_ref[rows, :].astype(f32)
        gain = chan_ref[rows, 7:8]
        sig = sigmoid(gates)
        swish = gates * sig
        gated = sent * swish
        dgated = grms * (dbranch_ref[rows, :] * gain - gated * pull)
        dsent_ref[rows, :] = (dgated * swish).astype(bf16)
        dgates_ref[rows, :] = (dgated * sent * sig * (1.0 + gates * (1.0 - sig))).astype(bf16)
        branch_ref[rows, :] = (gated * grms * gain).astype(bf16)
        return carry

    lax.fori_loop(0, gates_ref.shape[0] // Q, gate, 0, unroll=True)


def mixer_backward(
    own_width,
    heads,
    kernel_len,
    fresh,
    order_ref,
    dsent_ref,
    conv_ref,
    values_ref,
    table_ref,
    state_ref,
    chan_ref,
    head_ref,
    *refs,
):
    (
        dproj_ref,
        conv_acc,
        head_acc,
        adjoint,
        following,
        active,
        dactive,
        inter,
        reach,
        driven,
        tailed,
        rows_scr,
    ) = refs[-12:]
    channels = chan_ref.shape[0]
    width = own_width // heads
    token_block = dsent_ref.shape[1]

    @pl.when(pl.program_id(0) == 0)
    def _():
        for at, held in enumerate((conv_acc, head_acc, adjoint, following)):
            held[...] = jnp.zeros_like(held) if fresh else refs[at][...]
        rows_scr[...] = jnp.zeros_like(rows_scr)

    lane = lanes((Q, Q))
    sub = lax.broadcasted_iota(jnp.int32, (Q, Q), 0)
    lane_head = lanes((HP, Q))
    causal = sub >= lane
    strict = (sub < lane).astype(bf16)

    def block(index, carry):
        at = token_block // Q - 1 - index
        here = pl.ds(pl.multiple_of(at * Q, Q), Q)

        def activate(tile, inner):
            rows = pl.ds(pl.multiple_of(tile * Q, Q), Q)
            conv = conv_ref[rows, here]
            active[rows, :] = conv * sigmoid(conv)
            return inner

        lax.fori_loop(0, channels // Q, activate, 0, unroll=True)
        step = table_ref[0, :, here]
        within = table_ref[1, :, here]
        within_col = jnp.transpose(within)
        total = within[:, Q - 1 : Q]
        grow = jnp.exp(within)
        fade = jnp.exp(total - within)
        tail = fade * step
        total_decay = jnp.exp(total)
        b_cols_f = active[own_width : own_width + Q, :]
        c_cols_f = active[own_width + Q : own_width + 2 * Q, :]
        b_cols = b_cols_f.astype(bf16)
        c_cols = c_cols_f.astype(bf16)
        c_rows = jnp.transpose(c_cols_f).astype(bf16)
        scores = dot_nn(c_rows, b_cols)
        held = state_ref[at]
        after = adjoint[...].astype(bf16)
        inter[...] = dot_nn(held, c_cols)
        reach[...] = dot_nn(after, b_cols)
        dscores = jnp.zeros((Q, Q), f32)
        blank = jnp.zeros((width, Q), bf16)
        for pair in range(heads // 2):
            turned = jnp.transpose(dsent_ref[pair * 2 * width : (pair + 1) * 2 * width, here].astype(f32)).astype(bf16)
            for half in range(2):
                head = 2 * pair + half
                rows = slice(head * width, (head + 1) * width)
                one = slice(head, head + 1)
                x = active[rows, :]
                x_low = x.astype(bf16)
                grad_low = dsent_ref[rows, here]
                grad = grad_low.astype(f32)
                decay = jnp.exp(
                    jnp.where(causal, within_col[:, head : head + 1] - within[one, :], FLOOR)
                )
                lone = jnp.concatenate([x_low, blank] if half == 0 else [blank, x_low], axis=0)
                dweights = dot_nn(turned, lone)
                spread = decay * dweights * step[one, :]
                dscores = dscores + spread
                crossing = dot_nn((spread * scores).astype(bf16), strict)
                rows_scr[0, one, :] = jnp.sum(jnp.where(causal, crossing, 0.0), axis=0, keepdims=True)
                far = reach[rows, :]
                back = dot_nn(grad_low, (decay * scores).astype(bf16)) + far * fade[one, :]
                rows_scr[1, one, :] = jnp.sum(x * back, axis=0, keepdims=True)
                rows_scr[2, one, :] = jnp.sum(x * far, axis=0, keepdims=True) * tail[one, :]
                rows_scr[3, one, :] = jnp.sum(grad * inter[rows, :], axis=0, keepdims=True) * grow[one, :]
                rows_scr[4, one, :] = jnp.sum(grad * x, axis=0, keepdims=True)
                old = adjoint[rows, :]
                rows_scr[5, one, :] = jnp.sum(old * held[rows, :].astype(f32), axis=0, keepdims=True)
                dactive[rows, :] = back * step[one, :] + chan_ref[rows, 6:7] * grad
                driven[rows, :] = (grad * grow[one, :]).astype(bf16)
                tailed[rows, :] = (x * tail[one, :]).astype(bf16)
                adjoint[rows, :] = old * total_decay[one, :]
        dlow = dscores.astype(bf16)
        dactive[own_width : own_width + Q, :] = dot_nn(c_cols, dlow) + dot_tn(after, tailed[...])
        dactive[own_width + Q : own_width + 2 * Q, :] = dot_nt(b_cols, dlow) + dot_tn(held, driven[...])
        adjoint[...] += dot_nn(driven[...], c_rows)
        ahead = rows_scr[2]
        dlog = (
            rows_scr[0]
            + running_sum_back(rows_scr[3], lane_head)
            + (running_sum(ahead, lane_head) - ahead)
            + total_decay * jnp.sum(rows_scr[5], axis=1, keepdims=True)
        )
        dstep = (rows_scr[1] + head_ref[:, 0:1] * dlog) * table_ref[2, :, here]
        dproj_ref[channels:, here] = dstep.astype(bf16)
        head_acc[0] += step * dlog
        head_acc[1] += dstep
        head_acc[2] += rows_scr[4]

        def convolve(tile, inner):
            rows = pl.ds(pl.multiple_of(tile * Q, Q), Q)
            conv = conv_ref[rows, here]
            sig = sigmoid(conv)
            dconv = dactive[rows, :] * sig * (1.0 + conv * (1.0 - sig))
            taps = chan_ref[rows, :]
            raw = values_ref[rows, here].astype(f32)
            nxt = following[rows, :]
            dvalue = taps[:, kernel_len - 1 : kernel_len] * dconv
            conv_acc[kernel_len - 1, rows, :] += raw * dconv
            for shift in range(1, kernel_len):
                tap = kernel_len - 1 - shift
                moved = later_by(dconv, nxt, lane, shift)
                dvalue = dvalue + taps[:, tap : tap + 1] * moved
                conv_acc[tap, rows, :] += raw * moved
            conv_acc[kernel_len, rows, :] += dconv
            following[rows, :] = dconv
            dproj_ref[rows, here] = dvalue.astype(bf16)
            return inner

        lax.fori_loop(0, channels // Q, convolve, 0, unroll=True)
        return carry

    lax.fori_loop(0, token_block // Q, block, 0, unroll=True)


def run_forward(
    order, tokens, gain, chan, head_table, own_width, heads, kernel_len, start, count, weight, carry, written
):
    places = len(tokens)
    token_block, model_width = tokens[0].shape
    channels = chan.shape[0]
    full = places * token_block
    weight_shape = (own_width + channels + HP, model_width)
    assemble = len(weight) == 2
    solid = lambda x: pl.BlockSpec(x.shape, lambda k, order: (0,) * x.ndim)
    fixed = lambda k, order: (0, 0)
    cols = lambda k, order: (0, start + k)
    stored = lambda k, order: (order[start + k], 0, 0)
    spec = pltpu.PrefetchScalarGridSpec(
        num_scalar_prefetch=1,
        grid=(count,),
        in_specs=[solid(x) for x in (*tokens, gain, chan, head_table, *weight, *carry)]
        + [pl.BlockSpec(memory_space=pl.ANY)] * len(written),
        out_specs=[
            pl.BlockSpec(weight_shape if assemble else (8, Q), fixed),
            pl.BlockSpec((None, token_block, model_width), stored),
            pl.BlockSpec((own_width, token_block), cols),
            pl.BlockSpec((channels, token_block), cols),
            pl.BlockSpec((channels, token_block), cols),
            pl.BlockSpec((own_width, token_block), cols),
            pl.BlockSpec((3, HP, token_block), lambda k, order: (0, 0, start + k)),
            pl.BlockSpec((token_block // Q, own_width, Q), lambda k, order: (start + k, 0, 0)),
            pl.BlockSpec((channels, Q), fixed),
            pl.BlockSpec((own_width, Q), fixed),
        ],
        scratch_shapes=[
            pltpu.VMEM((channels, Q), f32),
            pltpu.VMEM((HP, token_block), f32),
            pltpu.VMEM((own_width, Q), f32),
            pltpu.VMEM((own_width, Q), bf16),
        ],
    )
    found = pl.pallas_call(
        functools.partial(mixer_forward, own_width, heads, kernel_len, places, start, assemble),
        grid_spec=spec,
        out_shape=[
            jax.ShapeDtypeStruct(weight_shape if assemble else (8, Q), bf16),
            jax.ShapeDtypeStruct((places, token_block, model_width), bf16),
            jax.ShapeDtypeStruct((own_width, full), f32),
            jax.ShapeDtypeStruct((channels, full), bf16),
            jax.ShapeDtypeStruct((channels, full), f32),
            jax.ShapeDtypeStruct((own_width, full), bf16),
            jax.ShapeDtypeStruct((3, HP, full), f32),
            jax.ShapeDtypeStruct((full // Q, own_width, Q), bf16),
            jax.ShapeDtypeStruct((channels, Q), bf16),
            jax.ShapeDtypeStruct((own_width, Q), f32),
        ],
        input_output_aliases={
            4 + places + len(weight) + len(carry) + i: 1 + i for i in range(len(written))
        },
        compiler_params=pltpu.CompilerParams(
            dimension_semantics=("arbitrary",), vmem_limit_bytes=56 * MIB
        ),
        cost_estimate=pl.CostEstimate(
            flops=8 * count * token_block * model_width * weight_shape[0],
            bytes_accessed=8 * MIB * count,
            transcendentals=MIB * count,
        ),
        name="mixer_forward",
    )(order, *tokens, gain, chan, head_table, *weight, *carry, *written)
    return found[0] if assemble else weight[0], found[1:8], found[8:]


def run_statistics(order, gates, sent, cotangents, weight, chan):
    places = len(cotangents)
    token_block, model_width = cotangents[0].shape
    own_width, full = gates.shape
    fixed = lambda k, order: (0, 0)
    cols = lambda k, order: (0, k)
    spec = pltpu.PrefetchScalarGridSpec(
        num_scalar_prefetch=1,
        grid=(places,),
        in_specs=[
            pl.BlockSpec((own_width, token_block), cols),
            pl.BlockSpec((own_width, token_block), cols),
            *[pl.BlockSpec((token_block, model_width), fixed)] * places,
            pl.BlockSpec(weight.shape, fixed),
            pl.BlockSpec(chan.shape, fixed),
        ],
        out_specs=[
            pl.BlockSpec((None, token_block, model_width), lambda k, order: (order[k], 0, 0)),
            pl.BlockSpec((own_width, token_block), cols),
            pl.BlockSpec((8, token_block), cols),
        ],
    )
    return pl.pallas_call(
        functools.partial(gate_statistics, places),
        grid_spec=spec,
        out_shape=[
            jax.ShapeDtypeStruct((places, token_block, model_width), bf16),
            jax.ShapeDtypeStruct((own_width, full), f32),
            jax.ShapeDtypeStruct((8, full), f32),
        ],
        compiler_params=pltpu.CompilerParams(
            dimension_semantics=("arbitrary",), vmem_limit_bytes=24 * MIB
        ),
        cost_estimate=pl.CostEstimate(
            flops=2 * full * model_width * own_width,
            bytes_accessed=16 * MIB,
            transcendentals=own_width * full,
        ),
        name="gate_statistics",
    )(order, gates, sent, *cotangents, weight, chan)


def run_gate(order, gates, sent, dbranch, stats, chan, places):
    own_width, full = gates.shape
    token_block = full // places
    cols = lambda k, order: (0, k)
    turned = lambda k, order: (0, order[k])
    spec = pltpu.PrefetchScalarGridSpec(
        num_scalar_prefetch=1,
        grid=(places,),
        in_specs=[
            pl.BlockSpec((own_width, token_block), cols),
            pl.BlockSpec((own_width, token_block), cols),
            pl.BlockSpec((own_width, token_block), cols),
            pl.BlockSpec((8, token_block), cols),
            pl.BlockSpec(chan.shape, lambda k, order: (0, 0)),
        ],
        out_specs=[
            pl.BlockSpec((own_width, token_block), cols),
            pl.BlockSpec((own_width, token_block), turned),
            pl.BlockSpec((own_width, token_block), turned),
        ],
    )
    return pl.pallas_call(
        gate_backward,
        grid_spec=spec,
        out_shape=[jax.ShapeDtypeStruct((own_width, full), bf16)] * 3,
        compiler_params=pltpu.CompilerParams(
            dimension_semantics=("arbitrary",), vmem_limit_bytes=20 * MIB
        ),
        cost_estimate=pl.CostEstimate(
            flops=20 * own_width * full, bytes_accessed=14 * own_width * full, transcendentals=own_width * full
        ),
        name="gate_backward",
    )(order, gates, sent, dbranch, stats, chan)


def run_backward(
    order, dsent, conv, values, table, states, chan, head_table, heads, kernel_len, places, start, count, carry, written
):
    own_width, full = dsent.shape
    channels = chan.shape[0]
    token_block = full // places
    out_rows = channels + HP
    last = start - 1
    fixed = lambda k, order: (0, 0)
    solid = lambda k, order: (0, 0, 0)
    cols = lambda k, order: (0, last - k)
    kept = [
        pl.BlockSpec((kernel_len + 1, channels, Q), solid),
        pl.BlockSpec((3, HP, Q), solid),
        pl.BlockSpec((own_width, Q), fixed),
        pl.BlockSpec((channels, Q), fixed),
    ]
    spec = pltpu.PrefetchScalarGridSpec(
        num_scalar_prefetch=1,
        grid=(count,),
        in_specs=[
            pl.BlockSpec((own_width, token_block), cols),
            pl.BlockSpec((channels, token_block), cols),
            pl.BlockSpec((channels, token_block), cols),
            pl.BlockSpec((3, HP, token_block), lambda k, order: (0, 0, last - k)),
            pl.BlockSpec((token_block // Q, own_width, Q), lambda k, order: (last - k, 0, 0)),
            pl.BlockSpec(chan.shape, fixed),
            pl.BlockSpec(head_table.shape, fixed),
        ]
        + kept[: len(carry)]
        + [pl.BlockSpec(memory_space=pl.ANY)] * len(written),
        out_specs=[pl.BlockSpec((out_rows, token_block), lambda k, order: (0, order[last - k]))] + kept,
        scratch_shapes=[
            pltpu.VMEM((channels, Q), f32),
            pltpu.VMEM((channels, Q), f32),
            pltpu.VMEM((own_width, Q), f32),
            pltpu.VMEM((own_width, Q), f32),
            pltpu.VMEM((own_width, Q), bf16),
            pltpu.VMEM((own_width, Q), bf16),
            pltpu.VMEM((6, HP, Q), f32),
        ],
    )
    found = pl.pallas_call(
        functools.partial(mixer_backward, own_width, heads, kernel_len, not carry),
        grid_spec=spec,
        out_shape=[jax.ShapeDtypeStruct((out_rows, full), bf16)]
        + [jax.ShapeDtypeStruct(x.block_shape, f32) for x in kept],
        input_output_aliases={8 + len(carry) + i: i for i in range(len(written))},
        compiler_params=pltpu.CompilerParams(
            dimension_semantics=("arbitrary",), vmem_limit_bytes=56 * MIB
        ),
        cost_estimate=pl.CostEstimate(
            flops=8 * 1024 * 1024 * 1024 * count,
            bytes_accessed=8 * 1024 * 1024 * count,
            transcendentals=1024 * 1024 * count,
        ),
        name="mixer_backward",
    )(order, dsent, conv, values, table, states, chan, head_table, *carry, *written)
    return found[:1], found[1:]


def token_gradient(dgates_ref, drest_ref, weight_ref, *out_refs):
    own_width = dgates_ref.shape[0]
    total = dot_tn(dgates_ref[...], weight_ref[:own_width, :]) + dot_tn(
        drest_ref[...], weight_ref[own_width:, :]
    )
    for piece, out_ref in enumerate(out_refs):

        @pl.when(pl.program_id(0) == piece)
        def _(out_ref=out_ref):
            out_ref[...] = total.astype(bf16)


def run_token_gradient(dgates, drest, weight, places):
    model_width = weight.shape[1]
    token_block = dgates.shape[1] // places
    fixed = lambda k: (0, 0)
    return pl.pallas_call(
        token_gradient,
        grid=(places,),
        in_specs=[
            pl.BlockSpec((dgates.shape[0], token_block), lambda k: (0, k)),
            pl.BlockSpec((drest.shape[0], token_block), lambda k: (0, k)),
            pl.BlockSpec(weight.shape, fixed),
        ],
        out_specs=[pl.BlockSpec((token_block, model_width), fixed)] * places,
        out_shape=[jax.ShapeDtypeStruct((token_block, model_width), bf16)] * places,
        compiler_params=pltpu.CompilerParams(
            dimension_semantics=("arbitrary",), vmem_limit_bytes=32 * MIB
        ),
        cost_estimate=pl.CostEstimate(
            flops=2 * dgates.shape[1] * weight.size, bytes_accessed=12 * MIB, transcendentals=0
        ),
        name="token_gradient",
    )(dgates, drest, weight)


def weight_gradient(in_rows, core_ref, normed_ref, grad_ref, kept_ref, given_ref):
    total = lax.dot_general(
        normed_ref[...], grad_ref[...], (((0,), (1,)), ((), ())), preferred_element_type=f32
    ).astype(bf16)
    for core in range(2):

        @pl.when(core_ref[0] == core)
        def _(core=core):
            for at in range(kept_ref.shape[0]):
                low = (2 * at + core) * in_rows
                kept_ref[at] = total[low : low + in_rows, :]
                low = (2 * at + 1 - core) * in_rows
                given_ref[at] = total[low : low + in_rows, :]


def run_weight_gradient(core, normed, grad, in_rows, steps):
    full, model_width = normed.shape
    columns = grad.shape[0]
    tile = model_width // steps
    groups = tile // (2 * in_rows)
    spec = pltpu.PrefetchScalarGridSpec(
        num_scalar_prefetch=1,
        grid=(steps,),
        in_specs=[
            pl.BlockSpec((full, tile), lambda k, core: (0, k)),
            pl.BlockSpec(grad.shape, lambda k, core: (0, 0)),
        ],
        out_specs=[pl.BlockSpec((groups, in_rows, columns), lambda k, core: (k, 0, 0))] * 2,
    )
    return pl.pallas_call(
        functools.partial(weight_gradient, in_rows),
        grid_spec=spec,
        out_shape=[jax.ShapeDtypeStruct((groups * steps, in_rows, columns), bf16)] * 2,
        compiler_params=pltpu.CompilerParams(
            dimension_semantics=("arbitrary",), vmem_limit_bytes=32 * MIB
        ),
        cost_estimate=pl.CostEstimate(
            flops=2 * full * model_width * columns, bytes_accessed=8 * MIB, transcendentals=0
        ),
        name="weight_gradient",
    )(core, normed, grad)


def adamw(grad, weight, first, second, decay):
    first_new = beta_one * first + (1.0 - beta_one) * grad
    second_new = beta_two * second + (1.0 - beta_two) * grad * grad
    update = -learn_rate * (
        first_new / first_fix / (jnp.sqrt(second_new / second_fix) + adam_eps) + decay * weight
    )
    return (grad, first_new, second_new, update)


def pieces_for(stacked, index):
    return lax.dynamic_index_in_dim(stacked, index, 0, keepdims=False)


def local(
    block_input,
    cotangent,
    norm_gain,
    norm_mean,
    norm_square,
    inproj_weight,
    inproj_mean,
    inproj_square,
    conv_params,
    conv_mean,
    conv_square,
    head_params,
    head_mean,
    head_square,
    gate_gain,
    gate_mean,
    gate_square,
    outproj_weight,
    outproj_mean,
    outproj_square,
):
    group = lax.axis_size("seq")
    shards = lax.axis_size("wshard")
    seq_index = lax.axis_index("seq")
    shard = lax.axis_index("wshard")
    places = group // 2
    place = seq_index // 2
    core = seq_index % 2
    sequences, local_len, model_width = block_input.shape
    inner_width = gate_gain.shape[0] * shards
    head_count = head_params.shape[1] * shards
    kernel_len = conv_params.shape[0] - 1
    state_two = conv_params.shape[1] * shards - inner_width
    if sequences != 2 or places != shards or state_two != 2 * Q:
        raise ValueError("unexpected sizes")
    own_width = inner_width // places
    heads = head_count // places
    width = inner_width // head_count

    def swap(x):
        return lax.ppermute(x, "seq", [(i, i ^ 1) for i in range(group)])

    def along(x, mask, among=None):
        pairs = [(i, i ^ (2 * mask)) for i in range(group)]
        if among is not None:
            pairs = [(a, b) for a, b in pairs if b // 2 in among]
        return lax.ppermute(x, "seq", pairs)

    def across(x, mask):
        return lax.ppermute(x, "wshard", [(i, i ^ mask) for i in range(shards)])

    def shard_exchange(x):
        return lax.all_to_all(x, "wshard", split_axis=0, concat_axis=0, tiled=True)

    def shard_gather(x):
        return shard_exchange(jnp.broadcast_to(x[None], (shards,) + x.shape))

    def line_exchange(x):
        groups = [[2 * i + c for i in range(places)] for c in range(2)]
        return lax.all_to_all(
            x, "seq", split_axis=0, concat_axis=0, tiled=True, axis_index_groups=groups
        )

    small = jnp.concatenate(
        [norm_gain, gate_gain, conv_params.reshape(-1), head_params.reshape(-1)]
    )
    tokens = block_input.astype(f32)
    scale = lax.rsqrt(jnp.mean(tokens * tokens, axis=-1, keepdims=True) + norm_eps)

    def join(kept, other):
        return jnp.where(core == 0, jnp.concatenate([kept, other]), jnp.concatenate([other, kept]))

    def to_sequence(x):
        kept = lax.dynamic_index_in_dim(x, core, 0, keepdims=False)
        other = swap(lax.dynamic_index_in_dim(x, 1 - core, 0, keepdims=False))
        return join(kept, other)

    def to_tokens(x):
        halves = x.reshape(2, local_len, -1)
        kept = lax.dynamic_index_in_dim(halves, core, 0, keepdims=True)
        other = swap(lax.dynamic_index_in_dim(halves, 1 - core, 0, keepdims=True))
        return join(kept, other)

    def gather_first(x):
        return [along(x, mask) for mask in range(1, 3 if places == 4 else places)]

    def gather_second(x, first):
        if places != 4:
            return [x] + first
        middle = along(x, 3, (1, 2))
        ends = along(first[1], 1, (0, 3))
        return [x] + first + [jnp.where((place == 0) | (place == 3), ends, middle)]

    def scatter_first(pieces):
        if places != 4:
            return []
        return [along(pieces[3], 1, (1, 2)), along(pieces[3], 3, (1, 2))]

    def scatter_second(pieces, first):
        if places != 4:
            return [pieces[0]] + [along(pieces[mask], mask) for mask in range(1, places)]
        far = (pieces[2].astype(f32) + first[0].astype(f32)).astype(pieces[2].dtype)
        return [pieces[0], along(pieces[1], 1), along(far, 2), first[1]]

    def in_order(found):
        stacked = jnp.stack(found)
        return jnp.stack([pieces_for(stacked, place ^ k) for k in range(places)])

    order = jnp.concatenate(
        [jnp.arange(places, dtype=jnp.int32) ^ place, core.reshape(1).astype(jnp.int32)]
    )
    token_own = to_sequence(block_input)

    half_cols = jnp.concatenate(
        [
            lax.dynamic_slice_in_dim(
                inproj_weight, core * inner_width + place * own_width, own_width, 1
            ),
            lax.dynamic_slice_in_dim(inproj_weight, 2 * inner_width + core * Q, Q, 1),
            jnp.pad(
                lax.dynamic_slice_in_dim(
                    inproj_weight, 2 * inner_width + state_two + place * heads, heads, 1
                ),
                ((0, 0), (0, HP - heads)),
            ),
        ],
        axis=1,
    ).T
    shard_rows = half_cols.shape[1]
    small_rows = -(-small.shape[0] // (16 * shard_rows)) * 16
    small_pad = jnp.pad(small, (0, small_rows * shard_rows - small.shape[0]))
    sending = jnp.concatenate([half_cols, small_pad.reshape(small_rows, shard_rows)])
    sending = jnp.broadcast_to(sending[None], (shards,) + sending.shape)
    token_own, sending = lax.optimization_barrier((token_own, sending))
    token_first = gather_first(token_own)
    found = shard_exchange(sending)
    token_own, found, *token_first = lax.optimization_barrier((token_own, found, *token_first))
    small_all = found[:, half_cols.shape[0] :].reshape(shards, -1)
    at_gate = norm_gain.shape[0]
    at_conv = at_gate + gate_gain.shape[0]
    at_head = at_conv + conv_params.size
    gain_f = small_all[:, :at_gate].reshape(-1).astype(f32)
    gate_f = small_all[:, at_gate:at_conv].reshape(-1).astype(f32)
    conv_f = (
        small_all[:, at_conv:at_head]
        .reshape(shards, kernel_len + 1, -1)
        .transpose(1, 0, 2)
        .reshape(kernel_len + 1, -1)
        .astype(f32)
    )
    head_f = (
        small_all[:, at_head : small.shape[0]].reshape(shards, 3, -1).transpose(1, 0, 2).reshape(3, -1).astype(f32)
    )
    taps = jnp.concatenate(
        [
            lax.dynamic_slice_in_dim(conv_f, place * own_width, own_width, 1),
            conv_f[:, inner_width:],
        ],
        axis=1,
    )
    channels = taps.shape[1]
    head_own = lax.dynamic_slice_in_dim(head_f, place * heads, heads, 1)
    gate_own = lax.dynamic_slice_in_dim(gate_f, place * own_width, own_width, 0)
    skip_gain = jnp.pad(
        jnp.stack([jnp.repeat(head_own[2], width), gate_own]), ((0, 0), (0, state_two))
    )
    chan = jnp.concatenate(
        [taps, jnp.zeros((6 - taps.shape[0], channels), f32), skip_gain], axis=0
    ).T
    rates = -jnp.exp(head_own[0])
    head_table = jnp.pad(
        jnp.stack([rates, head_own[1]], axis=1), ((0, HP - heads), (0, Q - 2))
    )

    token_pieces = gather_second(token_own, token_first)
    other_found = swap(found)
    out_half = lax.dynamic_slice_in_dim(outproj_weight, core * (model_width // 2), model_width // 2, 1)
    out_half = jnp.broadcast_to(out_half[None], (shards,) + out_half.shape)
    out_half, found = lax.optimization_barrier((out_half, found))
    if shard_rows % Q == 0:
        weight = [found, other_found]
    else:
        turned = lambda x: x[:, : half_cols.shape[0]].transpose(1, 0, 2).reshape(-1, model_width)
        own_half, other_half = turned(found), turned(other_found)
        first = jnp.where(core == 0, own_half, other_half)
        second = jnp.where(core == 0, other_half, own_half)
        weight = [
            jnp.concatenate(
                [
                    first[:own_width],
                    second[:own_width],
                    first[own_width : own_width + Q],
                    second[own_width : own_width + Q],
                    own_half[own_width + Q :],
                ]
            )
        ]
    out_half = shard_exchange(out_half).reshape(inner_width, model_width // 2)
    cot_own, *token_pieces = lax.optimization_barrier((to_sequence(cotangent), *token_pieces))
    cot_first = gather_first(cot_own)

    def whole_columns(own, other):
        return jnp.where(
            core == 0, jnp.concatenate([own, other], axis=1), jnp.concatenate([other, own], axis=1)
        )

    def own_piece(param, count, axis_dim):
        return lax.dynamic_slice_in_dim(param, seq_index * count, count, axis_dim)

    def own_rows(x):
        return lax.dynamic_slice_in_dim(x, place * own_width, own_width, 0)


    forward = functools.partial(
        run_forward, order, token_pieces, gain_f[None], chan, head_table, own_width, heads, kernel_len
    )
    weight, written, carry = forward(0, places - 1, weight, [], [])
    inproj_own = own_piece(inproj_weight, inproj_mean.shape[0], 0)
    carry, cot_own, inproj_own, *cot_first = lax.optimization_barrier(
        (carry, cot_own, inproj_own, *cot_first)
    )
    cot_pieces = gather_second(cot_own, cot_first)
    weight, written, carry = forward(places - 1, 1, [weight], carry, written)
    out_rows_own = own_rows(out_half)
    out_rows_other = swap(out_rows_own)
    written, out_rows_other, *cot_pieces = lax.optimization_barrier(
        (written, out_rows_other, *cot_pieces)
    )
    normed_all, gates, values, conv, sent, table, states = written
    outproj_own = whole_columns(out_rows_own, out_rows_other)
    cot_all, dbranch, stat = run_statistics(order, gates, sent, cot_pieces, outproj_own, chan)
    stat = stat[:2]
    stat = stat + sum(along(stat, mask) for mask in range(1, places))
    grms = lax.rsqrt(stat[0] / inner_width + norm_eps)
    stats = jnp.pad(
        jnp.stack([grms, grms * grms * (stat[1] / inner_width)]), ((0, 6), (0, 0))
    )
    dsent, dgates, branch = run_gate(order, gates, sent, dbranch, stats, chan, places)
    token_block = 2 * local_len
    flat = places * token_block

    def columns(x, m):
        return x[:, m * token_block : (m + 1) * token_block]

    token_block = 2 * local_len
    flat = places * token_block

    def columns(x, m):
        return x[:, m * token_block : (m + 1) * token_block]

    def over_cores(x, axis):
        kept = lax.dynamic_index_in_dim(x, core, axis, keepdims=False)
        other = lax.dynamic_index_in_dim(x, 1 - core, axis, keepdims=False)
        return kept, other

    def added(kept, other):
        return (kept.astype(f32) + other.astype(f32)).astype(bf16)

    in_rows = inproj_mean.shape[0]
    out_rows = outproj_mean.shape[0]

    def inproj_local(grad_rows):
        normed_flat = normed_all.reshape(flat, model_width)
        shape = (shards, places, in_rows, grad_rows.shape[0])
        if in_rows % 16 == 0:
            steps = min(shards, model_width // Q)
            kept, given = run_weight_gradient(
                core.reshape(1).astype(jnp.int32), normed_flat, grad_rows, in_rows, steps
            )
            return kept.reshape(shape), given.reshape(shape)
        part = lax.dot_general(
            normed_flat, grad_rows, (((0,), (1,)), ((), ())), preferred_element_type=f32
        ).astype(bf16)
        return over_cores(part.reshape(shards, places, 2, in_rows, -1), 2)

    branch_found = [along(columns(branch, m), m) for m in range(1, places)]
    out_part = jnp.dot(branch, cot_all.reshape(flat, model_width), preferred_element_type=f32).astype(bf16)
    out_kept, out_part = over_cores(out_part.reshape(places, 2, out_rows, model_width), 1)
    out_part = swap(out_part)
    gate_kept, gate_part = inproj_local(dgates)
    gate_part = swap(gate_part)
    dsent, out_kept, gate_kept = lax.optimization_barrier((dsent, out_kept, gate_kept))
    backward = functools.partial(
        run_backward, order, dsent, conv, values, table, states, chan, head_table, heads, kernel_len, places
    )
    written, carry = backward(places, places - 1, [], [])
    carry, out_part, gate_part = lax.optimization_barrier((carry, out_part, gate_part))
    out_sum = added(out_kept, out_part)
    early = jnp.concatenate(
        [out_sum[:, :, i : i + own_width] for i in range(0, model_width, own_width)]
        + [added(gate_kept, gate_part).reshape(shards, -1, own_width)],
        axis=1,
    )
    carry, early = lax.optimization_barrier((carry, early))
    early = shard_exchange(early)
    written, carry = backward(1, 1, carry, written)
    drest = written[0]
    conv_acc, head_acc = carry[:2]

    dn_pieces = run_token_gradient(dgates, drest, weight, places)
    drest, conv_acc, head_acc, branch_found, *dn_pieces = lax.optimization_barrier(
        (drest, conv_acc, head_acc, branch_found, *dn_pieces)
    )
    out_other = swap(out_half)
    dn_first = scatter_first(dn_pieces)
    rest_kept, rest_part = inproj_local(drest)
    rest_kept, rest_part, out_other, early, *dn_first = lax.optimization_barrier(
        (rest_kept, rest_part, out_other, early, *dn_first)
    )
    dn_found = scatter_second(dn_pieces, dn_first)
    rest = shard_exchange(added(rest_kept, swap(rest_part)))

    branch_all = in_order([columns(branch, 0)] + branch_found).reshape(inner_width, token_block)
    out = whole_columns(dot_tn(branch_all, out_half), dot_tn(branch_all, out_other))
    block_output = tokens + to_tokens(out)

    early = jnp.sum(early.astype(f32), axis=0)
    out_size = out_rows * model_width // own_width
    outproj_grad = lax.ppermute(
        jnp.concatenate(
            [early[i : i + out_rows] for i in range(0, out_size, out_rows)], axis=1
        ).astype(bf16),
        ("wshard", "seq"),
        [
            (a * group + 2 * b + c, b * group + 2 * a + c)
            for a in range(shards)
            for b in range(places)
            for c in range(2)
        ],
    ).astype(f32)
    conv_sums = jnp.sum(conv_acc, axis=-1)
    head_sums = jnp.sum(head_acc, axis=-1)[:, :heads]
    head_sums = jnp.concatenate([head_sums[:1] * rates, head_sums[1:]])
    sums = jnp.concatenate([conv_sums.reshape(-1), head_sums.reshape(-1)])
    sums = sums + swap(sums)
    mask = 1
    while mask < shards:
        sums = sums + across(sums, mask)
        mask *= 2
    block_output, outproj_grad, rest, sums, *dn_found = lax.optimization_barrier(
        (block_output, outproj_grad, rest, sums, *dn_found)
    )
    rest = jnp.sum(rest.astype(f32), axis=0).astype(bf16)
    early = early[out_size:].reshape(places, in_rows, own_width).astype(bf16)
    rest_side = line_exchange(jnp.concatenate([early, rest], axis=2))

    lines = in_order([sums] + [along(sums, m) for m in range(1, places)])
    conv_lines = lines[:, : conv_sums.size].reshape(places, kernel_len + 1, channels)
    conv_total = jnp.concatenate(
        [
            conv_lines[:, :, :own_width].transpose(1, 0, 2).reshape(kernel_len + 1, -1),
            jnp.sum(conv_lines[:, :, own_width:], axis=0),
        ],
        axis=1,
    )
    head_total = lines[:, conv_sums.size :].reshape(places, 3, heads).transpose(1, 0, 2).reshape(3, -1)
    dnormed = sum(piece.astype(f32) for piece in dn_found)
    dn_scaled = to_tokens(dnormed) * gain_f
    input_grad = (
        cotangent.astype(f32)
        + scale * dn_scaled
        - tokens * scale * scale * scale * jnp.mean(dn_scaled * tokens, axis=-1, keepdims=True)
    )

    def side(x):
        return x.astype(f32).transpose(1, 0, 2).reshape(in_rows, -1)

    inproj_grad = jnp.concatenate(
        [
            side(rest_side[:, :, :own_width]),
            side(rest_side[:, :, own_width : 2 * own_width]),
            jnp.sum(rest_side[:, :, 2 * own_width : own_width + channels].astype(f32), axis=0),
            side(rest_side[:, :, own_width + channels : own_width + channels + heads]),
        ],
        axis=1,
    )
    conv_width = conv_mean.shape[1]
    conv_grad = lax.dynamic_slice_in_dim(
        conv_total, (shard * group + seq_index) * conv_width, conv_width, 1
    )
    head_width = head_params.shape[1]
    head_grad = lax.dynamic_slice_in_dim(head_total, shard * head_width, head_width, 1)

    inproj_own = inproj_own.astype(f32)
    outproj_piece = own_piece(outproj_weight, out_rows, 0).astype(f32)
    norm_own = own_piece(norm_gain, in_rows, 0).astype(f32)
    gate_piece = own_piece(gate_gain, out_rows, 0).astype(f32)
    norm_grad = jnp.sum(inproj_own * inproj_grad, axis=1) / norm_own
    gate_grad = jnp.sum(outproj_piece * outproj_grad, axis=1) / gate_piece
    norm_res = adamw(norm_grad, norm_own, norm_mean, norm_square, 0.0)
    inproj_res = adamw(inproj_grad, inproj_own, inproj_mean, inproj_square, 0.1)
    conv_res = adamw(conv_grad, own_piece(conv_params, conv_width, 1).astype(f32), conv_mean, conv_square, 0.0)
    head_res = adamw(head_grad, head_params.astype(f32), head_mean, head_square, 0.0)
    gate_res = adamw(gate_grad, gate_piece, gate_mean, gate_square, 0.0)
    outproj_res = adamw(outproj_grad, outproj_piece, outproj_mean, outproj_square, 0.1)
    return (
        block_output,
        input_grad,
        norm_res[0],
        norm_res[1],
        norm_res[2],
        norm_res[3],
        inproj_res[0],
        inproj_res[1],
        inproj_res[2],
        inproj_res[3],
        conv_res[0],
        conv_res[1],
        conv_res[2],
        conv_res[3],
        head_res[0],
        head_res[1],
        head_res[2],
        head_res[3],
        gate_res[0],
        gate_res[1],
        gate_res[2],
        gate_res[3],
        outproj_res[0],
        outproj_res[1],
        outproj_res[2],
        outproj_res[3],
    )


def solution(mesh):
    placed = (
        P("wshard", "seq", None),
        P("wshard", "seq", None),
        P("wshard"),
        P(("wshard", "seq")),
        P(("wshard", "seq")),
        P("wshard", None),
        P(("wshard", "seq"), None),
        P(("wshard", "seq"), None),
        P(None, "wshard"),
        P(None, ("wshard", "seq")),
        P(None, ("wshard", "seq")),
        P(None, "wshard"),
        P(None, "wshard"),
        P(None, "wshard"),
        P("wshard"),
        P(("wshard", "seq")),
        P(("wshard", "seq")),
        P("wshard", None),
        P(("wshard", "seq"), None),
        P(("wshard", "seq"), None),
    )
    return jax.shard_map(
        local,
        mesh=mesh,
        in_specs=placed,
        out_specs=(
            P("wshard", "seq", None),
            P("wshard", "seq", None),
            P(("wshard", "seq")),
            P(("wshard", "seq")),
            P(("wshard", "seq")),
            P(("wshard", "seq")),
            P(("wshard", "seq"), None),
            P(("wshard", "seq"), None),
            P(("wshard", "seq"), None),
            P(("wshard", "seq"), None),
            P(None, ("wshard", "seq")),
            P(None, ("wshard", "seq")),
            P(None, ("wshard", "seq")),
            P(None, ("wshard", "seq")),
            P(None, "wshard"),
            P(None, "wshard"),
            P(None, "wshard"),
            P(None, "wshard"),
            P(("wshard", "seq")),
            P(("wshard", "seq")),
            P(("wshard", "seq")),
            P(("wshard", "seq")),
            P(("wshard", "seq"), None),
            P(("wshard", "seq"), None),
            P(("wshard", "seq"), None),
            P(("wshard", "seq"), None),
        ),
        check_vma=False,
    )
```

```python
import functools

import jax
import jax.numpy as jnp
from jax import lax
from jax.experimental import pallas as pl
from jax.experimental.pallas import tpu as pltpu
from jax.sharding import PartitionSpec as P

norm_eps = 1e-05
adam_eps = 1e-08
learn_rate = 0.02
beta_one = 0.9
beta_two = 0.999
first_fix = 1.0 - 0.9**10
second_fix = 1.0 - 0.999**10

f32 = jnp.float32
bf16 = jnp.bfloat16
Q = 128
HP = 16
FLOOR = -1e30
MIB = 1024 * 1024


def dot_nn(a, b):
    return lax.dot_general(a, b, (((1,), (0,)), ((), ())), preferred_element_type=f32)


def dot_nt(a, b):
    return lax.dot_general(a, b, (((1,), (1,)), ((), ())), preferred_element_type=f32)


def dot_tn(a, b):
    return lax.dot_general(a, b, (((0,), (0,)), ((), ())), preferred_element_type=f32)


def sigmoid(a):
    return 1.0 / (1.0 + jnp.exp(-a))


def lanes(shape):
    return lax.broadcasted_iota(jnp.int32, shape, 1)


def earlier_by(current, previous, lane, shift):
    return pltpu.roll(jnp.where(lane >= Q - shift, previous, current), shift, 1)


def later_by(current, following, lane, shift):
    return pltpu.roll(jnp.where(lane < shift, following, current), Q - shift, 1)


def running_sum(a, lane):
    shift = 1
    while shift < Q:
        a = a + jnp.where(lane >= shift, pltpu.roll(a, shift, 1), 0.0)
        shift *= 2
    return a


def running_sum_back(a, lane):
    shift = 1
    while shift < Q:
        a = a + jnp.where(lane < Q - shift, pltpu.roll(a, Q - shift, 1), 0.0)
        shift *= 2
    return a


def join_weight(own_width, channels, core, own_ref, other_ref, weight_ref):
    shards, _, depth = own_ref.shape
    for even in range(2):

        @pl.when(core == even)
        def _(first=(own_ref, other_ref)[even], second=(other_ref, own_ref)[even]):
            for at in range(shards):
                here = slice(at * depth, (at + 1) * depth)
                low = 2 * own_width
                weight_ref[:own_width, here] = first[at, :own_width, :]
                weight_ref[own_width:low, here] = second[at, :own_width, :]
                weight_ref[low : low + Q, here] = first[at, own_width : own_width + Q, :]
                weight_ref[low + Q : low + 2 * Q, here] = second[at, own_width : own_width + Q, :]
                weight_ref[low + 2 * Q :, here] = own_ref[at, own_width + Q : own_width + Q + HP, :]


def mixer_forward(own_width, heads, kernel_len, places, start, assemble, order_ref, *refs):
    token_refs = refs[:places]
    gain_ref, chan_ref, head_ref = refs[places : places + 3]
    given = refs[places + 3 : -14]
    (
        weight_out,
        normed_ref,
        gates_ref,
        values_ref,
        conv_ref,
        sent_ref,
        table_ref,
        state_ref,
        before,
        state,
        active,
        steps,
        inter,
        scaled,
    ) = refs[-14:]
    channels = chan_ref.shape[0]
    width = own_width // heads
    token_block = normed_ref.shape[0]

    @pl.when(pl.program_id(0) == 0)
    def _():
        before[...] = given[1][...] if start else jnp.zeros_like(before)
        state[...] = given[2][...] if start else jnp.zeros_like(state)
        if not assemble:
            weight_out[...] = jnp.zeros_like(weight_out)
        else:
            join_weight(own_width, channels, order_ref[places], *given[:2], weight_out)

    for piece in range(places):

        @pl.when(order_ref[start + pl.program_id(0)] == piece)
        def _(token_ref=token_refs[piece]):
            tokens = token_ref[...].astype(f32)
            scale = lax.rsqrt(jnp.mean(tokens * tokens, axis=1, keepdims=True) + norm_eps)
            normed_ref[...] = (tokens * scale * gain_ref[...]).astype(bf16)

    weight_ref = weight_out if assemble else given[0]
    normed = normed_ref[...]
    gates_ref[...] = dot_nt(weight_ref[0:own_width, :], normed)
    values_ref[...] = dot_nt(weight_ref[own_width : own_width + channels, :], normed).astype(bf16)
    steps[...] = dot_nt(weight_ref[own_width + channels :, :], normed).astype(bf16).astype(f32)
    lane = lanes((Q, Q))
    lane_head = lanes((HP, Q))
    causal = lax.broadcasted_iota(jnp.int32, (Q, Q), 0) <= lane

    def block(at, carry):
        here = pl.ds(pl.multiple_of(at * Q, Q), Q)

        def convolve(tile, inner):
            rows = pl.ds(pl.multiple_of(tile * Q, Q), Q)
            raw = values_ref[rows, here]
            current = raw.astype(f32)
            previous = before[rows, :].astype(f32)
            taps = chan_ref[rows, :]
            out = taps[:, kernel_len : kernel_len + 1] + taps[:, kernel_len - 1 : kernel_len] * current
            for shift in range(1, kernel_len):
                tap = kernel_len - 1 - shift
                out = out + taps[:, tap : tap + 1] * earlier_by(current, previous, lane, shift)
            before[rows, :] = raw
            conv_ref[rows, here] = out
            active[rows, :] = out * sigmoid(out)
            return inner

        lax.fori_loop(0, channels // Q, convolve, 0, unroll=True)
        drive = steps[:, here] + head_ref[:, 1:2]
        step = jnp.maximum(drive, 0.0) + jnp.log1p(jnp.exp(-jnp.abs(drive)))
        within = running_sum(step * head_ref[:, 0:1], lane_head)
        table_ref[0, :, here] = step
        table_ref[1, :, here] = within
        table_ref[2, :, here] = sigmoid(drive)
        within_col = jnp.transpose(within)
        total = within[:, Q - 1 : Q]
        grow = jnp.exp(within)
        tail = jnp.exp(total - within) * step
        total_decay = jnp.exp(total)
        b_rows = jnp.transpose(active[own_width : own_width + Q, :]).astype(bf16)
        c_cols = active[own_width + Q : own_width + 2 * Q, :].astype(bf16)
        scores = dot_nn(b_rows, c_cols)
        held = state[...].astype(bf16)
        state_ref[at] = held
        inter[...] = dot_nn(held, c_cols)
        for head in range(heads):
            rows = slice(head * width, (head + 1) * width)
            x = active[rows, :]
            decay = jnp.exp(
                jnp.where(causal, within[head : head + 1, :] - within_col[:, head : head + 1], FLOOR)
            )
            weights = (decay * scores).astype(bf16)
            driven = (x * step[head : head + 1, :]).astype(bf16)
            mixed = dot_nn(driven, weights)
            mixed = mixed + inter[rows, :] * grow[head : head + 1, :]
            mixed = mixed + chan_ref[rows, 6:7] * x
            sent_ref[rows, here] = mixed.astype(bf16)
            scaled[rows, :] = (x * tail[head : head + 1, :]).astype(bf16)
            state[rows, :] = state[rows, :] * total_decay[head : head + 1, :]
        state[...] += dot_nn(scaled[...], b_rows)
        return carry

    lax.fori_loop(0, token_block // Q, block, 0, unroll=True)


def gate_statistics(places, order_ref, gates_ref, sent_ref, *refs):
    cot_refs = refs[:places]
    weight_ref, chan_ref, cot_all, dbranch_ref, stat_ref = refs[places:]
    for piece in range(places):

        @pl.when(order_ref[pl.program_id(0)] == piece)
        def _(cot_ref=cot_refs[piece]):
            cot_all[...] = cot_ref[...]

    dbranch = dot_nt(weight_ref[...], cot_all[...])
    dbranch_ref[...] = dbranch
    gates = gates_ref[...]
    gated = sent_ref[...].astype(f32) * (gates * sigmoid(gates))
    square = jnp.sum(gated * gated, axis=0, keepdims=True)
    cross = jnp.sum(gated * (dbranch * chan_ref[0 : gates.shape[0], 7:8]), axis=0, keepdims=True)
    stat_ref[...] = jnp.concatenate([square, cross, jnp.zeros((6, square.shape[1]), f32)], axis=0)


def gate_backward(
    order_ref, gates_ref, sent_ref, dbranch_ref, stat_ref, chan_ref, dsent_ref, dgates_ref, branch_ref
):
    grms = stat_ref[0:1, :]
    pull = stat_ref[1:2, :]

    def gate(tile, carry):
        rows = pl.ds(pl.multiple_of(tile * Q, Q), Q)
        gates = gates_ref[rows, :]
        sent = sent_ref[rows, :].astype(f32)
        gain = chan_ref[rows, 7:8]
        sig = sigmoid(gates)
        swish = gates * sig
        gated = sent * swish
        dgated = grms * (dbranch_ref[rows, :] * gain - gated * pull)
        dsent_ref[rows, :] = (dgated * swish).astype(bf16)
        dgates_ref[rows, :] = (dgated * sent * sig * (1.0 + gates * (1.0 - sig))).astype(bf16)
        branch_ref[rows, :] = (gated * grms * gain).astype(bf16)
        return carry

    lax.fori_loop(0, gates_ref.shape[0] // Q, gate, 0, unroll=True)


def mixer_backward(
    own_width,
    heads,
    kernel_len,
    order_ref,
    dsent_ref,
    conv_ref,
    values_ref,
    table_ref,
    state_ref,
    chan_ref,
    head_ref,
    *refs,
):
    (
        dproj_ref,
        conv_sum,
        head_acc,
        conv_acc,
        adjoint,
        following,
        active,
        dactive,
        inter,
        reach,
        driven,
        tailed,
        rows_scr,
    ) = refs
    channels = chan_ref.shape[0]
    width = own_width // heads
    token_block = dsent_ref.shape[1]

    @pl.when(pl.program_id(0) == 0)
    def _():
        for held in (conv_acc, head_acc, adjoint, following):
            held[...] = jnp.zeros_like(held)
        rows_scr[...] = jnp.zeros_like(rows_scr)

    lane = lanes((Q, Q))
    sub = lax.broadcasted_iota(jnp.int32, (Q, Q), 0)
    lane_head = lanes((HP, Q))
    causal = sub >= lane
    strict = (sub < lane).astype(bf16)

    def block(index, carry):
        at = token_block // Q - 1 - index
        here = pl.ds(pl.multiple_of(at * Q, Q), Q)

        def activate(tile, inner):
            rows = pl.ds(pl.multiple_of(tile * Q, Q), Q)
            conv = conv_ref[rows, here]
            active[rows, :] = conv * sigmoid(conv)
            return inner

        lax.fori_loop(0, channels // Q, activate, 0, unroll=True)
        step = table_ref[0, :, here]
        within = table_ref[1, :, here]
        within_col = jnp.transpose(within)
        total = within[:, Q - 1 : Q]
        grow = jnp.exp(within)
        fade = jnp.exp(total - within)
        tail = fade * step
        total_decay = jnp.exp(total)
        b_cols_f = active[own_width : own_width + Q, :]
        c_cols_f = active[own_width + Q : own_width + 2 * Q, :]
        b_cols = b_cols_f.astype(bf16)
        c_cols = c_cols_f.astype(bf16)
        c_rows = jnp.transpose(c_cols_f).astype(bf16)
        scores = dot_nn(c_rows, b_cols)
        held = state_ref[at]
        after = adjoint[...].astype(bf16)
        inter[...] = dot_nn(held, c_cols)
        reach[...] = dot_nn(after, b_cols)
        dscores = jnp.zeros((Q, Q), f32)
        blank = jnp.zeros((width, Q), bf16)
        for pair in range(heads // 2):
            turned = jnp.transpose(dsent_ref[pair * 2 * width : (pair + 1) * 2 * width, here].astype(f32)).astype(bf16)
            for half in range(2):
                head = 2 * pair + half
                rows = slice(head * width, (head + 1) * width)
                one = slice(head, head + 1)
                x = active[rows, :]
                x_low = x.astype(bf16)
                grad_low = dsent_ref[rows, here]
                grad = grad_low.astype(f32)
                decay = jnp.exp(
                    jnp.where(causal, within_col[:, head : head + 1] - within[one, :], FLOOR)
                )
                lone = jnp.concatenate([x_low, blank] if half == 0 else [blank, x_low], axis=0)
                dweights = dot_nn(turned, lone)
                spread = decay * dweights * step[one, :]
                dscores = dscores + spread
                crossing = dot_nn((spread * scores).astype(bf16), strict)
                rows_scr[0, one, :] = jnp.sum(jnp.where(causal, crossing, 0.0), axis=0, keepdims=True)
                far = reach[rows, :]
                back = dot_nn(grad_low, (decay * scores).astype(bf16)) + far * fade[one, :]
                rows_scr[1, one, :] = jnp.sum(x * back, axis=0, keepdims=True)
                rows_scr[2, one, :] = jnp.sum(x * far, axis=0, keepdims=True) * tail[one, :]
                rows_scr[3, one, :] = jnp.sum(grad * inter[rows, :], axis=0, keepdims=True) * grow[one, :]
                rows_scr[4, one, :] = jnp.sum(grad * x, axis=0, keepdims=True)
                old = adjoint[rows, :]
                rows_scr[5, one, :] = jnp.sum(old * held[rows, :].astype(f32), axis=0, keepdims=True)
                dactive[rows, :] = back * step[one, :] + chan_ref[rows, 6:7] * grad
                driven[rows, :] = (grad * grow[one, :]).astype(bf16)
                tailed[rows, :] = (x * tail[one, :]).astype(bf16)
                adjoint[rows, :] = old * total_decay[one, :]
        dlow = dscores.astype(bf16)
        dactive[own_width : own_width + Q, :] = dot_nn(c_cols, dlow) + dot_tn(after, tailed[...])
        dactive[own_width + Q : own_width + 2 * Q, :] = dot_nt(b_cols, dlow) + dot_tn(held, driven[...])
        adjoint[...] += dot_nn(driven[...], c_rows)
        ahead = rows_scr[2]
        dlog = (
            rows_scr[0]
            + running_sum_back(rows_scr[3], lane_head)
            + (running_sum(ahead, lane_head) - ahead)
            + total_decay * jnp.sum(rows_scr[5], axis=1, keepdims=True)
        )
        dstep = (rows_scr[1] + head_ref[:, 0:1] * dlog) * table_ref[2, :, here]
        dproj_ref[channels:, here] = dstep.astype(bf16)
        head_acc[0] += step * dlog
        head_acc[1] += dstep
        head_acc[2] += rows_scr[4]

        def convolve(tile, inner):
            rows = pl.ds(pl.multiple_of(tile * Q, Q), Q)
            conv = conv_ref[rows, here]
            sig = sigmoid(conv)
            dconv = dactive[rows, :] * sig * (1.0 + conv * (1.0 - sig))
            taps = chan_ref[rows, :]
            raw = values_ref[rows, here].astype(f32)
            nxt = following[rows, :]
            dvalue = taps[:, kernel_len - 1 : kernel_len] * dconv
            conv_acc[kernel_len - 1, rows, :] += raw * dconv
            for shift in range(1, kernel_len):
                tap = kernel_len - 1 - shift
                moved = later_by(dconv, nxt, lane, shift)
                dvalue = dvalue + taps[:, tap : tap + 1] * moved
                conv_acc[tap, rows, :] += raw * moved
            conv_acc[kernel_len, rows, :] += dconv
            following[rows, :] = dconv
            dproj_ref[rows, here] = dvalue.astype(bf16)
            return inner

        lax.fori_loop(0, channels // Q, convolve, 0, unroll=True)
        return carry

    lax.fori_loop(0, token_block // Q, block, 0, unroll=True)

    @pl.when(pl.program_id(0) == pl.num_programs(0) - 1)
    def _():
        ones = jnp.ones((8, Q), f32)
        for tap in range(kernel_len + 1):
            total = lax.dot_general(
                ones,
                conv_acc[tap],
                (((1,), (1,)), ((), ())),
                precision=lax.Precision.HIGHEST,
                preferred_element_type=f32,
            )
            conv_sum[tap : tap + 1, :] = total[0:1, :]


def run_forward(
    order, tokens, gain, chan, head_table, own_width, heads, kernel_len, start, count, weight, carry, written
):
    places = len(tokens)
    token_block, model_width = tokens[0].shape
    channels = chan.shape[0]
    full = places * token_block
    weight_shape = (own_width + channels + HP, model_width)
    assemble = len(weight) == 2
    solid = lambda x: pl.BlockSpec(x.shape, lambda k, order: (0,) * x.ndim)
    fixed = lambda k, order: (0, 0)
    cols = lambda k, order: (0, start + k)
    stored = lambda k, order: (order[start + k], 0, 0)
    spec = pltpu.PrefetchScalarGridSpec(
        num_scalar_prefetch=1,
        grid=(count,),
        in_specs=[solid(x) for x in (*tokens, gain, chan, head_table, *weight, *carry)]
        + [pl.BlockSpec(memory_space=pl.ANY)] * len(written),
        out_specs=[
            pl.BlockSpec(weight_shape if assemble else (8, Q), fixed),
            pl.BlockSpec((None, token_block, model_width), stored),
            pl.BlockSpec((own_width, token_block), cols),
            pl.BlockSpec((channels, token_block), cols),
            pl.BlockSpec((channels, token_block), cols),
            pl.BlockSpec((own_width, token_block), cols),
            pl.BlockSpec((3, HP, token_block), lambda k, order: (0, 0, start + k)),
            pl.BlockSpec((token_block // Q, own_width, Q), lambda k, order: (start + k, 0, 0)),
            pl.BlockSpec((channels, Q), fixed),
            pl.BlockSpec((own_width, Q), fixed),
        ],
        scratch_shapes=[
            pltpu.VMEM((channels, Q), f32),
            pltpu.VMEM((HP, token_block), f32),
            pltpu.VMEM((own_width, Q), f32),
            pltpu.VMEM((own_width, Q), bf16),
        ],
    )
    found = pl.pallas_call(
        functools.partial(mixer_forward, own_width, heads, kernel_len, places, start, assemble),
        grid_spec=spec,
        out_shape=[
            jax.ShapeDtypeStruct(weight_shape if assemble else (8, Q), bf16),
            jax.ShapeDtypeStruct((places, token_block, model_width), bf16),
            jax.ShapeDtypeStruct((own_width, full), f32),
            jax.ShapeDtypeStruct((channels, full), bf16),
            jax.ShapeDtypeStruct((channels, full), f32),
            jax.ShapeDtypeStruct((own_width, full), bf16),
            jax.ShapeDtypeStruct((3, HP, full), f32),
            jax.ShapeDtypeStruct((full // Q, own_width, Q), bf16),
            jax.ShapeDtypeStruct((channels, Q), bf16),
            jax.ShapeDtypeStruct((own_width, Q), f32),
        ],
        input_output_aliases={
            4 + places + len(weight) + len(carry) + i: 1 + i for i in range(len(written))
        },
        compiler_params=pltpu.CompilerParams(
            dimension_semantics=("arbitrary",), vmem_limit_bytes=48 * MIB
        ),
        cost_estimate=pl.CostEstimate(
            flops=8 * count * token_block * model_width * weight_shape[0],
            bytes_accessed=8 * MIB * count,
            transcendentals=MIB * count,
        ),
        name="mixer_forward",
    )(order, *tokens, gain, chan, head_table, *weight, *carry, *written)
    return found[0] if assemble else weight[0], found[1:8], found[8:]


def run_statistics(order, gates, sent, cotangents, weight, chan):
    places = len(cotangents)
    token_block, model_width = cotangents[0].shape
    own_width, full = gates.shape
    fixed = lambda k, order: (0, 0)
    cols = lambda k, order: (0, k)
    spec = pltpu.PrefetchScalarGridSpec(
        num_scalar_prefetch=1,
        grid=(places,),
        in_specs=[
            pl.BlockSpec((own_width, token_block), cols),
            pl.BlockSpec((own_width, token_block), cols),
            *[pl.BlockSpec((token_block, model_width), fixed)] * places,
            pl.BlockSpec(weight.shape, fixed),
            pl.BlockSpec(chan.shape, fixed),
        ],
        out_specs=[
            pl.BlockSpec((None, token_block, model_width), lambda k, order: (order[k], 0, 0)),
            pl.BlockSpec((own_width, token_block), cols),
            pl.BlockSpec((8, token_block), cols),
        ],
    )
    return pl.pallas_call(
        functools.partial(gate_statistics, places),
        grid_spec=spec,
        out_shape=[
            jax.ShapeDtypeStruct((places, token_block, model_width), bf16),
            jax.ShapeDtypeStruct((own_width, full), f32),
            jax.ShapeDtypeStruct((8, full), f32),
        ],
        compiler_params=pltpu.CompilerParams(
            dimension_semantics=("arbitrary",), vmem_limit_bytes=24 * MIB
        ),
        cost_estimate=pl.CostEstimate(
            flops=2 * full * model_width * own_width,
            bytes_accessed=16 * MIB,
            transcendentals=own_width * full,
        ),
        name="gate_statistics",
    )(order, gates, sent, *cotangents, weight, chan)


def run_gate(order, gates, sent, dbranch, stats, chan, places):
    own_width, full = gates.shape
    token_block = full // places
    cols = lambda k, order: (0, k)
    turned = lambda k, order: (0, order[k])
    spec = pltpu.PrefetchScalarGridSpec(
        num_scalar_prefetch=1,
        grid=(places,),
        in_specs=[
            pl.BlockSpec((own_width, token_block), cols),
            pl.BlockSpec((own_width, token_block), cols),
            pl.BlockSpec((own_width, token_block), cols),
            pl.BlockSpec((8, token_block), cols),
            pl.BlockSpec(chan.shape, lambda k, order: (0, 0)),
        ],
        out_specs=[
            pl.BlockSpec((own_width, token_block), cols),
            pl.BlockSpec((own_width, token_block), turned),
            pl.BlockSpec((own_width, token_block), turned),
        ],
    )
    return pl.pallas_call(
        gate_backward,
        grid_spec=spec,
        out_shape=[jax.ShapeDtypeStruct((own_width, full), bf16)] * 3,
        compiler_params=pltpu.CompilerParams(
            dimension_semantics=("arbitrary",), vmem_limit_bytes=20 * MIB
        ),
        cost_estimate=pl.CostEstimate(
            flops=20 * own_width * full, bytes_accessed=14 * own_width * full, transcendentals=own_width * full
        ),
        name="gate_backward",
    )(order, gates, sent, dbranch, stats, chan)


def run_backward(order, dsent, conv, values, table, states, chan, head_table, heads, kernel_len, places):
    own_width, full = dsent.shape
    channels = chan.shape[0]
    token_block = full // places
    out_rows = channels + HP
    last = places - 1
    fixed = lambda k, order: (0, 0)
    cols = lambda k, order: (0, last - k)
    spec = pltpu.PrefetchScalarGridSpec(
        num_scalar_prefetch=1,
        grid=(places,),
        in_specs=[
            pl.BlockSpec((own_width, token_block), cols),
            pl.BlockSpec((channels, token_block), cols),
            pl.BlockSpec((channels, token_block), cols),
            pl.BlockSpec((3, HP, token_block), lambda k, order: (0, 0, last - k)),
            pl.BlockSpec((token_block // Q, own_width, Q), lambda k, order: (last - k, 0, 0)),
            pl.BlockSpec(chan.shape, fixed),
            pl.BlockSpec(head_table.shape, fixed),
        ],
        out_specs=[
            pl.BlockSpec((out_rows, token_block), lambda k, order: (0, order[last - k])),
            pl.BlockSpec((8, channels), fixed),
            pl.BlockSpec((3, HP, Q), lambda k, order: (0, 0, 0)),
        ],
        scratch_shapes=[
            pltpu.VMEM((kernel_len + 1, channels, Q), f32),
            pltpu.VMEM((own_width, Q), f32),
            pltpu.VMEM((channels, Q), f32),
            pltpu.VMEM((channels, Q), f32),
            pltpu.VMEM((channels, Q), f32),
            pltpu.VMEM((own_width, Q), f32),
            pltpu.VMEM((own_width, Q), f32),
            pltpu.VMEM((own_width, Q), bf16),
            pltpu.VMEM((own_width, Q), bf16),
            pltpu.VMEM((6, HP, Q), f32),
        ],
    )
    return pl.pallas_call(
        functools.partial(mixer_backward, own_width, heads, kernel_len),
        grid_spec=spec,
        out_shape=[
            jax.ShapeDtypeStruct((out_rows, full), bf16),
            jax.ShapeDtypeStruct((8, channels), f32),
            jax.ShapeDtypeStruct((3, HP, Q), f32),
        ],
        compiler_params=pltpu.CompilerParams(
            dimension_semantics=("arbitrary",), vmem_limit_bytes=56 * MIB
        ),
        cost_estimate=pl.CostEstimate(
            flops=32 * MIB * 1024, bytes_accessed=24 * MIB, transcendentals=4 * MIB
        ),
        name="mixer_backward",
    )(order, dsent, conv, values, table, states, chan, head_table)


def token_gradient(dgates_ref, drest_ref, weight_ref, *out_refs):
    own_width = dgates_ref.shape[0]
    total = dot_tn(dgates_ref[...], weight_ref[:own_width, :]) + dot_tn(
        drest_ref[...], weight_ref[own_width:, :]
    )
    for piece, out_ref in enumerate(out_refs):

        @pl.when(pl.program_id(0) == piece)
        def _(out_ref=out_ref):
            out_ref[...] = total.astype(bf16)


def run_token_gradient(dgates, drest, weight, places):
    model_width = weight.shape[1]
    token_block = dgates.shape[1] // places
    fixed = lambda k: (0, 0)
    return pl.pallas_call(
        token_gradient,
        grid=(places,),
        in_specs=[
            pl.BlockSpec((dgates.shape[0], token_block), lambda k: (0, k)),
            pl.BlockSpec((drest.shape[0], token_block), lambda k: (0, k)),
            pl.BlockSpec(weight.shape, fixed),
        ],
        out_specs=[pl.BlockSpec((token_block, model_width), fixed)] * places,
        out_shape=[jax.ShapeDtypeStruct((token_block, model_width), bf16)] * places,
        compiler_params=pltpu.CompilerParams(
            dimension_semantics=("arbitrary",), vmem_limit_bytes=56 * MIB
        ),
        cost_estimate=pl.CostEstimate(
            flops=2 * dgates.shape[1] * weight.size, bytes_accessed=12 * MIB, transcendentals=0
        ),
        name="token_gradient",
    )(dgates, drest, weight)


def weight_gradient(in_rows, core_ref, normed_ref, grad_ref, kept_ref, given_ref):
    total = lax.dot_general(
        normed_ref[...], grad_ref[...], (((0,), (1,)), ((), ())), preferred_element_type=f32
    ).astype(bf16)
    for core in range(2):

        @pl.when(core_ref[0] == core)
        def _(core=core):
            for at in range(kept_ref.shape[0]):
                low = (2 * at + core) * in_rows
                kept_ref[at] = total[low : low + in_rows, :]
                low = (2 * at + 1 - core) * in_rows
                given_ref[at] = total[low : low + in_rows, :]


def run_weight_gradient(core, normed, grad, in_rows, steps):
    full, model_width = normed.shape
    columns = grad.shape[0]
    tile = model_width // steps
    groups = tile // (2 * in_rows)
    spec = pltpu.PrefetchScalarGridSpec(
        num_scalar_prefetch=1,
        grid=(steps,),
        in_specs=[
            pl.BlockSpec((full, tile), lambda k, core: (0, k)),
            pl.BlockSpec(grad.shape, lambda k, core: (0, 0)),
        ],
        out_specs=[pl.BlockSpec((groups, in_rows, columns), lambda k, core: (k, 0, 0))] * 2,
    )
    return pl.pallas_call(
        functools.partial(weight_gradient, in_rows),
        grid_spec=spec,
        out_shape=[jax.ShapeDtypeStruct((groups * steps, in_rows, columns), bf16)] * 2,
        compiler_params=pltpu.CompilerParams(
            dimension_semantics=("arbitrary",), vmem_limit_bytes=56 * MIB
        ),
        cost_estimate=pl.CostEstimate(
            flops=MIB, bytes_accessed=MIB // 8, transcendentals=0
        ),
        name="weight_gradient",
    )(core, normed, grad)


def finish_weight(parts, own_width, state_two, heads, at_in, found_ref, weight_ref, first_ref, second_ref, *outs):
    grad_ref, first_out, second_out, update_out, dot_out = outs
    places = found_ref.shape[0]
    inner = own_width * places
    low = at_in
    for base, total in ((0, inner), (inner, inner), (2 * inner + state_two, heads * places)):
        share = total // (parts * places)
        for part in range(parts):
            for place in range(places):
                to = base + part * (total // parts) + place * share
                grad_ref[:, to : to + share] = found_ref[
                    place, :, low + part * share : low + (part + 1) * share
                ].astype(f32)
        low += total // places
        if base == inner:
            shared = found_ref[0, :, low : low + state_two].astype(f32)
            for place in range(1, places):
                shared = shared + found_ref[place, :, low : low + state_two].astype(f32)
            grad_ref[:, 2 * inner : 2 * inner + state_two] = shared
            low += state_two
    grad = grad_ref[...]
    weight = weight_ref[...].astype(f32)
    _, first_new, second_new, update = adamw(grad, weight, first_ref[...], second_ref[...], 0.1)
    first_out[...] = first_new
    second_out[...] = second_new
    update_out[...] = update
    dot_out[...] = jnp.broadcast_to(jnp.sum(grad * weight, axis=1, keepdims=True), dot_out.shape)


def run_finish(found, weight, first, second, parts, own_width, state_two, heads, at_in):
    rows, columns = weight.shape
    step = 16 if rows % 16 == 0 else rows
    whole = pl.BlockSpec((step, columns), lambda k: (k, 0))
    return pl.pallas_call(
        functools.partial(finish_weight, parts, own_width, state_two, heads, at_in),
        grid=(rows // step,),
        in_specs=[
            pl.BlockSpec((found.shape[0], step, found.shape[2]), lambda k: (0, k, 0)),
            whole,
            whole,
            whole,
        ],
        out_specs=[whole] * 4 + [pl.BlockSpec((step, Q), lambda k: (k, 0))],
        out_shape=[jax.ShapeDtypeStruct((rows, columns), f32)] * 4
        + [jax.ShapeDtypeStruct((rows, Q), f32)],
        compiler_params=pltpu.CompilerParams(
            dimension_semantics=("arbitrary",), vmem_limit_bytes=32 * MIB
        ),
        cost_estimate=pl.CostEstimate(
            flops=20 * rows * columns, bytes_accessed=28 * rows * columns, transcendentals=rows * columns
        ),
        name="finish_weight",
    )(found, weight, first, second)


def adamw(grad, weight, first, second, decay):
    first_new = beta_one * first + (1.0 - beta_one) * grad
    second_new = beta_two * second + (1.0 - beta_two) * grad * grad
    update = -learn_rate * (
        first_new / first_fix / (jnp.sqrt(second_new / second_fix) + adam_eps) + decay * weight
    )
    return (grad, first_new, second_new, update)


def pieces_for(stacked, index):
    return lax.dynamic_index_in_dim(stacked, index, 0, keepdims=False)


def local(
    block_input,
    cotangent,
    norm_gain,
    norm_mean,
    norm_square,
    inproj_weight,
    inproj_mean,
    inproj_square,
    conv_params,
    conv_mean,
    conv_square,
    head_params,
    head_mean,
    head_square,
    gate_gain,
    gate_mean,
    gate_square,
    outproj_weight,
    outproj_mean,
    outproj_square,
):
    group = lax.axis_size("seq")
    shards = lax.axis_size("wshard")
    seq_index = lax.axis_index("seq")
    shard = lax.axis_index("wshard")
    places = group // 2
    place = seq_index // 2
    core = seq_index % 2
    sequences, local_len, model_width = block_input.shape
    inner_width = gate_gain.shape[0] * shards
    head_count = head_params.shape[1] * shards
    kernel_len = conv_params.shape[0] - 1
    state_two = conv_params.shape[1] * shards - inner_width
    if sequences != 2 or places != shards or state_two != 2 * Q:
        raise ValueError("unexpected sizes")
    own_width = inner_width // places
    heads = head_count // places
    width = inner_width // head_count

    parts = shards if head_count % (shards * places) == 0 else 1

    def own_part(x, axis):
        size = x.shape[axis]
        share = size // (parts * places)
        return jnp.concatenate(
            [
                lax.dynamic_slice_in_dim(x, i * (size // parts) + place * share, share, axis)
                for i in range(parts)
            ],
            axis=axis,
        )

    def whole(x):
        x = x.reshape(x.shape[:-1] + (parts, -1))
        x = jnp.moveaxis(x, 0, -2)
        return x.reshape(x.shape[:-3] + (-1,))

    def swap(x):
        return lax.ppermute(x, "seq", [(i, i ^ 1) for i in range(group)])

    def along(x, mask, among=None):
        pairs = [(i, i ^ (2 * mask)) for i in range(group)]
        if among is not None:
            pairs = [(a, b) for a, b in pairs if b // 2 in among]
        return lax.ppermute(x, "seq", pairs)

    def across(x, mask):
        return lax.ppermute(x, "wshard", [(i, i ^ mask) for i in range(shards)])

    def shard_exchange(x):
        return lax.all_to_all(x, "wshard", split_axis=0, concat_axis=0, tiled=True)

    def shard_gather(x):
        return shard_exchange(jnp.broadcast_to(x[None], (shards,) + x.shape))

    def line_exchange(x):
        groups = [[2 * i + c for i in range(places)] for c in range(2)]
        return lax.all_to_all(
            x, "seq", split_axis=0, concat_axis=0, tiled=True, axis_index_groups=groups
        )

    small = jnp.concatenate(
        [norm_gain, gate_gain, conv_params.reshape(-1), head_params.reshape(-1)]
    )
    tokens = block_input.astype(f32)
    scale = lax.rsqrt(jnp.mean(tokens * tokens, axis=-1, keepdims=True) + norm_eps)

    def join(kept, other):
        return jnp.where(core == 0, jnp.concatenate([kept, other]), jnp.concatenate([other, kept]))

    def to_sequence(x):
        kept = lax.dynamic_index_in_dim(x, core, 0, keepdims=False)
        other = swap(lax.dynamic_index_in_dim(x, 1 - core, 0, keepdims=False))
        return join(kept, other)

    def to_tokens(x):
        halves = x.reshape(2, local_len, -1)
        kept = lax.dynamic_index_in_dim(halves, core, 0, keepdims=True)
        other = swap(lax.dynamic_index_in_dim(halves, 1 - core, 0, keepdims=True))
        return join(kept, other)

    def gather_first(x):
        return [along(x, mask) for mask in range(1, 3 if places == 4 else places)]

    def gather_last(x, first):
        return [along(x, 3, (1, 2)), along(first[1], 1, (0, 3))] if places == 4 else []

    def gathered(x, first, last):
        if places != 4:
            return [x] + first
        return [x] + first + [jnp.where((place == 0) | (place == 3), last[1], last[0])]

    def scatter_first(pieces):
        if places != 4:
            return []
        return [along(pieces[3], 1, (1, 2)), along(pieces[3], 3, (1, 2))]

    def scatter_second(pieces, first):
        if places != 4:
            return [pieces[0]] + [along(pieces[mask], mask) for mask in range(1, places)]
        far = (pieces[2].astype(f32) + first[0].astype(f32)).astype(pieces[2].dtype)
        return [pieces[0], along(pieces[1], 1), along(far, 2), first[1]]

    def in_order(found):
        stacked = jnp.stack(found)
        return jnp.stack([pieces_for(stacked, place ^ k) for k in range(places)])

    order = jnp.concatenate(
        [jnp.arange(places, dtype=jnp.int32) ^ place, core.reshape(1).astype(jnp.int32)]
    )
    token_own = to_sequence(block_input)

    half_cols = jnp.concatenate(
        [
            own_part(
                lax.dynamic_slice_in_dim(inproj_weight, core * inner_width, inner_width, 1), 1
            ),
            lax.dynamic_slice_in_dim(inproj_weight, 2 * inner_width + core * Q, Q, 1),
            jnp.pad(
                own_part(inproj_weight[:, 2 * inner_width + state_two :], 1),
                ((0, 0), (0, HP - heads)),
            ),
        ],
        axis=1,
    ).T
    shard_rows = half_cols.shape[1]
    small_rows = -(-small.shape[0] // (16 * shard_rows)) * 16
    small_pad = jnp.pad(small, (0, small_rows * shard_rows - small.shape[0]))
    sending = jnp.concatenate([half_cols, small_pad.reshape(small_rows, shard_rows)])
    sending = jnp.broadcast_to(sending[None], (shards,) + sending.shape)
    cot_own = to_sequence(cotangent)
    token_own, sending = lax.optimization_barrier((token_own, sending))
    token_first = gather_first(token_own)
    found = shard_exchange(sending)
    token_own, found, cot_own, outproj_late, *token_first = lax.optimization_barrier(
        (token_own, found, cot_own, outproj_weight, *token_first)
    )
    small_all = found[:, half_cols.shape[0] :].reshape(shards, -1)
    at_gate = norm_gain.shape[0]
    at_conv = at_gate + gate_gain.shape[0]
    at_head = at_conv + conv_params.size
    gain_f = small_all[:, :at_gate].reshape(-1).astype(f32)
    gate_f = small_all[:, at_gate:at_conv].reshape(-1).astype(f32)
    conv_f = (
        small_all[:, at_conv:at_head]
        .reshape(shards, kernel_len + 1, -1)
        .transpose(1, 0, 2)
        .reshape(kernel_len + 1, -1)
        .astype(f32)
    )
    head_f = (
        small_all[:, at_head : small.shape[0]].reshape(shards, 3, -1).transpose(1, 0, 2).reshape(3, -1).astype(f32)
    )
    taps = jnp.concatenate(
        [
            own_part(conv_f[:, :inner_width], 1),
            conv_f[:, inner_width:],
        ],
        axis=1,
    )
    channels = taps.shape[1]
    head_own = own_part(head_f, 1)
    gate_own = own_part(gate_f, 0)
    skip_gain = jnp.pad(
        jnp.stack([jnp.repeat(head_own[2], width), gate_own]), ((0, 0), (0, state_two))
    )
    chan = jnp.concatenate(
        [taps, jnp.zeros((6 - taps.shape[0], channels), f32), skip_gain], axis=0
    ).T
    rates = -jnp.exp(head_own[0])
    head_table = jnp.pad(
        jnp.stack([rates, head_own[1]], axis=1), ((0, HP - heads), (0, Q - 2))
    )

    token_last = gather_last(token_own, token_first)
    cot_first = gather_first(cot_own)
    half_width = model_width // 2
    share = own_width // parts
    out_sending = [lax.dynamic_slice_in_dim(outproj_late, core * half_width, half_width, 1)]
    if parts == shards:
        out_sending = [
            lax.dynamic_slice_in_dim(outproj_late, place * share, share, 0)
        ] + out_sending
    out_sending = [jnp.broadcast_to(x[None], (shards,) + x.shape) for x in out_sending]
    out_found = shard_exchange(out_sending[0])
    token_own, token_first, token_last, cot_own, cot_first, out_found = lax.optimization_barrier(
        (token_own, token_first, token_last, cot_own, cot_first, out_found)
    )
    token_pieces = gathered(token_own, token_first, token_last)
    other_found = swap(found)
    if shard_rows % Q == 0:
        weight = [found, other_found]
    else:
        turned = lambda x: x[:, : half_cols.shape[0]].transpose(1, 0, 2).reshape(-1, model_width)
        own_half, other_half = turned(found), turned(other_found)
        first = jnp.where(core == 0, own_half, other_half)
        second = jnp.where(core == 0, other_half, own_half)
        weight = [
            jnp.concatenate(
                [
                    first[:own_width],
                    second[:own_width],
                    first[own_width : own_width + Q],
                    second[own_width : own_width + Q],
                    own_half[own_width + Q :],
                ]
            )
        ]
    out_half = shard_exchange(out_sending[1]) if parts == shards else out_found
    def whole_columns(own, other):
        return jnp.where(
            core == 0, jnp.concatenate([own, other], axis=1), jnp.concatenate([other, own], axis=1)
        )

    def own_piece(param, count, axis_dim):
        return lax.dynamic_slice_in_dim(param, seq_index * count, count, axis_dim)

    def own_rows(x):
        return own_part(x, 0)


    forward = functools.partial(
        run_forward, order, token_pieces, gain_f[None], chan, head_table, own_width, heads, kernel_len
    )
    weight, written, carry = forward(0, places, weight, [], [])
    inproj_own = own_piece(inproj_weight, inproj_mean.shape[0], 0)
    cot_last = gather_last(cot_own, cot_first)
    written, inproj_own, cot_own, cot_first, cot_last = lax.optimization_barrier(
        (written, inproj_own, cot_own, cot_first, cot_last)
    )
    cot_pieces = gathered(cot_own, cot_first, cot_last)
    if parts == shards:
        outproj_own = out_found.reshape(own_width, model_width)
    else:
        out_rows_own = lax.optimization_barrier(own_rows(out_found.reshape(inner_width, half_width)))
        outproj_own = whole_columns(out_rows_own, swap(out_rows_own))
    normed_all, gates, values, conv, sent, table, states = written
    cot_all, dbranch, stat = run_statistics(order, gates, sent, cot_pieces, outproj_own, chan)
    stat = stat[:2]
    stat = stat + sum(along(stat, mask) for mask in range(1, places))
    grms = lax.rsqrt(stat[0] / inner_width + norm_eps)
    stats = jnp.pad(
        jnp.stack([grms, grms * grms * (stat[1] / inner_width)]), ((0, 6), (0, 0))
    )
    dsent, dgates, branch = run_gate(order, gates, sent, dbranch, stats, chan, places)
    dsent, dgates, branch, out_half = lax.optimization_barrier((dsent, dgates, branch, out_half))
    token_block = 2 * local_len
    flat = places * token_block

    def columns(x, m):
        return x[:, m * token_block : (m + 1) * token_block]

    token_block = 2 * local_len
    flat = places * token_block

    def columns(x, m):
        return x[:, m * token_block : (m + 1) * token_block]

    def over_cores(x, axis):
        kept = lax.dynamic_index_in_dim(x, core, axis, keepdims=False)
        other = lax.dynamic_index_in_dim(x, 1 - core, axis, keepdims=False)
        return kept, other

    def added(kept, other):
        return (kept.astype(f32) + other.astype(f32)).astype(bf16)

    in_rows = inproj_mean.shape[0]
    out_rows = outproj_mean.shape[0]

    def inproj_local(grad_rows):
        normed_flat = normed_all.reshape(flat, model_width)
        shape = (shards, places, in_rows, grad_rows.shape[0])
        if in_rows % 16 == 0:
            steps = min(shards, model_width // Q)
            kept, given = run_weight_gradient(
                core.reshape(1).astype(jnp.int32), normed_flat, grad_rows, in_rows, steps
            )
            return kept.reshape(shape), given.reshape(shape)
        part = lax.dot_general(
            normed_flat, grad_rows, (((0,), (1,)), ((), ())), preferred_element_type=f32
        ).astype(bf16)
        return over_cores(part.reshape(shards, places, 2, in_rows, -1), 2)

    branch_found = [along(columns(branch, m), m) for m in range(1, places)]
    out_part = jnp.dot(branch, cot_all.reshape(flat, model_width), preferred_element_type=f32).astype(bf16)
    out_kept, out_part = over_cores(out_part.reshape(shards, 2, out_rows, model_width), 1)
    out_part = swap(out_part)
    gate_kept, gate_part = inproj_local(dgates)
    gate_part = swap(gate_part)
    dsent, out_kept, gate_kept = lax.optimization_barrier((dsent, out_kept, gate_kept))
    drest, conv_sums, head_acc = run_backward(
        order, dsent, conv, values, table, states, chan, head_table, heads, kernel_len, places
    )
    rest_kept, rest_part = inproj_local(drest)
    rest_part = swap(rest_part)
    drest, rest_kept, branch_found, out_part, gate_part, conv_sums, head_acc, out_half = (
        lax.optimization_barrier(
            (drest, rest_kept, branch_found, out_part, gate_part, conv_sums, head_acc, out_half)
        )
    )
    out_half = out_half.reshape(inner_width, half_width)
    out_other = swap(out_half)
    head_sums = jnp.sum(head_acc, axis=-1)[:, :heads]
    head_sums = jnp.concatenate([head_sums[:1] * rates, head_sums[1:]])
    conv_sums = conv_sums[: kernel_len + 1]
    sums = jnp.concatenate([conv_sums.reshape(-1), head_sums.reshape(-1)])
    sums = sums + swap(sums)
    out_sum = added(out_kept, out_part)
    out_sum = jnp.concatenate(
        [out_sum[:, :, i : i + own_width] for i in range(0, model_width, own_width)], axis=1
    ).reshape(shards, places * in_rows, -1)
    gate_sum = added(gate_kept, gate_part).reshape(shards, places * in_rows, -1)
    drest, out_sum, gate_sum = lax.optimization_barrier((drest, out_sum, gate_sum))
    dn_pieces = run_token_gradient(dgates, drest, weight, places)
    sums, rest_part, out_other, *dn_pieces = lax.optimization_barrier(
        (sums, rest_part, out_other, *dn_pieces)
    )
    dn_first = scatter_first(dn_pieces)
    def halves(x, rows):
        high = lax.reduce_precision(x, 8, 7)
        both = jnp.concatenate([high, x - high]).astype(bf16)
        across_rows = -(-both.shape[0] // (rows * Q)) * Q
        return jnp.pad(both, (0, rows * across_rows - both.shape[0])).reshape(rows, across_rows)

    def joined_halves(x, count):
        x = x.reshape(x.shape[:-2] + (-1,))
        return x[..., :count] + x[..., count : 2 * count]

    small_sums = halves(sums, places * in_rows)
    joined = jnp.concatenate(
        [
            jnp.broadcast_to(small_sums[None], (shards,) + small_sums.shape),
            out_sum,
            gate_sum,
            added(rest_kept, rest_part).reshape(shards, places * in_rows, -1),
        ],
        axis=2,
    )
    joined = shard_exchange(joined)
    dn_pieces, dn_first = lax.optimization_barrier((dn_pieces, dn_first))
    dn_found = scatter_second(dn_pieces, dn_first)
    dn_found[1], branch_found, branch = lax.optimization_barrier((dn_found[1], branch_found, branch))
    branch_all = in_order([columns(branch, 0)] + branch_found)
    branch_all = branch_all.reshape(places, parts, -1, token_block).swapaxes(0, 1)
    branch_all = branch_all.reshape(inner_width, token_block)
    out = whole_columns(dot_tn(branch_all, out_half), dot_tn(branch_all, out_other))
    out, joined, dn_found = lax.optimization_barrier((out, joined, dn_found))
    joined = jnp.sum(joined.astype(f32), axis=0)
    at_out = small_sums.shape[1]
    at_in = at_out + out_rows * model_width // (places * in_rows)
    small_sums = halves(joined_halves(joined[:, :at_out], sums.shape[0]), in_rows)
    rest_side = jnp.concatenate(
        [
            jnp.broadcast_to(small_sums[None], (places,) + small_sums.shape),
            joined[:, at_in:].reshape(places, in_rows, -1).astype(bf16),
        ],
        axis=2,
    )
    rest_side, dn_found, out = lax.optimization_barrier((rest_side, dn_found, out))
    rest_side = line_exchange(rest_side)
    outproj_grad = joined[:, at_out:at_in].reshape(-1, out_rows, own_width)
    outproj_grad = outproj_grad.swapaxes(0, 1).reshape(out_rows, model_width)
    if parts == 1:
        outproj_grad = lax.ppermute(
            outproj_grad,
            ("wshard", "seq"),
            [
                (a * group + 2 * b + c, b * group + 2 * a + c)
                for a in range(shards)
                for b in range(places)
                for c in range(2)
            ],
        )

    at_in = small_sums.shape[1]
    lines = joined_halves(rest_side[:, :, :at_in].astype(f32), sums.shape[0])
    conv_lines = lines[:, : conv_sums.size].reshape(places, kernel_len + 1, channels)
    conv_total = jnp.concatenate(
        [
            whole(conv_lines[:, :, :own_width]),
            jnp.sum(conv_lines[:, :, own_width:], axis=0),
        ],
        axis=1,
    )
    head_total = whole(lines[:, conv_sums.size :].reshape(places, 3, heads))
    block_output = tokens + to_tokens(out)
    dnormed = sum(piece.astype(f32) for piece in dn_found)
    dn_scaled = to_tokens(dnormed) * gain_f
    input_grad = (
        cotangent.astype(f32)
        + scale * dn_scaled
        - tokens * scale * scale * scale * jnp.mean(dn_scaled * tokens, axis=-1, keepdims=True)
    )

    inproj_grad, *inproj_new, inproj_dot = run_finish(
        rest_side, inproj_own, inproj_mean, inproj_square, parts, own_width, state_two, heads, at_in
    )
    inproj_res = (inproj_grad, *inproj_new)
    conv_width = conv_mean.shape[1]
    conv_grad = lax.dynamic_slice_in_dim(
        conv_total, (shard * group + seq_index) * conv_width, conv_width, 1
    )
    head_width = head_params.shape[1]
    head_grad = lax.dynamic_slice_in_dim(head_total, shard * head_width, head_width, 1)

    outproj_piece = own_piece(outproj_weight, out_rows, 0).astype(f32)
    norm_own = own_piece(norm_gain, in_rows, 0).astype(f32)
    gate_piece = own_piece(gate_gain, out_rows, 0).astype(f32)
    norm_grad = inproj_dot[:, 0] / norm_own
    gate_grad = jnp.sum(outproj_piece * outproj_grad, axis=1) / gate_piece
    norm_res = adamw(norm_grad, norm_own, norm_mean, norm_square, 0.0)
    conv_res = adamw(conv_grad, own_piece(conv_params, conv_width, 1).astype(f32), conv_mean, conv_square, 0.0)
    head_res = adamw(head_grad, head_params.astype(f32), head_mean, head_square, 0.0)
    gate_res = adamw(gate_grad, gate_piece, gate_mean, gate_square, 0.0)
    outproj_res = adamw(outproj_grad, outproj_piece, outproj_mean, outproj_square, 0.1)
    return (
        block_output,
        input_grad,
        norm_res[0],
        norm_res[1],
        norm_res[2],
        norm_res[3],
        inproj_res[0],
        inproj_res[1],
        inproj_res[2],
        inproj_res[3],
        conv_res[0],
        conv_res[1],
        conv_res[2],
        conv_res[3],
        head_res[0],
        head_res[1],
        head_res[2],
        head_res[3],
        gate_res[0],
        gate_res[1],
        gate_res[2],
        gate_res[3],
        outproj_res[0],
        outproj_res[1],
        outproj_res[2],
        outproj_res[3],
    )


def solution(mesh):
    placed = (
        P("wshard", "seq", None),
        P("wshard", "seq", None),
        P("wshard"),
        P(("wshard", "seq")),
        P(("wshard", "seq")),
        P("wshard", None),
        P(("wshard", "seq"), None),
        P(("wshard", "seq"), None),
        P(None, "wshard"),
        P(None, ("wshard", "seq")),
        P(None, ("wshard", "seq")),
        P(None, "wshard"),
        P(None, "wshard"),
        P(None, "wshard"),
        P("wshard"),
        P(("wshard", "seq")),
        P(("wshard", "seq")),
        P("wshard", None),
        P(("wshard", "seq"), None),
        P(("wshard", "seq"), None),
    )
    return jax.shard_map(
        local,
        mesh=mesh,
        in_specs=placed,
        out_specs=(
            P("wshard", "seq", None),
            P("wshard", "seq", None),
            P(("wshard", "seq")),
            P(("wshard", "seq")),
            P(("wshard", "seq")),
            P(("wshard", "seq")),
            P(("wshard", "seq"), None),
            P(("wshard", "seq"), None),
            P(("wshard", "seq"), None),
            P(("wshard", "seq"), None),
            P(None, ("wshard", "seq")),
            P(None, ("wshard", "seq")),
            P(None, ("wshard", "seq")),
            P(None, ("wshard", "seq")),
            P(None, "wshard"),
            P(None, "wshard"),
            P(None, "wshard"),
            P(None, "wshard"),
            P(("wshard", "seq")),
            P(("wshard", "seq")),
            P(("wshard", "seq")),
            P(("wshard", "seq")),
            P(("wshard", "seq"), None),
            P(("wshard", "seq"), None),
            P(("wshard", "seq"), None),
            P(("wshard", "seq"), None),
        ),
        check_vma=False,
    )
```

```python
import functools

import jax
import jax.numpy as jnp
from jax import lax
from jax.experimental import pallas as pl
from jax.experimental.pallas import tpu as pltpu
from jax.sharding import PartitionSpec as P

norm_eps = 1e-05
adam_eps = 1e-08
learn_rate = 0.02
beta_one = 0.9
beta_two = 0.999
first_fix = 1.0 - 0.9**10
second_fix = 1.0 - 0.999**10

f32 = jnp.float32
bf16 = jnp.bfloat16
Q = 128
HP = 16
FLOOR = -1e30
MIB = 1024 * 1024


def dot_nn(a, b):
    return lax.dot_general(a, b, (((1,), (0,)), ((), ())), preferred_element_type=f32)


def dot_nt(a, b):
    return lax.dot_general(a, b, (((1,), (1,)), ((), ())), preferred_element_type=f32)


def dot_tn(a, b):
    return lax.dot_general(a, b, (((0,), (0,)), ((), ())), preferred_element_type=f32)


def sigmoid(a):
    return 1.0 / (1.0 + jnp.exp(-a))


def lanes(shape):
    return lax.broadcasted_iota(jnp.int32, shape, 1)


def earlier_by(current, previous, lane, shift):
    return pltpu.roll(jnp.where(lane >= Q - shift, previous, current), shift, 1)


def later_by(current, following, lane, shift):
    return pltpu.roll(jnp.where(lane < shift, following, current), Q - shift, 1)


def running_sum(a, lane):
    shift = 1
    while shift < Q:
        a = a + jnp.where(lane >= shift, pltpu.roll(a, shift, 1), 0.0)
        shift *= 2
    return a


def running_sum_back(a, lane):
    shift = 1
    while shift < Q:
        a = a + jnp.where(lane < Q - shift, pltpu.roll(a, Q - shift, 1), 0.0)
        shift *= 2
    return a


def join_weight(own_width, channels, core, own_ref, other_ref, weight_ref):
    shards, _, depth = own_ref.shape
    for even in range(2):

        @pl.when(core == even)
        def _(first=(own_ref, other_ref)[even], second=(other_ref, own_ref)[even]):
            for at in range(shards):
                here = slice(at * depth, (at + 1) * depth)
                low = 2 * own_width
                weight_ref[:own_width, here] = first[at, :own_width, :]
                weight_ref[own_width:low, here] = second[at, :own_width, :]
                weight_ref[low : low + Q, here] = first[at, own_width : own_width + Q, :]
                weight_ref[low + Q : low + 2 * Q, here] = second[at, own_width : own_width + Q, :]
                weight_ref[low + 2 * Q :, here] = own_ref[at, own_width + Q : own_width + Q + HP, :]


def mixer_forward(own_width, heads, kernel_len, places, start, assemble, order_ref, *refs):
    token_refs = refs[:places]
    gain_ref, chan_ref, head_ref = refs[places : places + 3]
    given = refs[places + 3 : -15]
    (
        weight_out,
        normed_ref,
        gates_ref,
        values_ref,
        conv_ref,
        sent_ref,
        table_ref,
        state_ref,
        before,
        state,
        active,
        steps,
        inter,
        scaled,
        wide,
    ) = refs[-15:]
    channels = chan_ref.shape[0]
    width = own_width // heads
    token_block = normed_ref.shape[0]

    @pl.when(pl.program_id(0) == 0)
    def _():
        before[...] = given[1][...] if start else jnp.zeros_like(before)
        state[...] = given[2][...] if start else jnp.zeros_like(state)
        for at, column in enumerate((*range(kernel_len + 1), 6)):
            wide[at] = jnp.broadcast_to(chan_ref[:, column : column + 1], wide.shape[1:])
        if not assemble:
            weight_out[...] = jnp.zeros_like(weight_out)
        else:
            join_weight(own_width, channels, order_ref[places], *given[:2], weight_out)

    for piece in range(places):

        @pl.when(order_ref[start + pl.program_id(0)] == piece)
        def _(token_ref=token_refs[piece]):
            tokens = token_ref[...].astype(f32)
            scale = lax.rsqrt(jnp.mean(tokens * tokens, axis=1, keepdims=True) + norm_eps)
            normed_ref[...] = (tokens * scale * gain_ref[...]).astype(bf16)

    weight_ref = weight_out if assemble else given[0]
    normed = normed_ref[...]
    gates_ref[...] = dot_nt(weight_ref[0:own_width, :], normed)
    values_ref[...] = dot_nt(weight_ref[own_width : own_width + channels, :], normed).astype(bf16)
    steps[...] = dot_nt(weight_ref[own_width + channels :, :], normed).astype(bf16).astype(f32)
    lane = lanes((Q, Q))
    lane_head = lanes((HP, Q))
    causal = lax.broadcasted_iota(jnp.int32, (Q, Q), 0) <= lane

    def block(at, carry):
        here = pl.ds(pl.multiple_of(at * Q, Q), Q)

        def convolve(tile, inner):
            rows = pl.ds(pl.multiple_of(tile * Q, Q), Q)
            raw = values_ref[rows, here]
            current = raw.astype(f32)
            previous = before[rows, :].astype(f32)
            out = wide[kernel_len, rows, :] + wide[kernel_len - 1, rows, :] * current
            for shift in range(1, kernel_len):
                tap = kernel_len - 1 - shift
                out = out + wide[tap, rows, :] * earlier_by(current, previous, lane, shift)
            before[rows, :] = raw
            conv_ref[rows, here] = out
            active[rows, :] = out * sigmoid(out)
            return inner

        lax.fori_loop(0, channels // Q, convolve, 0, unroll=True)
        drive = steps[:, here] + head_ref[:, 1:2]
        step = jnp.maximum(drive, 0.0) + jnp.log1p(jnp.exp(-jnp.abs(drive)))
        within = running_sum(step * head_ref[:, 0:1], lane_head)
        table_ref[0, :, here] = step
        table_ref[1, :, here] = within
        table_ref[2, :, here] = sigmoid(drive)
        within_col = jnp.transpose(within)
        total = within[:, Q - 1 : Q]
        grow = jnp.exp(within)
        tail = jnp.exp(total - within) * step
        total_decay = jnp.exp(total)
        b_rows = jnp.transpose(active[own_width : own_width + Q, :]).astype(bf16)
        c_cols = active[own_width + Q : own_width + 2 * Q, :].astype(bf16)
        scores = dot_nn(b_rows, c_cols)
        held = state[...].astype(bf16)
        state_ref[at] = held
        inter[...] = dot_nn(held, c_cols)
        for head in range(heads):
            rows = slice(head * width, (head + 1) * width)
            x = active[rows, :]
            decay = jnp.exp(
                jnp.where(causal, within[head : head + 1, :] - within_col[:, head : head + 1], FLOOR)
            )
            weights = (decay * scores).astype(bf16)
            driven = (x * step[head : head + 1, :]).astype(bf16)
            mixed = dot_nn(driven, weights)
            mixed = mixed + inter[rows, :] * grow[head : head + 1, :]
            mixed = mixed + wide[kernel_len + 1, rows, :] * x
            sent_ref[rows, here] = mixed.astype(bf16)
            scaled[rows, :] = (x * tail[head : head + 1, :]).astype(bf16)
            state[rows, :] = state[rows, :] * total_decay[head : head + 1, :]
        state[...] += dot_nn(scaled[...], b_rows)
        return carry

    lax.fori_loop(0, token_block // Q, block, 0, unroll=True)


def gate_statistics(places, order_ref, gates_ref, sent_ref, *refs):
    cot_refs = refs[:places]
    weight_ref, chan_ref, cot_all, dbranch_ref, stat_ref = refs[places:]
    for piece in range(places):

        @pl.when(order_ref[pl.program_id(0)] == piece)
        def _(cot_ref=cot_refs[piece]):
            cot_all[...] = cot_ref[...]

    dbranch = dot_nt(weight_ref[...], cot_all[...])
    dbranch_ref[...] = dbranch
    gates = gates_ref[...]
    gated = sent_ref[...].astype(f32) * (gates * sigmoid(gates))
    square = jnp.sum(gated * gated, axis=0, keepdims=True)
    cross = jnp.sum(gated * (dbranch * chan_ref[0 : gates.shape[0], 7:8]), axis=0, keepdims=True)
    stat_ref[...] = jnp.concatenate([square, cross, jnp.zeros((6, square.shape[1]), f32)], axis=0)


def gate_backward(
    order_ref, gates_ref, sent_ref, dbranch_ref, stat_ref, chan_ref, dsent_ref, dgates_ref, branch_ref
):
    grms = stat_ref[0:1, :]
    pull = stat_ref[1:2, :]

    def gate(tile, carry):
        rows = pl.ds(pl.multiple_of(tile * Q, Q), Q)
        gates = gates_ref[rows, :]
        sent = sent_ref[rows, :].astype(f32)
        gain = chan_ref[rows, 7:8]
        sig = sigmoid(gates)
        swish = gates * sig
        gated = sent * swish
        dgated = grms * (dbranch_ref[rows, :] * gain - gated * pull)
        dsent_ref[rows, :] = (dgated * swish).astype(bf16)
        dgates_ref[rows, :] = (dgated * sent * sig * (1.0 + gates * (1.0 - sig))).astype(bf16)
        branch_ref[rows, :] = (gated * grms * gain).astype(bf16)
        return carry

    lax.fori_loop(0, gates_ref.shape[0] // Q, gate, 0, unroll=True)


def mixer_backward(
    own_width,
    heads,
    kernel_len,
    order_ref,
    dsent_ref,
    conv_ref,
    values_ref,
    table_ref,
    state_ref,
    chan_ref,
    head_ref,
    *refs,
):
    (
        dproj_ref,
        conv_sum,
        head_acc,
        conv_acc,
        adjoint,
        following,
        active,
        dactive,
        inter,
        reach,
        driven,
        tailed,
        rows_scr,
        wide,
    ) = refs
    channels = chan_ref.shape[0]
    width = own_width // heads
    token_block = dsent_ref.shape[1]

    @pl.when(pl.program_id(0) == 0)
    def _():
        for held in (conv_acc, head_acc, adjoint, following):
            held[...] = jnp.zeros_like(held)
        rows_scr[...] = jnp.zeros_like(rows_scr)
        for at, column in enumerate((*range(kernel_len), 6)):
            wide[at] = jnp.broadcast_to(chan_ref[:, column : column + 1], wide.shape[1:])

    lane = lanes((Q, Q))
    sub = lax.broadcasted_iota(jnp.int32, (Q, Q), 0)
    lane_head = lanes((HP, Q))
    causal = sub >= lane
    strict = (sub < lane).astype(bf16)

    def block(index, carry):
        at = token_block // Q - 1 - index
        here = pl.ds(pl.multiple_of(at * Q, Q), Q)

        def activate(tile, inner):
            rows = pl.ds(pl.multiple_of(tile * Q, Q), Q)
            conv = conv_ref[rows, here]
            active[rows, :] = conv * sigmoid(conv)
            return inner

        lax.fori_loop(0, channels // Q, activate, 0, unroll=True)
        step = table_ref[0, :, here]
        within = table_ref[1, :, here]
        within_col = jnp.transpose(within)
        total = within[:, Q - 1 : Q]
        grow = jnp.exp(within)
        fade = jnp.exp(total - within)
        tail = fade * step
        total_decay = jnp.exp(total)
        b_cols_f = active[own_width : own_width + Q, :]
        c_cols_f = active[own_width + Q : own_width + 2 * Q, :]
        b_cols = b_cols_f.astype(bf16)
        c_cols = c_cols_f.astype(bf16)
        c_rows = jnp.transpose(c_cols_f).astype(bf16)
        scores = dot_nn(c_rows, b_cols)
        held = state_ref[at]
        after = adjoint[...].astype(bf16)
        inter[...] = dot_nn(held, c_cols)
        reach[...] = dot_nn(after, b_cols)
        dscores = jnp.zeros((Q, Q), f32)
        blank = jnp.zeros((width, Q), bf16)
        for pair in range(heads // 2):
            turned = jnp.transpose(dsent_ref[pair * 2 * width : (pair + 1) * 2 * width, here].astype(f32)).astype(bf16)
            for half in range(2):
                head = 2 * pair + half
                rows = slice(head * width, (head + 1) * width)
                one = slice(head, head + 1)
                x = active[rows, :]
                x_low = x.astype(bf16)
                grad_low = dsent_ref[rows, here]
                grad = grad_low.astype(f32)
                decay = jnp.exp(
                    jnp.where(causal, within_col[:, head : head + 1] - within[one, :], FLOOR)
                )
                lone = jnp.concatenate([x_low, blank] if half == 0 else [blank, x_low], axis=0)
                dweights = dot_nn(turned, lone)
                spread = decay * dweights * step[one, :]
                dscores = dscores + spread
                crossing = dot_nn((spread * scores).astype(bf16), strict)
                rows_scr[0, one, :] = jnp.sum(jnp.where(causal, crossing, 0.0), axis=0, keepdims=True)
                far = reach[rows, :]
                back = dot_nn(grad_low, (decay * scores).astype(bf16)) + far * fade[one, :]
                rows_scr[1, one, :] = jnp.sum(x * back, axis=0, keepdims=True)
                rows_scr[2, one, :] = jnp.sum(x * far, axis=0, keepdims=True) * tail[one, :]
                rows_scr[3, one, :] = jnp.sum(grad * inter[rows, :], axis=0, keepdims=True) * grow[one, :]
                rows_scr[4, one, :] = jnp.sum(grad * x, axis=0, keepdims=True)
                old = adjoint[rows, :]
                rows_scr[5, one, :] = jnp.sum(old * held[rows, :].astype(f32), axis=0, keepdims=True)
                dactive[rows, :] = back * step[one, :] + wide[kernel_len, rows, :] * grad
                driven[rows, :] = (grad * grow[one, :]).astype(bf16)
                tailed[rows, :] = (x * tail[one, :]).astype(bf16)
                adjoint[rows, :] = old * total_decay[one, :]
        dlow = dscores.astype(bf16)
        dactive[own_width : own_width + Q, :] = dot_nn(c_cols, dlow) + dot_tn(after, tailed[...])
        dactive[own_width + Q : own_width + 2 * Q, :] = dot_nt(b_cols, dlow) + dot_tn(held, driven[...])
        adjoint[...] += dot_nn(driven[...], c_rows)
        ahead = rows_scr[2]
        dlog = (
            rows_scr[0]
            + running_sum_back(rows_scr[3], lane_head)
            + (running_sum(ahead, lane_head) - ahead)
            + total_decay * jnp.sum(rows_scr[5], axis=1, keepdims=True)
        )
        dstep = (rows_scr[1] + head_ref[:, 0:1] * dlog) * table_ref[2, :, here]
        dproj_ref[channels:, here] = dstep.astype(bf16)
        head_acc[0] += step * dlog
        head_acc[1] += dstep
        head_acc[2] += rows_scr[4]

        def convolve(tile, inner):
            rows = pl.ds(pl.multiple_of(tile * Q, Q), Q)
            conv = conv_ref[rows, here]
            sig = sigmoid(conv)
            dconv = dactive[rows, :] * sig * (1.0 + conv * (1.0 - sig))
            raw = values_ref[rows, here].astype(f32)
            nxt = following[rows, :]
            dvalue = wide[kernel_len - 1, rows, :] * dconv
            conv_acc[kernel_len - 1, rows, :] += raw * dconv
            for shift in range(1, kernel_len):
                tap = kernel_len - 1 - shift
                moved = later_by(dconv, nxt, lane, shift)
                dvalue = dvalue + wide[tap, rows, :] * moved
                conv_acc[tap, rows, :] += raw * moved
            conv_acc[kernel_len, rows, :] += dconv
            following[rows, :] = dconv
            dproj_ref[rows, here] = dvalue.astype(bf16)
            return inner

        lax.fori_loop(0, channels // Q, convolve, 0, unroll=True)
        return carry

    lax.fori_loop(0, token_block // Q, block, 0, unroll=True)

    @pl.when(pl.program_id(0) == pl.num_programs(0) - 1)
    def _():
        ones = jnp.ones((8, Q), f32)
        for tap in range(kernel_len + 1):
            total = lax.dot_general(
                ones,
                conv_acc[tap],
                (((1,), (1,)), ((), ())),
                precision=lax.Precision.HIGHEST,
                preferred_element_type=f32,
            )
            conv_sum[tap : tap + 1, :] = total[0:1, :]


def run_forward(
    order, tokens, gain, chan, head_table, own_width, heads, kernel_len, start, count, weight, carry, written
):
    places = len(tokens)
    token_block, model_width = tokens[0].shape
    channels = chan.shape[0]
    full = places * token_block
    weight_shape = (own_width + channels + HP, model_width)
    assemble = len(weight) == 2
    solid = lambda x: pl.BlockSpec(x.shape, lambda k, order: (0,) * x.ndim)
    fixed = lambda k, order: (0, 0)
    cols = lambda k, order: (0, start + k)
    stored = lambda k, order: (order[start + k], 0, 0)
    spec = pltpu.PrefetchScalarGridSpec(
        num_scalar_prefetch=1,
        grid=(count,),
        in_specs=[solid(x) for x in (*tokens, gain, chan, head_table, *weight, *carry)]
        + [pl.BlockSpec(memory_space=pl.ANY)] * len(written),
        out_specs=[
            pl.BlockSpec(weight_shape if assemble else (8, Q), fixed),
            pl.BlockSpec((None, token_block, model_width), stored),
            pl.BlockSpec((own_width, token_block), cols),
            pl.BlockSpec((channels, token_block), cols),
            pl.BlockSpec((channels, token_block), cols),
            pl.BlockSpec((own_width, token_block), cols),
            pl.BlockSpec((3, HP, token_block), lambda k, order: (0, 0, start + k)),
            pl.BlockSpec((token_block // Q, own_width, Q), lambda k, order: (start + k, 0, 0)),
            pl.BlockSpec((channels, Q), fixed),
            pl.BlockSpec((own_width, Q), fixed),
        ],
        scratch_shapes=[
            pltpu.VMEM((channels, Q), f32),
            pltpu.VMEM((HP, token_block), f32),
            pltpu.VMEM((own_width, Q), f32),
            pltpu.VMEM((own_width, Q), bf16),
            pltpu.VMEM((kernel_len + 2, channels, Q), f32),
        ],
    )
    found = pl.pallas_call(
        functools.partial(mixer_forward, own_width, heads, kernel_len, places, start, assemble),
        grid_spec=spec,
        out_shape=[
            jax.ShapeDtypeStruct(weight_shape if assemble else (8, Q), bf16),
            jax.ShapeDtypeStruct((places, token_block, model_width), bf16),
            jax.ShapeDtypeStruct((own_width, full), f32),
            jax.ShapeDtypeStruct((channels, full), bf16),
            jax.ShapeDtypeStruct((channels, full), f32),
            jax.ShapeDtypeStruct((own_width, full), bf16),
            jax.ShapeDtypeStruct((3, HP, full), f32),
            jax.ShapeDtypeStruct((full // Q, own_width, Q), bf16),
            jax.ShapeDtypeStruct((channels, Q), bf16),
            jax.ShapeDtypeStruct((own_width, Q), f32),
        ],
        input_output_aliases={
            4 + places + len(weight) + len(carry) + i: 1 + i for i in range(len(written))
        },
        compiler_params=pltpu.CompilerParams(
            dimension_semantics=("arbitrary",), vmem_limit_bytes=48 * MIB
        ),
        cost_estimate=pl.CostEstimate(
            flops=8 * count * token_block * model_width * weight_shape[0],
            bytes_accessed=8 * MIB * count,
            transcendentals=MIB * count,
        ),
        name="mixer_forward",
    )(order, *tokens, gain, chan, head_table, *weight, *carry, *written)
    return found[0] if assemble else weight[0], found[1:8], found[8:]


def run_statistics(order, gates, sent, cotangents, weight, chan):
    places = len(cotangents)
    token_block, model_width = cotangents[0].shape
    own_width, full = gates.shape
    fixed = lambda k, order: (0, 0)
    cols = lambda k, order: (0, k)
    spec = pltpu.PrefetchScalarGridSpec(
        num_scalar_prefetch=1,
        grid=(places,),
        in_specs=[
            pl.BlockSpec((own_width, token_block), cols),
            pl.BlockSpec((own_width, token_block), cols),
            *[pl.BlockSpec((token_block, model_width), fixed)] * places,
            pl.BlockSpec(weight.shape, fixed),
            pl.BlockSpec(chan.shape, fixed),
        ],
        out_specs=[
            pl.BlockSpec((None, token_block, model_width), lambda k, order: (order[k], 0, 0)),
            pl.BlockSpec((own_width, token_block), cols),
            pl.BlockSpec((8, token_block), cols),
        ],
    )
    return pl.pallas_call(
        functools.partial(gate_statistics, places),
        grid_spec=spec,
        out_shape=[
            jax.ShapeDtypeStruct((places, token_block, model_width), bf16),
            jax.ShapeDtypeStruct((own_width, full), f32),
            jax.ShapeDtypeStruct((8, full), f32),
        ],
        compiler_params=pltpu.CompilerParams(
            dimension_semantics=("arbitrary",), vmem_limit_bytes=24 * MIB
        ),
        cost_estimate=pl.CostEstimate(
            flops=2 * full * model_width * own_width,
            bytes_accessed=16 * MIB,
            transcendentals=own_width * full,
        ),
        name="gate_statistics",
    )(order, gates, sent, *cotangents, weight, chan)


def run_gate(order, gates, sent, dbranch, stats, chan, places):
    own_width, full = gates.shape
    token_block = full // places
    cols = lambda k, order: (0, k)
    turned = lambda k, order: (0, order[k])
    spec = pltpu.PrefetchScalarGridSpec(
        num_scalar_prefetch=1,
        grid=(places,),
        in_specs=[
            pl.BlockSpec((own_width, token_block), cols),
            pl.BlockSpec((own_width, token_block), cols),
            pl.BlockSpec((own_width, token_block), cols),
            pl.BlockSpec((8, token_block), cols),
            pl.BlockSpec(chan.shape, lambda k, order: (0, 0)),
        ],
        out_specs=[
            pl.BlockSpec((own_width, token_block), cols),
            pl.BlockSpec((own_width, token_block), turned),
            pl.BlockSpec((own_width, token_block), turned),
        ],
    )
    return pl.pallas_call(
        gate_backward,
        grid_spec=spec,
        out_shape=[jax.ShapeDtypeStruct((own_width, full), bf16)] * 3,
        compiler_params=pltpu.CompilerParams(
            dimension_semantics=("arbitrary",), vmem_limit_bytes=20 * MIB
        ),
        cost_estimate=pl.CostEstimate(
            flops=20 * own_width * full, bytes_accessed=14 * own_width * full, transcendentals=own_width * full
        ),
        name="gate_backward",
    )(order, gates, sent, dbranch, stats, chan)


def run_backward(order, dsent, conv, values, table, states, chan, head_table, heads, kernel_len, places):
    own_width, full = dsent.shape
    channels = chan.shape[0]
    token_block = full // places
    out_rows = channels + HP
    last = places - 1
    fixed = lambda k, order: (0, 0)
    cols = lambda k, order: (0, last - k)
    spec = pltpu.PrefetchScalarGridSpec(
        num_scalar_prefetch=1,
        grid=(places,),
        in_specs=[
            pl.BlockSpec((own_width, token_block), cols),
            pl.BlockSpec((channels, token_block), cols),
            pl.BlockSpec((channels, token_block), cols),
            pl.BlockSpec((3, HP, token_block), lambda k, order: (0, 0, last - k)),
            pl.BlockSpec((token_block // Q, own_width, Q), lambda k, order: (last - k, 0, 0)),
            pl.BlockSpec(chan.shape, fixed),
            pl.BlockSpec(head_table.shape, fixed),
        ],
        out_specs=[
            pl.BlockSpec((out_rows, token_block), lambda k, order: (0, order[last - k])),
            pl.BlockSpec((8, channels), fixed),
            pl.BlockSpec((3, HP, Q), lambda k, order: (0, 0, 0)),
        ],
        scratch_shapes=[
            pltpu.VMEM((kernel_len + 1, channels, Q), f32),
            pltpu.VMEM((own_width, Q), f32),
            pltpu.VMEM((channels, Q), f32),
            pltpu.VMEM((channels, Q), f32),
            pltpu.VMEM((channels, Q), f32),
            pltpu.VMEM((own_width, Q), f32),
            pltpu.VMEM((own_width, Q), f32),
            pltpu.VMEM((own_width, Q), bf16),
            pltpu.VMEM((own_width, Q), bf16),
            pltpu.VMEM((6, HP, Q), f32),
            pltpu.VMEM((kernel_len + 1, channels, Q), f32),
        ],
    )
    return pl.pallas_call(
        functools.partial(mixer_backward, own_width, heads, kernel_len),
        grid_spec=spec,
        out_shape=[
            jax.ShapeDtypeStruct((out_rows, full), bf16),
            jax.ShapeDtypeStruct((8, channels), f32),
            jax.ShapeDtypeStruct((3, HP, Q), f32),
        ],
        compiler_params=pltpu.CompilerParams(
            dimension_semantics=("arbitrary",), vmem_limit_bytes=56 * MIB
        ),
        cost_estimate=pl.CostEstimate(
            flops=32 * MIB * 1024, bytes_accessed=24 * MIB, transcendentals=4 * MIB
        ),
        name="mixer_backward",
    )(order, dsent, conv, values, table, states, chan, head_table)


def token_gradient(dgates_ref, drest_ref, weight_ref, *out_refs):
    own_width = dgates_ref.shape[0]
    total = dot_tn(dgates_ref[...], weight_ref[:own_width, :]) + dot_tn(
        drest_ref[...], weight_ref[own_width:, :]
    )
    for piece, out_ref in enumerate(out_refs):

        @pl.when(pl.program_id(0) == piece)
        def _(out_ref=out_ref):
            out_ref[...] = total.astype(bf16)


def run_token_gradient(dgates, drest, weight, places):
    model_width = weight.shape[1]
    token_block = dgates.shape[1] // places
    fixed = lambda k: (0, 0)
    return pl.pallas_call(
        token_gradient,
        grid=(places,),
        in_specs=[
            pl.BlockSpec((dgates.shape[0], token_block), lambda k: (0, k)),
            pl.BlockSpec((drest.shape[0], token_block), lambda k: (0, k)),
            pl.BlockSpec(weight.shape, fixed),
        ],
        out_specs=[pl.BlockSpec((token_block, model_width), fixed)] * places,
        out_shape=[jax.ShapeDtypeStruct((token_block, model_width), bf16)] * places,
        compiler_params=pltpu.CompilerParams(
            dimension_semantics=("arbitrary",), vmem_limit_bytes=56 * MIB
        ),
        cost_estimate=pl.CostEstimate(
            flops=2 * dgates.shape[1] * weight.size, bytes_accessed=12 * MIB, transcendentals=0
        ),
        name="token_gradient",
    )(dgates, drest, weight)


def weight_gradient(in_rows, core_ref, normed_ref, grad_ref, kept_ref, given_ref):
    total = lax.dot_general(
        normed_ref[...], grad_ref[...], (((0,), (1,)), ((), ())), preferred_element_type=f32
    ).astype(bf16)
    for core in range(2):

        @pl.when(core_ref[0] == core)
        def _(core=core):
            for at in range(kept_ref.shape[0]):
                low = (2 * at + core) * in_rows
                kept_ref[at] = total[low : low + in_rows, :]
                low = (2 * at + 1 - core) * in_rows
                given_ref[at] = total[low : low + in_rows, :]


def run_weight_gradient(core, normed, grad, in_rows, steps):
    full, model_width = normed.shape
    columns = grad.shape[0]
    tile = model_width // steps
    groups = tile // (2 * in_rows)
    spec = pltpu.PrefetchScalarGridSpec(
        num_scalar_prefetch=1,
        grid=(steps,),
        in_specs=[
            pl.BlockSpec((full, tile), lambda k, core: (0, k)),
            pl.BlockSpec(grad.shape, lambda k, core: (0, 0)),
        ],
        out_specs=[pl.BlockSpec((groups, in_rows, columns), lambda k, core: (k, 0, 0))] * 2,
    )
    return pl.pallas_call(
        functools.partial(weight_gradient, in_rows),
        grid_spec=spec,
        out_shape=[jax.ShapeDtypeStruct((groups * steps, in_rows, columns), bf16)] * 2,
        compiler_params=pltpu.CompilerParams(
            dimension_semantics=("arbitrary",), vmem_limit_bytes=56 * MIB
        ),
        cost_estimate=pl.CostEstimate(
            flops=MIB, bytes_accessed=MIB // 8, transcendentals=0
        ),
        name="weight_gradient",
    )(core, normed, grad)


def finish_weight(parts, own_width, state_two, heads, at_in, found_ref, weight_ref, first_ref, second_ref, *outs):
    grad_ref, first_out, second_out, update_out, dot_out = outs
    places = found_ref.shape[0]
    inner = own_width * places
    low = at_in
    for base, total in ((0, inner), (inner, inner), (2 * inner + state_two, heads * places)):
        share = total // (parts * places)
        for part in range(parts):
            for place in range(places):
                to = base + part * (total // parts) + place * share
                grad_ref[:, to : to + share] = found_ref[
                    place, :, low + part * share : low + (part + 1) * share
                ].astype(f32)
        low += total // places
        if base == inner:
            shared = found_ref[0, :, low : low + state_two].astype(f32)
            for place in range(1, places):
                shared = shared + found_ref[place, :, low : low + state_two].astype(f32)
            grad_ref[:, 2 * inner : 2 * inner + state_two] = shared
            low += state_two
    grad = grad_ref[...]
    weight = weight_ref[...].astype(f32)
    _, first_new, second_new, update = adamw(grad, weight, first_ref[...], second_ref[...], 0.1)
    first_out[...] = first_new
    second_out[...] = second_new
    update_out[...] = update
    dot_out[...] = jnp.broadcast_to(jnp.sum(grad * weight, axis=1, keepdims=True), dot_out.shape)


def run_finish(found, weight, first, second, parts, own_width, state_two, heads, at_in):
    rows, columns = weight.shape
    step = 16 if rows % 16 == 0 else rows
    whole = pl.BlockSpec((step, columns), lambda k: (k, 0))
    return pl.pallas_call(
        functools.partial(finish_weight, parts, own_width, state_two, heads, at_in),
        grid=(rows // step,),
        in_specs=[
            pl.BlockSpec((found.shape[0], step, found.shape[2]), lambda k: (0, k, 0)),
            whole,
            whole,
            whole,
        ],
        out_specs=[whole] * 4 + [pl.BlockSpec((step, Q), lambda k: (k, 0))],
        out_shape=[jax.ShapeDtypeStruct((rows, columns), f32)] * 4
        + [jax.ShapeDtypeStruct((rows, Q), f32)],
        compiler_params=pltpu.CompilerParams(
            dimension_semantics=("arbitrary",), vmem_limit_bytes=32 * MIB
        ),
        cost_estimate=pl.CostEstimate(
            flops=20 * rows * columns, bytes_accessed=28 * rows * columns, transcendentals=rows * columns
        ),
        name="finish_weight",
    )(found, weight, first, second)


def adamw(grad, weight, first, second, decay):
    first_new = beta_one * first + (1.0 - beta_one) * grad
    second_new = beta_two * second + (1.0 - beta_two) * grad * grad
    update = -learn_rate * (
        first_new / first_fix / (jnp.sqrt(second_new / second_fix) + adam_eps) + decay * weight
    )
    return (grad, first_new, second_new, update)


def pieces_for(stacked, index):
    return lax.dynamic_index_in_dim(stacked, index, 0, keepdims=False)


def local(
    block_input,
    cotangent,
    norm_gain,
    norm_mean,
    norm_square,
    inproj_weight,
    inproj_mean,
    inproj_square,
    conv_params,
    conv_mean,
    conv_square,
    head_params,
    head_mean,
    head_square,
    gate_gain,
    gate_mean,
    gate_square,
    outproj_weight,
    outproj_mean,
    outproj_square,
):
    group = lax.axis_size("seq")
    shards = lax.axis_size("wshard")
    seq_index = lax.axis_index("seq")
    shard = lax.axis_index("wshard")
    places = group // 2
    place = seq_index // 2
    core = seq_index % 2
    sequences, local_len, model_width = block_input.shape
    inner_width = gate_gain.shape[0] * shards
    head_count = head_params.shape[1] * shards
    kernel_len = conv_params.shape[0] - 1
    state_two = conv_params.shape[1] * shards - inner_width
    if sequences != 2 or places != shards or state_two != 2 * Q:
        raise ValueError("unexpected sizes")
    own_width = inner_width // places
    heads = head_count // places
    width = inner_width // head_count

    parts = shards if head_count % (shards * places) == 0 else 1

    def own_part(x, axis):
        size = x.shape[axis]
        share = size // (parts * places)
        return jnp.concatenate(
            [
                lax.dynamic_slice_in_dim(x, i * (size // parts) + place * share, share, axis)
                for i in range(parts)
            ],
            axis=axis,
        )

    def whole(x):
        x = x.reshape(x.shape[:-1] + (parts, -1))
        x = jnp.moveaxis(x, 0, -2)
        return x.reshape(x.shape[:-3] + (-1,))

    def swap(x):
        return lax.ppermute(x, "seq", [(i, i ^ 1) for i in range(group)])

    def along(x, mask, among=None):
        pairs = [(i, i ^ (2 * mask)) for i in range(group)]
        if among is not None:
            pairs = [(a, b) for a, b in pairs if b // 2 in among]
        return lax.ppermute(x, "seq", pairs)

    def across(x, mask):
        return lax.ppermute(x, "wshard", [(i, i ^ mask) for i in range(shards)])

    def shard_exchange(x):
        return lax.all_to_all(x, "wshard", split_axis=0, concat_axis=0, tiled=True)

    def shard_gather(x):
        return shard_exchange(jnp.broadcast_to(x[None], (shards,) + x.shape))

    def line_exchange(x):
        groups = [[2 * i + c for i in range(places)] for c in range(2)]
        return lax.all_to_all(
            x, "seq", split_axis=0, concat_axis=0, tiled=True, axis_index_groups=groups
        )

    small = jnp.concatenate(
        [norm_gain, gate_gain, conv_params.reshape(-1), head_params.reshape(-1)]
    )
    tokens = block_input.astype(f32)
    scale = lax.rsqrt(jnp.mean(tokens * tokens, axis=-1, keepdims=True) + norm_eps)

    def join(kept, other):
        return jnp.where(core == 0, jnp.concatenate([kept, other]), jnp.concatenate([other, kept]))

    def to_sequence(x):
        kept = lax.dynamic_index_in_dim(x, core, 0, keepdims=False)
        other = swap(lax.dynamic_index_in_dim(x, 1 - core, 0, keepdims=False))
        return join(kept, other)

    def to_tokens(x):
        halves = x.reshape(2, local_len, -1)
        kept = lax.dynamic_index_in_dim(halves, core, 0, keepdims=True)
        other = swap(lax.dynamic_index_in_dim(halves, 1 - core, 0, keepdims=True))
        return join(kept, other)

    def gather_first(x):
        return [along(x, mask) for mask in range(1, 3 if places == 4 else places)]

    def gather_last(x, first):
        return [along(x, 3, (1, 2)), along(first[1], 1, (0, 3))] if places == 4 else []

    def gathered(x, first, last):
        if places != 4:
            return [x] + first
        return [x] + first + [jnp.where((place == 0) | (place == 3), last[1], last[0])]

    def scatter_first(pieces):
        if places != 4:
            return []
        return [along(pieces[3], 1, (1, 2)), along(pieces[3], 3, (1, 2))]

    def scatter_second(pieces, first):
        if places != 4:
            return [pieces[0]] + [along(pieces[mask], mask) for mask in range(1, places)]
        far = (pieces[2].astype(f32) + first[0].astype(f32)).astype(pieces[2].dtype)
        return [pieces[0], along(pieces[1], 1), along(far, 2), first[1]]

    def in_order(found):
        stacked = jnp.stack(found)
        return jnp.stack([pieces_for(stacked, place ^ k) for k in range(places)])

    order = jnp.concatenate(
        [jnp.arange(places, dtype=jnp.int32) ^ place, core.reshape(1).astype(jnp.int32)]
    )
    token_own = to_sequence(block_input)

    half_cols = jnp.concatenate(
        [
            own_part(
                lax.dynamic_slice_in_dim(inproj_weight, core * inner_width, inner_width, 1), 1
            ),
            lax.dynamic_slice_in_dim(inproj_weight, 2 * inner_width + core * Q, Q, 1),
            jnp.pad(
                own_part(inproj_weight[:, 2 * inner_width + state_two :], 1),
                ((0, 0), (0, HP - heads)),
            ),
        ],
        axis=1,
    ).T
    shard_rows = half_cols.shape[1]
    small_rows = -(-small.shape[0] // (16 * shard_rows)) * 16
    small_pad = jnp.pad(small, (0, small_rows * shard_rows - small.shape[0]))
    sending = jnp.concatenate([half_cols, small_pad.reshape(small_rows, shard_rows)])
    sending = jnp.broadcast_to(sending[None], (shards,) + sending.shape)
    cot_own = to_sequence(cotangent)
    token_own, sending = lax.optimization_barrier((token_own, sending))
    token_first = gather_first(token_own)
    found = shard_exchange(sending)
    token_own, found, cot_own, outproj_late, *token_first = lax.optimization_barrier(
        (token_own, found, cot_own, outproj_weight, *token_first)
    )
    small_all = found[:, half_cols.shape[0] :].reshape(shards, -1)
    at_gate = norm_gain.shape[0]
    at_conv = at_gate + gate_gain.shape[0]
    at_head = at_conv + conv_params.size
    gain_f = small_all[:, :at_gate].reshape(-1).astype(f32)
    gate_f = small_all[:, at_gate:at_conv].reshape(-1).astype(f32)
    conv_f = (
        small_all[:, at_conv:at_head]
        .reshape(shards, kernel_len + 1, -1)
        .transpose(1, 0, 2)
        .reshape(kernel_len + 1, -1)
        .astype(f32)
    )
    head_f = (
        small_all[:, at_head : small.shape[0]].reshape(shards, 3, -1).transpose(1, 0, 2).reshape(3, -1).astype(f32)
    )
    taps = jnp.concatenate(
        [
            own_part(conv_f[:, :inner_width], 1),
            conv_f[:, inner_width:],
        ],
        axis=1,
    )
    channels = taps.shape[1]
    head_own = own_part(head_f, 1)
    gate_own = own_part(gate_f, 0)
    skip_gain = jnp.pad(
        jnp.stack([jnp.repeat(head_own[2], width), gate_own]), ((0, 0), (0, state_two))
    )
    chan = jnp.concatenate(
        [taps, jnp.zeros((6 - taps.shape[0], channels), f32), skip_gain], axis=0
    ).T
    rates = -jnp.exp(head_own[0])
    head_table = jnp.pad(
        jnp.stack([rates, head_own[1]], axis=1), ((0, HP - heads), (0, Q - 2))
    )

    token_last = gather_last(token_own, token_first)
    cot_first = gather_first(cot_own)
    half_width = model_width // 2
    share = own_width // parts
    out_sending = [lax.dynamic_slice_in_dim(outproj_late, core * half_width, half_width, 1)]
    if parts == shards:
        out_sending = [
            lax.dynamic_slice_in_dim(outproj_late, place * share, share, 0)
        ] + out_sending
    out_sending = [jnp.broadcast_to(x[None], (shards,) + x.shape) for x in out_sending]
    out_found = shard_exchange(out_sending[0])
    token_own, token_first, token_last, cot_own, cot_first, out_found = lax.optimization_barrier(
        (token_own, token_first, token_last, cot_own, cot_first, out_found)
    )
    token_pieces = gathered(token_own, token_first, token_last)
    other_found = swap(found)
    if shard_rows % Q == 0:
        weight = [found, other_found]
    else:
        turned = lambda x: x[:, : half_cols.shape[0]].transpose(1, 0, 2).reshape(-1, model_width)
        own_half, other_half = turned(found), turned(other_found)
        first = jnp.where(core == 0, own_half, other_half)
        second = jnp.where(core == 0, other_half, own_half)
        weight = [
            jnp.concatenate(
                [
                    first[:own_width],
                    second[:own_width],
                    first[own_width : own_width + Q],
                    second[own_width : own_width + Q],
                    own_half[own_width + Q :],
                ]
            )
        ]
    out_half = shard_exchange(out_sending[1]) if parts == shards else out_found
    def whole_columns(own, other):
        return jnp.where(
            core == 0, jnp.concatenate([own, other], axis=1), jnp.concatenate([other, own], axis=1)
        )

    def own_piece(param, count, axis_dim):
        return lax.dynamic_slice_in_dim(param, seq_index * count, count, axis_dim)

    def own_rows(x):
        return own_part(x, 0)


    forward = functools.partial(
        run_forward, order, token_pieces, gain_f[None], chan, head_table, own_width, heads, kernel_len
    )
    weight, written, carry = forward(0, places, weight, [], [])
    inproj_own = own_piece(inproj_weight, inproj_mean.shape[0], 0)
    cot_last = gather_last(cot_own, cot_first)
    written, inproj_own, cot_own, cot_first, cot_last = lax.optimization_barrier(
        (written, inproj_own, cot_own, cot_first, cot_last)
    )
    cot_pieces = gathered(cot_own, cot_first, cot_last)
    if parts == shards:
        outproj_own = out_found.reshape(own_width, model_width)
    else:
        out_rows_own = lax.optimization_barrier(own_rows(out_found.reshape(inner_width, half_width)))
        outproj_own = whole_columns(out_rows_own, swap(out_rows_own))
    normed_all, gates, values, conv, sent, table, states = written
    cot_all, dbranch, stat = run_statistics(order, gates, sent, cot_pieces, outproj_own, chan)
    stat = stat[:2]
    stat = stat + sum(along(stat, mask) for mask in range(1, places))
    grms = lax.rsqrt(stat[0] / inner_width + norm_eps)
    stats = jnp.pad(
        jnp.stack([grms, grms * grms * (stat[1] / inner_width)]), ((0, 6), (0, 0))
    )
    dsent, dgates, branch = run_gate(order, gates, sent, dbranch, stats, chan, places)
    dsent, dgates, branch, out_half = lax.optimization_barrier((dsent, dgates, branch, out_half))
    token_block = 2 * local_len
    flat = places * token_block

    def columns(x, m):
        return x[:, m * token_block : (m + 1) * token_block]

    token_block = 2 * local_len
    flat = places * token_block

    def columns(x, m):
        return x[:, m * token_block : (m + 1) * token_block]

    def over_cores(x, axis):
        kept = lax.dynamic_index_in_dim(x, core, axis, keepdims=False)
        other = lax.dynamic_index_in_dim(x, 1 - core, axis, keepdims=False)
        return kept, other

    def added(kept, other):
        return (kept.astype(f32) + other.astype(f32)).astype(bf16)

    in_rows = inproj_mean.shape[0]
    out_rows = outproj_mean.shape[0]

    def inproj_local(grad_rows):
        normed_flat = normed_all.reshape(flat, model_width)
        shape = (shards, places, in_rows, grad_rows.shape[0])
        if in_rows % 16 == 0:
            steps = min(shards, model_width // Q)
            kept, given = run_weight_gradient(
                core.reshape(1).astype(jnp.int32), normed_flat, grad_rows, in_rows, steps
            )
            return kept.reshape(shape), given.reshape(shape)
        part = lax.dot_general(
            normed_flat, grad_rows, (((0,), (1,)), ((), ())), preferred_element_type=f32
        ).astype(bf16)
        return over_cores(part.reshape(shards, places, 2, in_rows, -1), 2)

    branch_found = [along(columns(branch, m), m) for m in range(1, places)]
    out_part = jnp.dot(branch, cot_all.reshape(flat, model_width), preferred_element_type=f32).astype(bf16)
    out_kept, out_part = over_cores(out_part.reshape(shards, 2, out_rows, model_width), 1)
    out_part = swap(out_part)
    gate_kept, gate_part = inproj_local(dgates)
    gate_part = swap(gate_part)
    dsent, out_kept, gate_kept = lax.optimization_barrier((dsent, out_kept, gate_kept))
    drest, conv_sums, head_acc = run_backward(
        order, dsent, conv, values, table, states, chan, head_table, heads, kernel_len, places
    )
    rest_kept, rest_part = inproj_local(drest)
    rest_part = swap(rest_part)
    drest, rest_kept, branch_found, out_part, gate_part, conv_sums, head_acc, out_half = (
        lax.optimization_barrier(
            (drest, rest_kept, branch_found, out_part, gate_part, conv_sums, head_acc, out_half)
        )
    )
    out_half = out_half.reshape(inner_width, half_width)
    out_other = swap(out_half)
    head_sums = jnp.sum(head_acc, axis=-1)[:, :heads]
    head_sums = jnp.concatenate([head_sums[:1] * rates, head_sums[1:]])
    conv_sums = conv_sums[: kernel_len + 1]
    sums = jnp.concatenate([conv_sums.reshape(-1), head_sums.reshape(-1)])
    sums = sums + swap(sums)
    out_sum = added(out_kept, out_part)
    out_sum = jnp.concatenate(
        [out_sum[:, :, i : i + own_width] for i in range(0, model_width, own_width)], axis=1
    ).reshape(shards, places * in_rows, -1)
    gate_sum = added(gate_kept, gate_part).reshape(shards, places * in_rows, -1)
    drest, out_sum, gate_sum = lax.optimization_barrier((drest, out_sum, gate_sum))
    dn_pieces = run_token_gradient(dgates, drest, weight, places)
    sums, rest_part, out_other, *dn_pieces = lax.optimization_barrier(
        (sums, rest_part, out_other, *dn_pieces)
    )
    dn_first = scatter_first(dn_pieces)
    def halves(x, rows):
        high = lax.reduce_precision(x, 8, 7)
        both = jnp.concatenate([high, x - high]).astype(bf16)
        across_rows = -(-both.shape[0] // (rows * Q)) * Q
        return jnp.pad(both, (0, rows * across_rows - both.shape[0])).reshape(rows, across_rows)

    def joined_halves(x, count):
        x = x.reshape(x.shape[:-2] + (-1,))
        return x[..., :count] + x[..., count : 2 * count]

    small_sums = halves(sums, places * in_rows)
    joined = jnp.concatenate(
        [
            jnp.broadcast_to(small_sums[None], (shards,) + small_sums.shape),
            out_sum,
            gate_sum,
            added(rest_kept, rest_part).reshape(shards, places * in_rows, -1),
        ],
        axis=2,
    )
    joined = shard_exchange(joined)
    dn_pieces, dn_first = lax.optimization_barrier((dn_pieces, dn_first))
    dn_found = scatter_second(dn_pieces, dn_first)
    dn_found[1], branch_found, branch = lax.optimization_barrier((dn_found[1], branch_found, branch))
    branch_all = in_order([columns(branch, 0)] + branch_found)
    branch_all = branch_all.reshape(places, parts, -1, token_block).swapaxes(0, 1)
    branch_all = branch_all.reshape(inner_width, token_block)
    out = whole_columns(dot_tn(branch_all, out_half), dot_tn(branch_all, out_other))
    out, joined, dn_found = lax.optimization_barrier((out, joined, dn_found))
    joined = jnp.sum(joined.astype(f32), axis=0)
    at_out = small_sums.shape[1]
    at_in = at_out + out_rows * model_width // (places * in_rows)
    small_sums = halves(joined_halves(joined[:, :at_out], sums.shape[0]), in_rows)
    rest_side = jnp.concatenate(
        [
            jnp.broadcast_to(small_sums[None], (places,) + small_sums.shape),
            joined[:, at_in:].reshape(places, in_rows, -1).astype(bf16),
        ],
        axis=2,
    )
    rest_side, dn_found, out = lax.optimization_barrier((rest_side, dn_found, out))
    rest_side = line_exchange(rest_side)
    outproj_grad = joined[:, at_out:at_in].reshape(-1, out_rows, own_width)
    outproj_grad = outproj_grad.swapaxes(0, 1).reshape(out_rows, model_width)
    if parts == 1:
        outproj_grad = lax.ppermute(
            outproj_grad,
            ("wshard", "seq"),
            [
                (a * group + 2 * b + c, b * group + 2 * a + c)
                for a in range(shards)
                for b in range(places)
                for c in range(2)
            ],
        )

    at_in = small_sums.shape[1]
    lines = joined_halves(rest_side[:, :, :at_in].astype(f32), sums.shape[0])
    conv_lines = lines[:, : conv_sums.size].reshape(places, kernel_len + 1, channels)
    conv_total = jnp.concatenate(
        [
            whole(conv_lines[:, :, :own_width]),
            jnp.sum(conv_lines[:, :, own_width:], axis=0),
        ],
        axis=1,
    )
    head_total = whole(lines[:, conv_sums.size :].reshape(places, 3, heads))
    block_output = tokens + to_tokens(out)
    dnormed = sum(piece.astype(f32) for piece in dn_found)
    dn_scaled = to_tokens(dnormed) * gain_f
    input_grad = (
        cotangent.astype(f32)
        + scale * dn_scaled
        - tokens * scale * scale * scale * jnp.mean(dn_scaled * tokens, axis=-1, keepdims=True)
    )

    inproj_grad, *inproj_new, inproj_dot = run_finish(
        rest_side, inproj_own, inproj_mean, inproj_square, parts, own_width, state_two, heads, at_in
    )
    inproj_res = (inproj_grad, *inproj_new)
    conv_width = conv_mean.shape[1]
    conv_grad = lax.dynamic_slice_in_dim(
        conv_total, (shard * group + seq_index) * conv_width, conv_width, 1
    )
    head_width = head_params.shape[1]
    head_grad = lax.dynamic_slice_in_dim(head_total, shard * head_width, head_width, 1)

    outproj_piece = own_piece(outproj_weight, out_rows, 0).astype(f32)
    norm_own = own_piece(norm_gain, in_rows, 0).astype(f32)
    gate_piece = own_piece(gate_gain, out_rows, 0).astype(f32)
    norm_grad = inproj_dot[:, 0] / norm_own
    gate_grad = jnp.sum(outproj_piece * outproj_grad, axis=1) / gate_piece
    norm_res = adamw(norm_grad, norm_own, norm_mean, norm_square, 0.0)
    conv_res = adamw(conv_grad, own_piece(conv_params, conv_width, 1).astype(f32), conv_mean, conv_square, 0.0)
    head_res = adamw(head_grad, head_params.astype(f32), head_mean, head_square, 0.0)
    gate_res = adamw(gate_grad, gate_piece, gate_mean, gate_square, 0.0)
    outproj_res = adamw(outproj_grad, outproj_piece, outproj_mean, outproj_square, 0.1)
    return (
        block_output,
        input_grad,
        norm_res[0],
        norm_res[1],
        norm_res[2],
        norm_res[3],
        inproj_res[0],
        inproj_res[1],
        inproj_res[2],
        inproj_res[3],
        conv_res[0],
        conv_res[1],
        conv_res[2],
        conv_res[3],
        head_res[0],
        head_res[1],
        head_res[2],
        head_res[3],
        gate_res[0],
        gate_res[1],
        gate_res[2],
        gate_res[3],
        outproj_res[0],
        outproj_res[1],
        outproj_res[2],
        outproj_res[3],
    )


def solution(mesh):
    placed = (
        P("wshard", "seq", None),
        P("wshard", "seq", None),
        P("wshard"),
        P(("wshard", "seq")),
        P(("wshard", "seq")),
        P("wshard", None),
        P(("wshard", "seq"), None),
        P(("wshard", "seq"), None),
        P(None, "wshard"),
        P(None, ("wshard", "seq")),
        P(None, ("wshard", "seq")),
        P(None, "wshard"),
        P(None, "wshard"),
        P(None, "wshard"),
        P("wshard"),
        P(("wshard", "seq")),
        P(("wshard", "seq")),
        P("wshard", None),
        P(("wshard", "seq"), None),
        P(("wshard", "seq"), None),
    )
    return jax.shard_map(
        local,
        mesh=mesh,
        in_specs=placed,
        out_specs=(
            P("wshard", "seq", None),
            P("wshard", "seq", None),
            P(("wshard", "seq")),
            P(("wshard", "seq")),
            P(("wshard", "seq")),
            P(("wshard", "seq")),
            P(("wshard", "seq"), None),
            P(("wshard", "seq"), None),
            P(("wshard", "seq"), None),
            P(("wshard", "seq"), None),
            P(None, ("wshard", "seq")),
            P(None, ("wshard", "seq")),
            P(None, ("wshard", "seq")),
            P(None, ("wshard", "seq")),
            P(None, "wshard"),
            P(None, "wshard"),
            P(None, "wshard"),
            P(None, "wshard"),
            P(("wshard", "seq")),
            P(("wshard", "seq")),
            P(("wshard", "seq")),
            P(("wshard", "seq")),
            P(("wshard", "seq"), None),
            P(("wshard", "seq"), None),
            P(("wshard", "seq"), None),
            P(("wshard", "seq"), None),
        ),
        check_vma=False,
    )
```
